32 devices in a mesh: walker: 8 (over z, x), gx: 2 (over y), gy: 2 (over core).
Axes of the slice: x: 2, y: 2, z: 4, core: 2. Of those that a mesh axis runs over, the one named last changes fastest.
Arguments:
- positions: float32 [8, 8, 8, 3, 128], P('walker', 'gx', 'gy')
- velocities: float32 [8, 8, 8, 3, 128], P('walker', 'gx', 'gy'), may hold values from -6 to 6
- lambda_theta: float32 [8, 4, 8], P('walker'), may hold values from -3 to 3
- theta_velocity: float32 [8, 4, 8], P('walker'), may hold values from -4 to 4
- source_slot: int32 [8], replicated, may hold values from 0 to 7
- atom_noise: float32 [8, 4, 8, 8, 3, 128], P('walker', None, 'gx', 'gy'), may hold values from -6 to 6
- theta_noise: float32 [8, 4, 4, 8], P('walker'), may hold values from -6 to 6
- charges: float32 [8, 8, 128], P('gx', 'gy'), may hold values from -3 to 3
- strengths: float32 [8, 8, 128], P('gx', 'gy'), may hold values from 0.3 to 1.2
- inverse_mass: float32 [8, 8, 128], P('gx', 'gy'), may hold values from 0.1 to 1
- atom_site: int32 [8, 8, 128], P('gx', 'gy'), may hold values from 0 to 4
- atom_sub: int32 [8, 8, 128], P('gx', 'gy'), may hold values from 0 to 7
- partners: int32 [8, 8, 9], P('gx', 'gy'), may hold values from -1 to 35, as said below
Outputs:
- displacement: float32 [8, 8, 8, 3, 128], P('walker', 'gx', 'gy')
- new_velocities: float32 [8, 8, 8, 3, 128], P('walker', 'gx', 'gy')
- new_theta: float32 [8, 4, 8], P('walker')
- new_theta_velocity: float32 [8, 4, 8], P('walker')
The draws below stay inside these ranges and needn't reach their ends.
Inputs may be any that keep to these rules, and one draw needn't show every extreme that they name: `atom_site`: 4 marks an environment atom. `partners`: entry values are indices (i mod 4 + 1 + di) * 6 + (j mod 4) + 1 + dj of tiles of the 3 x 3 neighbourhood of tile (i, j), with -1 <= di, dj <= 1, in increasing order of (di, dj), followed by -1 padding; the tile itself is always listed; tile A lists tile B exactly when B lists A; some tile lists all 9.
All inputs are finite; a program needn't handle non-finite values.
Results may differ from the reference program's by a relative error of at most 0.0003.
Values sent between devices are 32-bit elements; how exact they have to be, the bound alone decides.
No kernel may reach another device: no remote copies, remote signals or barrier semaphores. Data moves between devices by JAX's collectives and lax.ppermute only.
A program may use at most 64 MiB of HBM per device.

```python
import math
import jax
import jax.numpy as jnp
from jax import lax

CTX = 4
CTY = 4
TILE = 128
KT = 9
NSITE = 4
NSUB = 8
STEPS = 4
WALKERS = 8
NTX = 8
NTY = 8


def draw_positions(key, part):
    spread = jax.random.uniform(key, (WALKERS, NTX, NTY, 3, TILE), jnp.float32)
    rows_i = jnp.arange(NTX, dtype=jnp.float32)[None, :, None, None, None]
    cols_j = jnp.arange(NTY, dtype=jnp.float32)[None, None, :, None, None]
    component = jnp.arange(3)[None, None, None, :, None]
    anchor = jnp.where(component == 0, rows_i, jnp.where(component == 1, cols_j, 0.0))
    extent = jnp.where(component == 2, 2.0, 1.0)
    return anchor + extent * spread


def draw_source_slot(key, part):
    base = jax.random.randint(jax.random.fold_in(key, 21), (WALKERS,), 0, WALKERS)
    picked = jax.random.randint(jax.random.fold_in(key, 22), (), 0, WALKERS)
    slots = jnp.arange(WALKERS, dtype=jnp.int32)
    across = (picked + WALKERS // 2) % WALKERS
    top_slot = (picked + 1) % WALKERS
    low_slot = (picked + 2) % WALKERS
    chosen = jnp.where(slots == picked, across, base)
    chosen = jnp.where(slots == top_slot, WALKERS - 1, chosen)
    chosen = jnp.where(slots == low_slot, 0, chosen)
    return chosen.astype(jnp.int32)


def draw_partners(key, part):
    key_pair = jax.random.fold_in(key, 11)
    key_level = jax.random.fold_in(key, 12)
    forward = jax.random.randint(key_pair, (NTX, NTY, 4), 0, 8)
    levels = jax.random.randint(key_level, (NTX // CTX, NTY // CTY), 1, 9)
    levels = levels.at[0, 0].set(8)
    tile_level = jnp.repeat(jnp.repeat(levels, CTX, axis=0), CTY, axis=1)
    keep_forward = forward < tile_level[:, :, None]
    back_zero = jnp.roll(keep_forward[:, :, 0], 1, axis=1)
    back_one = jnp.roll(jnp.roll(keep_forward[:, :, 1], 1, axis=0), -1, axis=1)
    back_two = jnp.roll(keep_forward[:, :, 2], 1, axis=0)
    back_three = jnp.roll(jnp.roll(keep_forward[:, :, 3], 1, axis=0), 1, axis=1)
    itself = jnp.ones((NTX, NTY), dtype=bool)
    kept = jnp.stack([back_three, back_two, back_one, back_zero, itself, keep_forward[:, :, 0], keep_forward[:, :, 1], keep_forward[:, :, 2], keep_forward[:, :, 3]], axis=-1)
    slots = jnp.arange(9, dtype=jnp.int32)
    ordering = jnp.sort(jnp.where(kept, slots, 9 + slots), axis=-1)
    living = ordering < 9
    slot_value = ordering % 9
    offset_i = slot_value // 3 - 1
    offset_j = slot_value % 3 - 1
    local_i = jnp.arange(NTX, dtype=jnp.int32)[:, None, None] % CTX
    local_j = jnp.arange(NTY, dtype=jnp.int32)[None, :, None] % CTY
    index_value = (local_i + 1 + offset_i) * (CTY + 2) + (local_j + 1 + offset_j)
    return jnp.where(living, index_value, -1).astype(jnp.int32)


def plant(result, rng, least, high):
    dims = result.shape
    index_at = [jax.random.randint(jax.random.fold_in(rng, axis), (), 0, dims[axis]) for axis in range(len(dims))]
    result = result.at[tuple(index_at)].set(least)
    longest = dims.index(max(dims))
    index_at[longest] = (index_at[longest] + 1) % dims[longest]
    return result.at[tuple(index_at)].set(high)


def block_scale(stream_key, dims, cuts, least, largest):
    def one(position, parts):
        draws = jax.random.uniform(jax.random.fold_in(jax.random.fold_in(stream_key, 6), position), (parts,), jnp.float32, least / len(cuts), largest / len(cuts))
        return jnp.repeat(jnp.exp(draws), dims[position] // parts).reshape((-1,) + (1,) * (len(dims) - position - 1))

    level = one(*cuts[0])
    for cut in cuts[1:]:
        level = level * one(*cut)
    return level


def noise(stream_key, shape, scale, bound, shards=(), kind=jnp.bfloat16):
    loudness = block_scale(stream_key, shape, shards, -0.22, 0.18) if shards else 1.0
    entries = jax.random.normal(stream_key, shape, jnp.float32) * scale * loudness
    return jnp.minimum(jnp.maximum(entries, -bound), bound).astype(kind)


def setup_inputs(seed: int = 0) -> dict:
    key_list = jax.random.split(jax.random.key(seed), 14)
    return {
        "positions": draw_positions(jax.random.fold_in(key_list[13], 71), 0),
        "velocities": noise(key_list[1], (WALKERS, NTX, NTY, 3, TILE), 1.0, 6.0, ((0, 8), (1, 2), (2, 2)), jnp.float32),
        "lambda_theta": noise(key_list[2], (WALKERS, NSITE, NSUB), 1.0, 3.0, ((0, 8),), jnp.float32),
        "theta_velocity": noise(key_list[3], (WALKERS, NSITE, NSUB), 1.0, 4.0, ((0, 8),), jnp.float32),
        "source_slot": draw_source_slot(jax.random.fold_in(key_list[13], 71), 0),
        "atom_noise": noise(key_list[5], (WALKERS, STEPS, NTX, NTY, 3, TILE), 1.0, 6.0, ((0, 8), (2, 2), (3, 2)), jnp.float32),
        "theta_noise": noise(key_list[6], (WALKERS, STEPS, NSITE, NSUB), 1.0, 6.0, ((0, 8),), jnp.float32),
        "charges": noise(key_list[7], (NTX, NTY, TILE), 0.5, 3.0, ((0, 2), (1, 2)), jnp.float32),
        "strengths": jnp.clip(jnp.exp(math.log(1.2) - 1.3862944 * jax.random.uniform(key_list[8], (NTX, NTY, TILE), jnp.float32) ** block_scale(key_list[8], (NTX, NTY, TILE), ((0, 2), (1, 2)), -0.2, 0.2)), 0.3, 1.2),
        "inverse_mass": jnp.clip(jnp.exp(math.log(1.0) - 2.3025851 * jax.random.uniform(key_list[9], (NTX, NTY, TILE), jnp.float32) ** block_scale(key_list[9], (NTX, NTY, TILE), ((0, 2), (1, 2)), -0.2, 0.2)), 0.1, 1.0),
        "atom_site": plant(jax.random.randint(key_list[10], (NTX, NTY, TILE), 0, NSITE + 1), jax.random.fold_in(key_list[10], 1), 0, NSITE).astype(jnp.int32),
        "atom_sub": plant(jax.random.randint(key_list[11], (NTX, NTY, TILE), 0, NSUB), jax.random.fold_in(key_list[11], 1), 0, NSUB - 1).astype(jnp.int32),
        "partners": draw_partners(jax.random.fold_in(key_list[13], 71), 0),
    }


step_size = 0.02
friction_rate = 1.0
theta_friction = 20.0
soft_alpha = 0.5
soft_beta = 0.5
theta_share = 1.0 / 1024.0

def wrap_image(offset, length):
    upper = (offset > 0.5 * length).astype(jnp.float32)
    lower = (offset < -0.5 * length).astype(jnp.float32)
    return offset - length * upper + length * lower

def pair_terms(pool_coords, pool_params, pool_labels, pool_lambda, partner_rows, own_rows, box_x, box_y):
    atom_width = pool_coords.shape[-1]
    diagonal = jnp.arange(atom_width)[:, None] == jnp.arange(atom_width)[None, :]

    def one_tile(tile_entry):
        partner_list, own_index = tile_entry
        usable = partner_list >= 0
        chosen = jnp.maximum(partner_list, 0)
        own_coords = pool_coords[own_index]
        others = pool_coords[chosen]
        offset = own_coords[None, :, :, None] - others[:, :, None, :]
        delta_x = wrap_image(offset[:, 0], box_x)
        delta_y = wrap_image(offset[:, 1], box_y)
        delta_z = offset[:, 2]
        distance = delta_x * delta_x + delta_y * delta_y + delta_z * delta_z
        lambda_own = pool_lambda[own_index][None, :, None]
        lambda_other = pool_lambda[chosen][:, None, :]
        group_own = pool_labels[own_index, 0][None, :, None]
        group_other = pool_labels[chosen, 0][:, None, :]
        site_own = pool_labels[own_index, 1][None, :, None]
        site_other = pool_labels[chosen, 1][:, None, :]
        same_group = (group_own == group_other) & (group_own >= 0)
        clashing = (site_own == site_other) & (site_own >= 0) & jnp.logical_not(same_group)
        itself = (chosen == own_index)[:, None, None] & diagonal[None]
        keep_mask = (usable[:, None, None] & jnp.logical_not(clashing) & jnp.logical_not(itself)).astype(jnp.float32)
        coupling = jnp.where(same_group, lambda_own, lambda_own * lambda_other)
        weighting = jnp.where(same_group, 0.5, lambda_other)
        strength = pool_params[own_index, 1][None, :, None] * pool_params[chosen, 1][:, None, :]
        charge = pool_params[own_index, 0][None, :, None] * pool_params[chosen, 0][:, None, :]
        soft_vdw = 1.0 / (1.0 + soft_alpha * (1.0 - coupling) + distance)
        soft_elec = lax.rsqrt(1.0 + soft_beta * (1.0 - coupling) + distance)
        vdw_two = soft_vdw * soft_vdw
        vdw_three = vdw_two * soft_vdw
        elec_three = soft_elec * soft_elec * soft_elec
        radial = keep_mask * (-2.0 * coupling * strength * vdw_three - 0.5 * coupling * charge * elec_three)
        sensitivity = keep_mask * (strength * vdw_two + 2.0 * soft_alpha * coupling * strength * vdw_three + charge * soft_elec + 0.5 * soft_beta * coupling * charge * elec_three)
        forces = -2.0 * jnp.stack([lax.optimization_barrier(jnp.sum(radial * delta_x, axis=(0, 2))), lax.optimization_barrier(jnp.sum(radial * delta_y, axis=(0, 2))), lax.optimization_barrier(jnp.sum(radial * delta_z, axis=(0, 2)))])
        drive_sum = lax.optimization_barrier(jnp.sum(sensitivity * weighting, axis=(0, 2)))
        return (forces, drive_sum)
    return lax.map(one_tile, (partner_rows, own_rows))

def atom_lambda(labels, lambda_flat):
    groups = labels[..., 0, :]
    labels_range = jnp.arange(lambda_flat.shape[0])
    picked = lax.optimization_barrier(jnp.sum(jnp.where(groups[..., None] == labels_range, lambda_flat, 0.0), axis=-1))
    return jnp.where(groups >= 0, picked, 1.0)

def group_sums(groups, drive_sum, group_count):
    labels_range = jnp.arange(group_count)
    return lax.optimization_barrier(jnp.sum(jnp.where(groups[..., None] == labels_range, drive_sum[..., None], 0.0), axis=tuple(range(groups.ndim))))

def advance(coords, speeds, angles, angle_speeds, impulse, angle_impulse, pool_params, pool_labels, inverse_mass, partner_rows, own_rows):
    tile_count = NTX * NTY
    damping = math.exp(-friction_rate * step_size)
    angle_damping = math.exp(-theta_friction * step_size)
    angle_mass = NTX * NTY * TILE * theta_share
    start_coords = coords
    for moment in range(STEPS):
        weights = jnp.exp(angles)
        lambdas = weights / lax.optimization_barrier(jnp.sum(weights, axis=-1, keepdims=True))
        pool_lambda = atom_lambda(pool_labels, lambdas.reshape(-1))
        forces, drive_sum = pair_terms(coords.reshape(tile_count, 3, TILE), pool_params, pool_labels, pool_lambda, partner_rows, own_rows, float(NTX), float(NTY))
        totals = group_sums(pool_labels[:, 0], drive_sum, NSITE * NSUB).reshape(NSITE, NSUB)
        angle_force = -lambdas * (totals - lax.optimization_barrier(jnp.sum(lambdas * totals, axis=-1, keepdims=True)))
        angle_speeds = angle_damping * angle_speeds + step_size * angle_force / angle_mass + math.sqrt((1.0 - angle_damping ** 2) / angle_mass) * angle_impulse[moment]
        angles = angles + step_size * angle_speeds
        speeds = damping * speeds + step_size * forces.reshape(NTX, NTY, 3, TILE) * inverse_mass[:, :, None, :] + jnp.sqrt((1.0 - damping ** 2) * inverse_mass)[:, :, None, :] * impulse[moment]
        coords = coords + step_size * speeds
    return (coords - start_coords, speeds, angles, angle_speeds)

def reference(positions, velocities, lambda_theta, theta_velocity, source_slot, atom_noise, theta_noise, charges, strengths, inverse_mass, atom_site, atom_sub, partners):
    tile_count = NTX * NTY
    is_group = atom_site < NSITE
    groups = jnp.where(is_group, atom_site * NSUB + atom_sub, -1).astype(jnp.int32)
    sites = jnp.where(is_group, atom_site, -1).astype(jnp.int32)
    pool_labels = jnp.stack([groups, sites], axis=2).reshape(tile_count, 2, TILE)
    pool_params = jnp.stack([charges, strengths], axis=2).reshape(tile_count, 2, TILE)
    rows_i = jnp.arange(NTX, dtype=jnp.int32)[:, None, None]
    cols_j = jnp.arange(NTY, dtype=jnp.int32)[None, :, None]
    shift_i = partners // (CTY + 2) - 1 - rows_i % CTX
    shift_j = partners % (CTY + 2) - 1 - cols_j % CTY
    global_rows = jnp.where(partners >= 0, (rows_i + shift_i) % NTX * NTY + (cols_j + shift_j) % NTY, -1)
    global_rows = global_rows.reshape(tile_count, KT).astype(jnp.int32)
    own_rows = jnp.arange(tile_count, dtype=jnp.int32)

    def walker_run(walker_entry):
        coords, speeds, angles, angle_speeds, impulse, angle_impulse = walker_entry
        return advance(coords, speeds, angles, angle_speeds, impulse, angle_impulse, pool_params, pool_labels, inverse_mass, global_rows, own_rows)
    displacement, new_velocities, new_theta, new_theta_velocity = lax.map(walker_run, (positions[source_slot], velocities[source_slot], lambda_theta[source_slot], theta_velocity[source_slot], atom_noise, theta_noise))
    return (displacement, new_velocities, new_theta, new_theta_velocity)
```

```python
import functools
import math

import jax
import jax.numpy as jnp
from jax import lax
from jax.experimental import pallas as pl
from jax.experimental.pallas import tpu as pltpu
from jax.sharding import PartitionSpec as P

NSITE = 4
NSUB = 8
STEPS = 4

step_size = 0.02
friction_rate = 1.0
theta_friction = 20.0
soft_alpha = 0.5
soft_beta = 0.5
theta_share = 1.0 / 1024.0

X, Y, Z, LAM, CHG, STR, GRP, SIT = range(8)


def wrap_image(offset, length):
    shift = jnp.where(offset > 0.5 * length, length, 0.0)
    shift = jnp.where(offset < -0.5 * length, -length, shift)
    return offset - shift


def neighbour_offsets(count_x, count_y):
    found = []
    for di in (-1, 0, 1):
        for dj in (-1, 0, 1):
            key = (di % count_x, dj % count_y)
            if key != (0, 0) and key not in found:
                found.append(key)
    return found


def shifted(value, offset, count_x, count_y):
    pairs = []
    for i in range(count_x):
        for j in range(count_y):
            source = ((i + offset[0]) % count_x) * count_y + (j + offset[1]) % count_y
            pairs.append((source, i * count_y + j))
    return lax.ppermute(value, ("gx", "gy"), pairs)


def pool_sources(rows_x, rows_y, count_x, count_y, offsets):
    sources = []
    for pi in range(rows_x + 2):
        for pj in range(rows_y + 2):
            di = -1 if pi == 0 else (1 if pi == rows_x + 1 else 0)
            dj = -1 if pj == 0 else (1 if pj == rows_y + 1 else 0)
            key = (di % count_x, dj % count_y)
            block = 0 if key == (0, 0) else 1 + offsets.index(key)
            tile = ((pi - 1) % rows_x) * rows_y + (pj - 1) % rows_y
            sources.append((block, tile))
    return sources


def softmax_angles(angles):
    weights = jnp.exp(angles)
    return weights / jnp.sum(weights, axis=1, keepdims=True)


def angle_step(angles, speeds, packed, noise, angle_mass):
    lanes = packed.shape[1]
    share = lanes // NSITE
    lane_site = lax.broadcasted_iota(jnp.int32, packed.shape, 1) // share
    lambdas = softmax_angles(angles)
    totals = jnp.stack(
        [
            jnp.broadcast_to(
                jnp.sum(jnp.where(lane_site == site, packed, 0.0), axis=1, keepdims=True),
                packed.shape,
            )
            for site in range(NSITE)
        ]
    )
    angle_damping = math.exp(-theta_friction * step_size)
    force = -lambdas * (totals - jnp.sum(lambdas * totals, axis=1, keepdims=True))
    speeds = (
        angle_damping * speeds
        + step_size * force / angle_mass
        + math.sqrt((1.0 - angle_damping**2) / angle_mass) * noise
    )
    return angles + step_size * speeds, speeds


def step_kernel(cfg, moment, *refs):
    nb = cfg["blocks"]
    tiles, pool = cfg["tiles"], cfg["pool"]
    lanes = cfg["lanes"]
    count_ref, part_ref = refs[:2]
    coord_refs = refs[2 : 2 + nb]
    stat_refs = refs[2 + nb : 2 + 2 * nb]
    tot_ref, vel_ref, ang_ref, noise_ref, anoise_ref, inv_ref = refs[2 + 2 * nb : 8 + 2 * nb]
    pay_ref, velo_ref, ango_ref = refs[8 + 2 * nb : 11 + 2 * nb]
    pool_ref, col_ref, fcol_ref, sum_ref = refs[11 + 2 * nb :]

    angles, aspeeds = ang_ref[0], ang_ref[1]
    if moment > 0:
        if cfg["covered"]:
            packed = coord_refs[0][0:NSUB, 3, :]
            for ref in coord_refs[1:]:
                packed = packed + ref[0:NSUB, 3, :]
        else:
            packed = tot_ref[...]
        angles, aspeeds = angle_step(
            angles, aspeeds, packed, anoise_ref[moment - 1], cfg["angle_mass"]
        )
    ango_ref[0] = angles
    ango_ref[1] = aspeeds
    lambdas = softmax_angles(angles)

    sub_iota = lax.broadcasted_iota(jnp.int32, (NSUB, lanes), 0).astype(jnp.float32)
    for index, (block, tile) in enumerate(cfg["sources"]):
        stat = stat_refs[block][tile]
        pool_ref[index, 0:3, :] = coord_refs[block][tile, 0:3, :]
        pool_ref[index, 4:8, :] = stat
        group = stat[2:3, :]
        lam = jnp.zeros((NSUB, lanes), jnp.float32)
        for site in range(NSITE):
            lam = lam + jnp.where(group == sub_iota + float(site * NSUB), lambdas[site], 0.0)
        lam = jnp.sum(lam, axis=0, keepdims=True)
        pool_ref[index, 3:4, :] = jnp.where(group >= 0.0, lam, 1.0)

    sum_ref[...] = jnp.zeros_like(sum_ref)
    chunk = 32

    def one_tile(tile, carry):
        own = (tile // cfg["rows_y"] + 1) * (cfg["rows_y"] + 2) + tile % cfg["rows_y"] + 1
        block = pool_ref[own]
        col_ref[...] = block.T
        count = count_ref[tile]

        def one_chunk(c, carry):
            start = pl.multiple_of(c * chunk, chunk)
            cols = col_ref[pl.ds(start, chunk), :]
            lanes_iota = lax.broadcasted_iota(jnp.int32, (chunk, lanes), 1)
            diagonal = lanes_iota == lax.broadcasted_iota(jnp.int32, (chunk, lanes), 0) + start

            def one_partner(k, sums):
                fx, fy, fz, fd = sums
                index = part_ref[tile, k]
                other = pool_ref[index]

                def own_col(row):
                    return cols[:, row : row + 1]

                def other_row(row):
                    return other[row : row + 1, :]

                dx = wrap_image(own_col(X) - other_row(X), cfg["box_x"])
                dy = wrap_image(own_col(Y) - other_row(Y), cfg["box_y"])
                dz = own_col(Z) - other_row(Z)
                r2 = dx * dx + dy * dy + dz * dz
                same = (own_col(GRP) == other_row(GRP)) & (own_col(GRP) >= 0.0)
                site = (own_col(SIT) == other_row(SIT)) & (own_col(SIT) >= 0.0)
                drop = (site & jnp.logical_not(same)) | (diagonal & (index == own))
                lam_a, lam_b = own_col(LAM), other_row(LAM)
                s = jnp.where(same, lam_a, lam_a * lam_b)
                w = jnp.where(same, 0.5, lam_b)
                e = own_col(STR) * other_row(STR)
                q = own_col(CHG) * other_row(CHG)
                rs = lax.rsqrt(1.0 + 0.5 * (1.0 - s) + r2)
                t = rs * rs * rs
                a = e * t
                b = s * t * (a + 0.25 * q)
                sens = rs * (a + q) + b
                b = jnp.where(drop, 0.0, b)
                sens = jnp.where(drop, 0.0, sens * w)
                return fx + b * dx, fy + b * dy, fz + b * dz, fd + sens

            zero = jnp.zeros((chunk, lanes), jnp.float32)
            sums = lax.fori_loop(0, count, one_partner, (zero, zero, zero, zero))
            for row, value in enumerate(sums):
                fcol_ref[pl.ds(start, chunk), row : row + 1] = jnp.sum(
                    value, axis=1, keepdims=True
                )
            return carry

        lax.fori_loop(0, lanes // chunk, one_chunk, 0)
        forces = fcol_ref[...].T
        finish_tile(
            cfg, tile, 4.0 * forces[0:3, :], forces[3:4, :], block,
            (vel_ref, noise_ref, inv_ref), (pay_ref, velo_ref, sum_ref), sub_iota,
        )
        return carry

    fcol_ref[...] = jnp.zeros_like(fcol_ref)
    lax.fori_loop(0, tiles, one_tile, 0)
    pay_sums(cfg, pay_ref, sum_ref)


def finish_tile(cfg, tile, forces, drive, block, ins, outs, sub_iota):
    vel_ref, noise_ref, inv_ref = ins
    pay_ref, velo_ref, sum_ref = outs
    damping = math.exp(-friction_rate * step_size)
    inverse = inv_ref[tile]
    speeds = (
        damping * vel_ref[tile, 0:3, :]
        + step_size * forces * inverse
        + jnp.sqrt((1.0 - damping**2) * inverse) * noise_ref[0, tile]
    )
    velo_ref[tile] = speeds
    pay_ref[tile, 0:3, :] = block[0:3, :] + step_size * speeds
    group = block[GRP : GRP + 1, :]
    for site in range(NSITE):
        sum_ref[site] += jnp.where(group == sub_iota + float(site * NSUB), drive, 0.0)


def pay_sums(cfg, pay_ref, sum_ref):
    lanes = cfg["lanes"]
    share = lanes // NSITE
    lane_site = lax.broadcasted_iota(jnp.int32, (NSUB, lanes), 1) // share
    packed = jnp.zeros((NSUB, lanes), jnp.float32)
    for site in range(NSITE):
        folded = sum_ref[site]
        width = lanes
        while width > share:
            width //= 2
            folded = folded + pltpu.roll(folded, width, 1)
        packed = packed + jnp.where(lane_site == site, folded, 0.0)
    for sub in range(cfg["tiles"]):
        pay_ref[sub, 3:4, :] = (
            packed[sub : sub + 1, :] if sub < NSUB else jnp.zeros((1, lanes), jnp.float32)
        )


def step_call(cfg, moment, count, parts, blocks, stats, totals, vel, ang, noise, anoise, inverse):
    tiles, lanes = cfg["tiles"], cfg["lanes"]
    nb = cfg["blocks"]
    vmem = pl.BlockSpec(memory_space=pltpu.VMEM)
    smem = pl.BlockSpec(memory_space=pltpu.SMEM)
    noise_spec = pl.BlockSpec((1, tiles, 3, lanes), lambda i: (moment, 0, 0, 0))

    return pl.pallas_call(
        functools.partial(step_kernel, cfg, moment),
        grid=(1,),
        out_shape=(
            jax.ShapeDtypeStruct((tiles, 4, lanes), jnp.float32),
            jax.ShapeDtypeStruct((tiles, 3, lanes), jnp.float32),
            jax.ShapeDtypeStruct((2, NSITE, NSUB, lanes), jnp.float32),
        ),
        in_specs=[smem, smem] + [vmem] * (2 * nb + 3) + [noise_spec, vmem, vmem],
        out_specs=(vmem, vmem, vmem),
        scratch_shapes=[
            pltpu.VMEM((cfg["pool"], 8, lanes), jnp.float32),
            pltpu.VMEM((lanes, 8), jnp.float32),
            pltpu.VMEM((lanes, 8), jnp.float32),
            pltpu.VMEM((NSITE, NSUB, lanes), jnp.float32),
        ],
        name="langevin_step",
    )(count, parts, *blocks, *stats, totals, vel, ang, noise, anoise, inverse)


def per_device(
    positions,
    velocities,
    lambda_theta,
    theta_velocity,
    source_slot,
    atom_noise,
    theta_noise,
    charges,
    strengths,
    inverse_mass,
    atom_site,
    atom_sub,
    partners,
):
    count_x, count_y = lax.axis_size("gx"), lax.axis_size("gy")
    peers = lax.axis_size("walker")
    rows_x, rows_y, lanes = charges.shape
    tiles = rows_x * rows_y
    offsets = neighbour_offsets(count_x, count_y)
    cfg = dict(
        blocks=1 + len(offsets),
        covered=1 + len(offsets) == count_x * count_y,
        tiles=tiles,
        lanes=lanes,
        rows_y=rows_y,
        pool=(rows_x + 2) * (rows_y + 2),
        sources=pool_sources(rows_x, rows_y, count_x, count_y, offsets),
        box_x=float(rows_x * count_x),
        box_y=float(rows_y * count_y),
        angle_mass=rows_x * count_x * rows_y * count_y * lanes * theta_share,
    )

    def gather_blocks(value):
        return [value] + [shifted(value, offset, count_x, count_y) for offset in offsets]

    is_group = atom_site < NSITE
    groups = jnp.where(is_group, atom_site * NSUB + atom_sub, -1)
    sites = jnp.where(is_group, atom_site, -1)
    stat = jnp.stack(
        [charges, strengths, groups.astype(jnp.float32), sites.astype(jnp.float32)], axis=2
    ).reshape(tiles, 4, lanes)
    stats = gather_blocks(stat)

    mine = source_slot[lax.axis_index("walker")]
    angles = jnp.stack([lambda_theta[0], theta_velocity[0]]).reshape(1, 2 * NSITE * NSUB)
    angles = jnp.pad(angles, ((0, 0), (0, lanes - 2 * NSITE * NSUB)))
    extra = jnp.broadcast_to(angles[:, None, :], (tiles, 1, lanes))
    first = jnp.concatenate([positions.reshape(tiles, 3, lanes), extra], axis=1)
    second = velocities.reshape(tiles, 3, lanes)

    def picked(value):
        everyone = lax.all_to_all(
            jnp.broadcast_to(value, (peers,) + value.shape), "walker", 0, 0, tiled=True
        )
        return lax.dynamic_index_in_dim(everyone, mine, 0, keepdims=False)

    start = picked(first)
    vel = picked(second)
    ang = start[0, 3, : 2 * NSITE * NSUB].reshape(2, NSITE, NSUB, 1)
    ang = jnp.broadcast_to(ang, (2, NSITE, NSUB, lanes))
    anoise = jnp.broadcast_to(theta_noise[0][..., None], (STEPS, NSITE, NSUB, lanes))
    noise = atom_noise.reshape(STEPS, tiles, 3, lanes)
    inverse = inverse_mass.reshape(tiles, 1, lanes)
    parts = partners.reshape(tiles, -1)
    count = jnp.sum((parts >= 0).astype(jnp.int32), axis=1)

    pay = start
    for moment in range(STEPS):
        blocks = gather_blocks(pay)
        if moment > 0 and not cfg["covered"]:
            totals = lax.psum(pay[:NSUB, 3, :], ("gx", "gy"))
        else:
            totals = jnp.zeros((NSUB, lanes), jnp.float32)
        pay, vel, ang = step_call(
            cfg, moment, count, parts, blocks, stats, totals, vel, ang, noise, anoise, inverse
        )
    packed = pay[:NSUB, 3, :]
    if cfg["covered"]:
        totals = packed
        for offset in offsets:
            totals = totals + shifted(packed, offset, count_x, count_y)
    else:
        totals = lax.psum(packed, ("gx", "gy"))
    angles, aspeeds = angle_step(ang[0], ang[1], totals, anoise[STEPS - 1], cfg["angle_mass"])
    displacement = (pay[:, 0:3, :] - start[:, 0:3, :]).reshape(positions.shape)
    return (
        displacement,
        vel.reshape(velocities.shape),
        angles[None, :, :, 0],
        aspeeds[None, :, :, 0],
    )


def solution(mesh):
    in_specs = (
        P("walker", "gx", "gy", None, None),
        P("walker", "gx", "gy", None, None),
        P("walker", None, None),
        P("walker", None, None),
        P(),
        P("walker", None, "gx", "gy", None, None),
        P("walker", None, None, None),
        P("gx", "gy", None),
        P("gx", "gy", None),
        P("gx", "gy", None),
        P("gx", "gy", None),
        P("gx", "gy", None),
        P("gx", "gy", None),
    )
    out_specs = (
        P("walker", "gx", "gy", None, None),
        P("walker", "gx", "gy", None, None),
        P("walker", None, None),
        P("walker", None, None),
    )
    return jax.shard_map(
        per_device, mesh=mesh, in_specs=in_specs, out_specs=out_specs, check_vma=False
    )
```

```python
import functools
import math

import jax
import jax.numpy as jnp
from jax import lax
from jax.experimental import pallas as pl
from jax.experimental.pallas import tpu as pltpu
from jax.sharding import PartitionSpec as P

NSITE = 4
NSUB = 8
STEPS = 4

step_size = 0.02
friction_rate = 1.0
theta_friction = 20.0
soft_alpha = 0.5
soft_beta = 0.5
theta_share = 1.0 / 1024.0

MIDDLE_Z = 1.0
REACH = 1.49
FAR = 2.0**126

X, Y, Z, LAM, CHG, STR, GRP, SIT = range(8)


def wrap_image(offset, length):
    shift = jnp.where(offset > 0.5 * length, length, 0.0)
    shift = jnp.where(offset < -0.5 * length, -length, shift)
    return offset - shift


def neighbour_offsets(count_x, count_y):
    found = []
    for di in (-1, 0, 1):
        for dj in (-1, 0, 1):
            key = (di % count_x, dj % count_y)
            if key != (0, 0) and key not in found:
                found.append(key)
    return found


def shifted(value, offset, count_x, count_y):
    pairs = []
    for i in range(count_x):
        for j in range(count_y):
            source = ((i + offset[0]) % count_x) * count_y + (j + offset[1]) % count_y
            pairs.append((source, i * count_y + j))
    return lax.ppermute(value, ("gx", "gy"), pairs)


def pool_sources(rows_x, rows_y, count_x, count_y, offsets):
    sources = []
    for pi in range(rows_x + 2):
        for pj in range(rows_y + 2):
            di = -1 if pi == 0 else (1 if pi == rows_x + 1 else 0)
            dj = -1 if pj == 0 else (1 if pj == rows_y + 1 else 0)
            key = (di % count_x, dj % count_y)
            block = 0 if key == (0, 0) else 1 + offsets.index(key)
            tile = ((pi - 1) % rows_x) * rows_y + (pj - 1) % rows_y
            sources.append((block, tile))
    return sources


def softmax_angles(angles):
    weights = jnp.exp(angles)
    return weights / jnp.sum(weights, axis=1, keepdims=True)


def angle_step(angles, speeds, packed, noise, angle_mass):
    lanes = packed.shape[1]
    share = lanes // NSITE
    lane_site = lax.broadcasted_iota(jnp.int32, packed.shape, 1) // share
    lambdas = softmax_angles(angles)
    totals = jnp.stack(
        [
            jnp.broadcast_to(
                jnp.sum(jnp.where(lane_site == site, packed, 0.0), axis=1, keepdims=True),
                packed.shape,
            )
            for site in range(NSITE)
        ]
    )
    angle_damping = math.exp(-theta_friction * step_size)
    force = -lambdas * (totals - jnp.sum(lambdas * totals, axis=1, keepdims=True))
    speeds = (
        angle_damping * speeds
        + step_size * force / angle_mass
        + math.sqrt((1.0 - angle_damping**2) / angle_mass) * noise
    )
    return angles + step_size * speeds, speeds


def step_kernel(cfg, moment, *refs):
    nb = cfg["blocks"]
    tiles, pool = cfg["tiles"], cfg["pool"]
    lanes = cfg["lanes"]
    count_ref, part_ref, off_ref = refs[:3]
    refs = refs[1:]
    coord_refs = refs[2 : 2 + nb]
    stat_refs = refs[2 + nb : 2 + 2 * nb]
    tot_ref, vel_ref, ang_ref, noise_ref, anoise_ref, inv_ref = refs[2 + 2 * nb : 8 + 2 * nb]
    pay_ref, velo_ref, ango_ref = refs[8 + 2 * nb : 11 + 2 * nb]
    pool_ref, col_ref, fcol_ref, sum_ref, feat_ref, wide_ref, rhs_ref, sel_ref = refs[11 + 2 * nb :]

    angles, aspeeds = ang_ref[0], ang_ref[1]
    if moment > 0:
        if cfg["covered"]:
            packed = coord_refs[0][0:NSUB, 3, :]
            for ref in coord_refs[1:]:
                packed = packed + ref[0:NSUB, 3, :]
        else:
            packed = tot_ref[...]
        angles, aspeeds = angle_step(
            angles, aspeeds, packed, anoise_ref[moment - 1], cfg["angle_mass"]
        )
    ango_ref[0] = angles
    ango_ref[1] = aspeeds
    lambdas = softmax_angles(angles)

    sub_iota = lax.broadcasted_iota(jnp.int32, (NSUB, lanes), 0).astype(jnp.float32)
    worst = jnp.zeros((3, lanes), jnp.float32)
    row3 = lax.broadcasted_iota(jnp.int32, (3, lanes), 0)
    for index, (block, tile) in enumerate(cfg["sources"]):
        stat = stat_refs[block][tile]
        cell = jnp.where(row3 == 0, off_ref[2, index], off_ref[3, index])
        cell = jnp.where(row3 == 2, -MIDDLE_Z, cell)
        worst = jnp.maximum(worst, jnp.abs(coord_refs[block][tile, 0:3, :] + cell))
        pool_ref[index, 0:3, :] = coord_refs[block][tile, 0:3, :]
        pool_ref[index, 4:8, :] = stat
        group = stat[2:3, :]
        lam = jnp.zeros((NSUB, lanes), jnp.float32)
        for site in range(NSITE):
            lam = lam + jnp.where(group == sub_iota + float(site * NSUB), lambdas[site], 0.0)
        lam = jnp.sum(lam, axis=0, keepdims=True)
        pool_ref[index, 3:4, :] = jnp.where(group >= 0.0, lam, 1.0)

    stray = jnp.max(worst * jnp.where(row3 == 2, 0.5, 1.0))
    sum_ref[...] = jnp.zeros_like(sum_ref)
    fcol_ref[...] = jnp.zeros_like(fcol_ref)
    ins = (vel_ref, noise_ref, inv_ref)
    outs = (pay_ref, velo_ref, sum_ref)
    near = cfg["roomy"] & (stray < REACH)

    @pl.when(near)
    def _():
        near_forces(
            cfg, lambdas, count_ref, part_ref, off_ref, pool_ref, feat_ref, wide_ref, rhs_ref,
            sel_ref, ins, outs, sub_iota,
        )

    @pl.when(jnp.logical_not(near))
    def _():
        any_forces(cfg, count_ref, part_ref, pool_ref, col_ref, fcol_ref, ins, outs, sub_iota)

    pay_sums(cfg, pay_ref, sum_ref)


def split3(value):
    high = value.astype(jnp.bfloat16).astype(jnp.float32)
    rest = value - high
    middle = rest.astype(jnp.bfloat16).astype(jnp.float32)
    return high, middle, rest - middle


def by_group(lambdas_of_site, group, sub_iota):
    return [
        jnp.where(group == sub_iota + float(site * NSUB), lambdas_of_site[site], 0.0)
        for site in range(NSITE)
    ]


def near_forces(
    cfg, lambdas, count_ref, part_ref, off_ref, pool_ref, feat_ref, wide_ref, rhs_ref,
    sel_ref, ins, outs, sub_iota,
):
    lanes = cfg["lanes"]
    depth = cfg["depth"]
    rows = lax.broadcasted_iota(jnp.int32, (8, lanes), 0)
    ones = jnp.ones((NSUB, lanes), jnp.float32)
    nothing = jnp.zeros((8, lanes), jnp.float32)
    pad = [nothing] * ((depth - 6 * 8 - 2 * NSITE * NSUB) // 8)

    pick_rows = lax.broadcasted_iota(jnp.int32, (depth, lanes), 0)
    for column, row in enumerate((0, 1, 2, 7)):
        hit = (pick_rows == row) | (pick_rows == 16 + row) | (pick_rows == 40 + row)
        sel_ref[:, column * lanes : (column + 1) * lanes] = jnp.where(hit, 1.0, 0.0).astype(
            jnp.bfloat16
        )

    def centred(index):
        block = pool_ref[index]
        shift = jnp.where(rows == 0, off_ref[0, index], 0.0)
        shift = jnp.where(rows == 1, off_ref[1, index], shift)
        shift = jnp.where(rows == 2, -MIDDLE_Z, shift)
        moved = block + shift
        square = jnp.where(rows < 3, moved * moved, 0.0)
        return block, moved, jnp.sum(square, axis=0, keepdims=True)

    def one_pool(index, carry):
        block, moved, norm = centred(index)
        table = jnp.where(rows == 5, norm, moved)
        table = jnp.where(rows == 6, 1.0, table)
        table = jnp.where(rows == 7, block[STR : STR + 1, :], table)
        high, middle, low = split3(table)
        member = by_group([ones] * NSITE, block[GRP : GRP + 1, :], sub_iota)
        features = jnp.concatenate(
            [high, high, middle, middle, high, low] + member + member + pad, axis=0
        )
        features = features.T.astype(jnp.bfloat16)
        feat_ref[index] = features
        wide_ref[index] = jnp.dot(features, sel_ref[...], preferred_element_type=jnp.float32)
        return carry

    lax.fori_loop(0, cfg["pool"], one_pool, 0)

    spread = [lam - lam * lam for lam in lambdas]
    half = [0.5 - lam for lam in lambdas]

    def one_tile(tile, carry):
        own = (tile // cfg["rows_y"] + 1) * (cfg["rows_y"] + 2) + tile % cfg["rows_y"] + 1
        block, moved, norm = centred(own)
        group, site_row = block[GRP : GRP + 1, :], block[SIT : SIT + 1, :]
        lam, charge, strength = (block[r : r + 1, :] for r in (LAM, CHG, STR))
        ratio = charge / strength

        gap = jnp.where(rows < 3, -2.0 * moved, 0.0)
        gap = jnp.where(rows == 3, -0.5 * lam, gap)
        gap = jnp.where(rows == 5, 1.0, gap)
        gap = jnp.where(rows == 6, norm + 1.5, gap)
        pair = by_group(spread, group, sub_iota)
        far = [
            jnp.where(
                (site_row == float(site)) & (group != sub_iota + float(site * NSUB)), FAR, 0.0
            )
            for site in range(NSITE)
        ]
        columns = (
            (gap, [f - 0.5 * p for f, p in zip(far, pair)]),
            (jnp.where(rows == 3, lam, 0.0), pair),
            (jnp.where(rows == 3, 1.0, 0.0), by_group(half, group, sub_iota)),
            (jnp.where(rows == 4, ratio, 0.0), [nothing] * NSITE),
        )
        for column, (table, member) in enumerate(columns):
            high, middle, low = split3(table)
            tops = [m.astype(jnp.bfloat16).astype(jnp.float32) for m in member]
            rests = [m - t for m, t in zip(member, tops)]
            rhs_ref[:, column * lanes : (column + 1) * lanes] = jnp.concatenate(
                [high, middle, high, middle, low, high] + tops + rests + pad, axis=0
            ).astype(jnp.bfloat16)

        def one_partner(k, sums):
            index = part_ref[tile, k]
            out = jnp.dot(feat_ref[index], rhs_ref[...], preferred_element_type=jnp.float32)
            fx, fy, fz, fo, fd = sums
            for i in range(lanes // 8):
                here = slice(8 * i, 8 * i + 8)
                gap2, s, w, q = (out[here, c * lanes : (c + 1) * lanes] for c in range(4))
                xb, yb, zb, eb = (
                    wide_ref[index, here, c * lanes : (c + 1) * lanes] for c in range(4)
                )
                rs = lax.rsqrt(gap2)
                t = rs * rs * rs
                a = eb * t
                b = (s * t) * (a + 0.25 * q)
                sens = rs * (a + q) + b
                fx = fx + b * xb
                fy = fy + b * yb
                fz = fz + b * zb
                fo = fo + b
                fd = fd + sens * w
            return fx, fy, fz, fo, fd

        sums = lax.fori_loop(0, count_ref[tile], one_partner, (nothing,) * 5)
        fx, fy, fz, fo, fd = (jnp.sum(value, axis=0, keepdims=True) for value in sums)
        forces = jnp.concatenate(
            [moved[r : r + 1, :] * fo - f for r, f in enumerate((fx, fy, fz))], axis=0
        )
        rs = lax.rsqrt(1.5 - 0.5 * lam)
        t = rs * rs * rs
        a, q = strength * t, ratio * charge
        itself = rs * (a + q) + lam * t * (a + 0.25 * q)
        drive = strength * (fd - 0.5 * itself)
        finish_tile(cfg, tile, (4.0 * strength) * forces, drive, block, ins, outs, sub_iota)
        return carry

    lax.fori_loop(0, cfg["tiles"], one_tile, 0)


def any_forces(cfg, count_ref, part_ref, pool_ref, col_ref, fcol_ref, ins, outs, sub_iota):
    tiles, lanes = cfg["tiles"], cfg["lanes"]
    chunk = 32

    def one_tile(tile, carry):
        own = (tile // cfg["rows_y"] + 1) * (cfg["rows_y"] + 2) + tile % cfg["rows_y"] + 1
        block = pool_ref[own]
        col_ref[...] = block.T
        count = count_ref[tile]

        def one_chunk(c, carry):
            start = pl.multiple_of(c * chunk, chunk)
            cols = col_ref[pl.ds(start, chunk), :]
            lanes_iota = lax.broadcasted_iota(jnp.int32, (chunk, lanes), 1)
            diagonal = lanes_iota == lax.broadcasted_iota(jnp.int32, (chunk, lanes), 0) + start

            def one_partner(k, sums):
                fx, fy, fz, fd = sums
                index = part_ref[tile, k]
                other = pool_ref[index]

                def own_col(row):
                    return cols[:, row : row + 1]

                def other_row(row):
                    return other[row : row + 1, :]

                dx = wrap_image(own_col(X) - other_row(X), cfg["box_x"])
                dy = wrap_image(own_col(Y) - other_row(Y), cfg["box_y"])
                dz = own_col(Z) - other_row(Z)
                r2 = dx * dx + dy * dy + dz * dz
                same = (own_col(GRP) == other_row(GRP)) & (own_col(GRP) >= 0.0)
                site = (own_col(SIT) == other_row(SIT)) & (own_col(SIT) >= 0.0)
                drop = (site & jnp.logical_not(same)) | (diagonal & (index == own))
                lam_a, lam_b = own_col(LAM), other_row(LAM)
                s = jnp.where(same, lam_a, lam_a * lam_b)
                w = jnp.where(same, 0.5, lam_b)
                e = own_col(STR) * other_row(STR)
                q = own_col(CHG) * other_row(CHG)
                rs = lax.rsqrt(1.0 + 0.5 * (1.0 - s) + r2)
                t = rs * rs * rs
                a = e * t
                b = s * t * (a + 0.25 * q)
                sens = rs * (a + q) + b
                b = jnp.where(drop, 0.0, b)
                sens = jnp.where(drop, 0.0, sens * w)
                return fx + b * dx, fy + b * dy, fz + b * dz, fd + sens

            zero = jnp.zeros((chunk, lanes), jnp.float32)
            sums = lax.fori_loop(0, count, one_partner, (zero, zero, zero, zero))
            for row, value in enumerate(sums):
                fcol_ref[pl.ds(start, chunk), row : row + 1] = jnp.sum(
                    value, axis=1, keepdims=True
                )
            return carry

        lax.fori_loop(0, lanes // chunk, one_chunk, 0)
        forces = fcol_ref[...].T
        finish_tile(
            cfg, tile, 4.0 * forces[0:3, :], forces[3:4, :], block,
            ins, outs, sub_iota,
        )
        return carry

    lax.fori_loop(0, tiles, one_tile, 0)


def finish_tile(cfg, tile, forces, drive, block, ins, outs, sub_iota):
    vel_ref, noise_ref, inv_ref = ins
    pay_ref, velo_ref, sum_ref = outs
    damping = math.exp(-friction_rate * step_size)
    inverse = inv_ref[tile]
    speeds = (
        damping * vel_ref[tile, 0:3, :]
        + step_size * forces * inverse
        + jnp.sqrt((1.0 - damping**2) * inverse) * noise_ref[0, tile]
    )
    velo_ref[tile] = speeds
    pay_ref[tile, 0:3, :] = block[0:3, :] + step_size * speeds
    group = block[GRP : GRP + 1, :]
    for site in range(NSITE):
        sum_ref[site] += jnp.where(group == sub_iota + float(site * NSUB), drive, 0.0)


def pay_sums(cfg, pay_ref, sum_ref):
    lanes = cfg["lanes"]
    share = lanes // NSITE
    lane_site = lax.broadcasted_iota(jnp.int32, (NSUB, lanes), 1) // share
    packed = jnp.zeros((NSUB, lanes), jnp.float32)
    for site in range(NSITE):
        folded = sum_ref[site]
        width = lanes
        while width > share:
            width //= 2
            folded = folded + pltpu.roll(folded, width, 1)
        packed = packed + jnp.where(lane_site == site, folded, 0.0)
    for sub in range(cfg["tiles"]):
        pay_ref[sub, 3:4, :] = (
            packed[sub : sub + 1, :] if sub < NSUB else jnp.zeros((1, lanes), jnp.float32)
        )


def step_call(cfg, moment, count, parts, places, blocks, stats, totals, vel, ang, noise, anoise, inverse):
    tiles, lanes = cfg["tiles"], cfg["lanes"]
    nb = cfg["blocks"]
    vmem = pl.BlockSpec(memory_space=pltpu.VMEM)
    smem = pl.BlockSpec(memory_space=pltpu.SMEM)
    noise_spec = pl.BlockSpec((1, tiles, 3, lanes), lambda i: (moment, 0, 0, 0))

    return pl.pallas_call(
        functools.partial(step_kernel, cfg, moment),
        grid=(1,),
        out_shape=(
            jax.ShapeDtypeStruct((tiles, 4, lanes), jnp.float32),
            jax.ShapeDtypeStruct((tiles, 3, lanes), jnp.float32),
            jax.ShapeDtypeStruct((2, NSITE, NSUB, lanes), jnp.float32),
        ),
        in_specs=[smem, smem, smem] + [vmem] * (2 * nb + 3) + [noise_spec, vmem, vmem],
        out_specs=(vmem, vmem, vmem),
        scratch_shapes=[
            pltpu.VMEM((cfg["pool"], 8, lanes), jnp.float32),
            pltpu.VMEM((lanes, 8), jnp.float32),
            pltpu.VMEM((lanes, 8), jnp.float32),
            pltpu.VMEM((NSITE, NSUB, lanes), jnp.float32),
            pltpu.VMEM((cfg["pool"], lanes, cfg["depth"]), jnp.bfloat16),
            pltpu.VMEM((cfg["pool"], lanes, 4 * lanes), jnp.float32),
            pltpu.VMEM((cfg["depth"], 4 * lanes), jnp.bfloat16),
            pltpu.VMEM((cfg["depth"], 4 * lanes), jnp.bfloat16),
        ],
        name="langevin_step",
    )(count, parts, places, *blocks, *stats, totals, vel, ang, noise, anoise, inverse)


def per_device(
    positions,
    velocities,
    lambda_theta,
    theta_velocity,
    source_slot,
    atom_noise,
    theta_noise,
    charges,
    strengths,
    inverse_mass,
    atom_site,
    atom_sub,
    partners,
):
    count_x, count_y = lax.axis_size("gx"), lax.axis_size("gy")
    peers = lax.axis_size("walker")
    rows_x, rows_y, lanes = charges.shape
    tiles = rows_x * rows_y
    offsets = neighbour_offsets(count_x, count_y)
    cfg = dict(
        blocks=1 + len(offsets),
        covered=1 + len(offsets) == count_x * count_y,
        tiles=tiles,
        lanes=lanes,
        rows_y=rows_y,
        pool=(rows_x + 2) * (rows_y + 2),
        sources=pool_sources(rows_x, rows_y, count_x, count_y, offsets),
        depth=128,
        roomy=min(rows_x * count_x, rows_y * count_y) >= 8,
        box_x=float(rows_x * count_x),
        box_y=float(rows_y * count_y),
        angle_mass=rows_x * count_x * rows_y * count_y * lanes * theta_share,
    )

    def gather_blocks(value):
        return [value] + [shifted(value, offset, count_x, count_y) for offset in offsets]

    is_group = atom_site < NSITE
    groups = jnp.where(is_group, atom_site * NSUB + atom_sub, -1)
    sites = jnp.where(is_group, atom_site, -1)
    stat = jnp.stack(
        [charges, strengths, groups.astype(jnp.float32), sites.astype(jnp.float32)], axis=2
    ).reshape(tiles, 4, lanes)
    stats = gather_blocks(stat)

    mine = source_slot[lax.axis_index("walker")]
    angles = jnp.stack([lambda_theta[0], theta_velocity[0]]).reshape(1, 2 * NSITE * NSUB)
    angles = jnp.pad(angles, ((0, 0), (0, lanes - 2 * NSITE * NSUB)))
    extra = jnp.broadcast_to(angles[:, None, :], (tiles, 1, lanes))
    first = jnp.concatenate([positions.reshape(tiles, 3, lanes), extra], axis=1)
    second = velocities.reshape(tiles, 3, lanes)

    def picked(value):
        everyone = lax.all_to_all(
            jnp.broadcast_to(value, (peers,) + value.shape), "walker", 0, 0, tiled=True
        )
        return lax.dynamic_index_in_dim(everyone, mine, 0, keepdims=False)

    start = picked(first)
    vel = picked(second)
    ang = start[0, 3, : 2 * NSITE * NSUB].reshape(2, NSITE, NSUB, 1)
    ang = jnp.broadcast_to(ang, (2, NSITE, NSUB, lanes))
    anoise = jnp.broadcast_to(theta_noise[0][..., None], (STEPS, NSITE, NSUB, lanes))
    noise = atom_noise.reshape(STEPS, tiles, 3, lanes)
    inverse = inverse_mass.reshape(tiles, 1, lanes)
    parts = partners.reshape(tiles, -1)
    count = jnp.sum((parts >= 0).astype(jnp.int32), axis=1)

    def line(axis, rows, count):
        at = lax.axis_index(axis)
        ring = jnp.arange(rows + 2)
        turn = jnp.where(ring == 0, jnp.where(at == 0, -1.0, 0.0), 0.0)
        turn = jnp.where(ring == rows + 1, jnp.where(at == count - 1, 1.0, 0.0), turn)
        middle = at.astype(jnp.float32) * rows + 0.5 * rows
        shift = turn * (rows * count) - middle
        return shift, shift - (ring.astype(jnp.float32) - 0.5 - 0.5 * rows)

    shift_x, cell_x = line("gx", rows_x, count_x)
    shift_y, cell_y = line("gy", rows_y, count_y)
    places = jnp.stack(
        [
            jnp.broadcast_to(value, (rows_x + 2, rows_y + 2)).reshape(-1)
            for value in (shift_x[:, None], shift_y, cell_x[:, None], cell_y)
        ]
    )

    pay = start
    for moment in range(STEPS):
        blocks = gather_blocks(pay)
        if moment > 0 and not cfg["covered"]:
            totals = lax.psum(pay[:NSUB, 3, :], ("gx", "gy"))
        else:
            totals = jnp.zeros((NSUB, lanes), jnp.float32)
        pay, vel, ang = step_call(
            cfg, moment, count, parts, places, blocks, stats, totals, vel, ang, noise, anoise, inverse
        )
    packed = pay[:NSUB, 3, :]
    if cfg["covered"]:
        totals = packed
        for offset in offsets:
            totals = totals + shifted(packed, offset, count_x, count_y)
    else:
        totals = lax.psum(packed, ("gx", "gy"))
    angles, aspeeds = angle_step(ang[0], ang[1], totals, anoise[STEPS - 1], cfg["angle_mass"])
    displacement = (pay[:, 0:3, :] - start[:, 0:3, :]).reshape(positions.shape)
    return (
        displacement,
        vel.reshape(velocities.shape),
        angles[None, :, :, 0],
        aspeeds[None, :, :, 0],
    )


def solution(mesh):
    in_specs = (
        P("walker", "gx", "gy", None, None),
        P("walker", "gx", "gy", None, None),
        P("walker", None, None),
        P("walker", None, None),
        P(),
        P("walker", None, "gx", "gy", None, None),
        P("walker", None, None, None),
        P("gx", "gy", None),
        P("gx", "gy", None),
        P("gx", "gy", None),
        P("gx", "gy", None),
        P("gx", "gy", None),
        P("gx", "gy", None),
    )
    out_specs = (
        P("walker", "gx", "gy", None, None),
        P("walker", "gx", "gy", None, None),
        P("walker", None, None),
        P("walker", None, None),
    )
    return jax.shard_map(
        per_device, mesh=mesh, in_specs=in_specs, out_specs=out_specs, check_vma=False
    )
```

```python
import functools
import math

import jax
import jax.numpy as jnp
from jax import lax
from jax.experimental import pallas as pl
from jax.experimental.pallas import tpu as pltpu
from jax.sharding import PartitionSpec as P

NSITE = 4
NSUB = 8
STEPS = 4

step_size = 0.02
friction_rate = 1.0
theta_friction = 20.0
soft_alpha = 0.5
soft_beta = 0.5
theta_share = 1.0 / 1024.0

MIDDLE_Z = 1.0
REACH = 1.49
FAR = 2.0**126
GROUP = 9
ROWS = 16

X, Y, Z, LAM, CHG, STR, GRP, SIT = range(8)


def wrap_image(offset, length):
    shift = jnp.where(offset > 0.5 * length, length, 0.0)
    shift = jnp.where(offset < -0.5 * length, -length, shift)
    return offset - shift


def neighbour_offsets(count_x, count_y):
    found = []
    for di in (-1, 0, 1):
        for dj in (-1, 0, 1):
            key = (di % count_x, dj % count_y)
            if key != (0, 0) and key not in found:
                found.append(key)
    return found


def shifted(value, offset, count_x, count_y):
    pairs = []
    for i in range(count_x):
        for j in range(count_y):
            source = ((i + offset[0]) % count_x) * count_y + (j + offset[1]) % count_y
            pairs.append((source, i * count_y + j))
    return lax.ppermute(value, ("gx", "gy"), pairs)


def pool_sources(rows_x, rows_y, count_x, count_y, offsets):
    sources = []
    for pi in range(rows_x + 2):
        for pj in range(rows_y + 2):
            di = -1 if pi == 0 else (1 if pi == rows_x + 1 else 0)
            dj = -1 if pj == 0 else (1 if pj == rows_y + 1 else 0)
            key = (di % count_x, dj % count_y)
            block = 0 if key == (0, 0) else 1 + offsets.index(key)
            tile = ((pi - 1) % rows_x) * rows_y + (pj - 1) % rows_y
            sources.append((block, tile))
    return sources


def softmax_angles(angles):
    weights = jnp.exp(angles)
    return weights / jnp.sum(weights, axis=1, keepdims=True)


def angle_step(angles, speeds, packed, noise, angle_mass):
    lanes = packed.shape[1]
    share = lanes // NSITE
    lane_site = lax.broadcasted_iota(jnp.int32, packed.shape, 1) // share
    lambdas = softmax_angles(angles)
    totals = jnp.stack(
        [
            jnp.broadcast_to(
                jnp.sum(jnp.where(lane_site == site, packed, 0.0), axis=1, keepdims=True),
                packed.shape,
            )
            for site in range(NSITE)
        ]
    )
    angle_damping = math.exp(-theta_friction * step_size)
    force = -lambdas * (totals - jnp.sum(lambdas * totals, axis=1, keepdims=True))
    speeds = (
        angle_damping * speeds
        + step_size * force / angle_mass
        + math.sqrt((1.0 - angle_damping**2) / angle_mass) * noise
    )
    return angles + step_size * speeds, speeds


def step_kernel(cfg, moment, *refs):
    nb = cfg["blocks"]
    tiles, pool = cfg["tiles"], cfg["pool"]
    lanes = cfg["lanes"]
    count_ref, part_ref, off_ref = refs[:3]
    refs = refs[1:]
    coord_refs = refs[2 : 2 + nb]
    stat_refs = refs[2 + nb : 2 + 2 * nb]
    tot_ref, vel_ref, ang_ref, noise_ref, anoise_ref, inv_ref = refs[2 + 2 * nb : 8 + 2 * nb]
    pay_ref, velo_ref, ango_ref = refs[8 + 2 * nb : 11 + 2 * nb]
    pool_ref, col_ref, fcol_ref, sum_ref, feat_ref, wide_ref, rhs_ref, coef_ref = refs[11 + 2 * nb :]

    angles, aspeeds = ang_ref[0], ang_ref[1]
    if moment > 0:
        if cfg["covered"]:
            packed = coord_refs[0][0:NSUB, 3, :]
            for ref in coord_refs[1:]:
                packed = packed + ref[0:NSUB, 3, :]
        else:
            packed = tot_ref[...]
        angles, aspeeds = angle_step(
            angles, aspeeds, packed, anoise_ref[moment - 1], cfg["angle_mass"]
        )
    ango_ref[0] = angles
    ango_ref[1] = aspeeds
    lambdas = softmax_angles(angles)

    sub_iota = lax.broadcasted_iota(jnp.int32, (NSUB, lanes), 0).astype(jnp.float32)
    worst = jnp.zeros((3, lanes), jnp.float32)
    row3 = lax.broadcasted_iota(jnp.int32, (3, lanes), 0)
    for index, (block, tile) in enumerate(cfg["sources"]):
        stat = stat_refs[block][tile]
        cell = jnp.where(row3 == 0, off_ref[2, index], off_ref[3, index])
        cell = jnp.where(row3 == 2, -MIDDLE_Z, cell)
        worst = jnp.maximum(worst, jnp.abs(coord_refs[block][tile, 0:3, :] + cell))
        pool_ref[index, 0:3, :] = coord_refs[block][tile, 0:3, :]
        pool_ref[index, 4:8, :] = stat
        group = stat[2:3, :]
        lam = jnp.zeros((NSUB, lanes), jnp.float32)
        for site in range(NSITE):
            lam = lam + jnp.where(group == sub_iota + float(site * NSUB), lambdas[site], 0.0)
        lam = jnp.sum(lam, axis=0, keepdims=True)
        pool_ref[index, 3:4, :] = jnp.where(group >= 0.0, lam, 1.0)

    stray = jnp.max(worst * jnp.where(row3 == 2, 0.5, 1.0))
    sum_ref[...] = jnp.zeros_like(sum_ref)
    fcol_ref[...] = jnp.zeros_like(fcol_ref)
    ins = (vel_ref, noise_ref, inv_ref)
    outs = (pay_ref, velo_ref, sum_ref)
    near = cfg["roomy"] & (stray < REACH)

    @pl.when(near)
    def _():
        near_forces(
            cfg, lambdas, count_ref, part_ref, off_ref, pool_ref, feat_ref, wide_ref, rhs_ref,
            coef_ref, ins, outs, sub_iota,
        )

    @pl.when(jnp.logical_not(near))
    def _():
        any_forces(cfg, count_ref, part_ref, pool_ref, col_ref, fcol_ref, ins, outs, sub_iota)

    pay_sums(cfg, pay_ref, sum_ref)


def split3(value):
    high = value.astype(jnp.bfloat16).astype(jnp.float32)
    rest = value - high
    middle = rest.astype(jnp.bfloat16).astype(jnp.float32)
    return high, middle, rest - middle


def by_group(lambdas_of_site, group, sub_iota):
    return [
        jnp.where(group == sub_iota + float(site * NSUB), lambdas_of_site[site], 0.0)
        for site in range(NSITE)
    ]


def near_forces(
    cfg, lambdas, count_ref, part_ref, off_ref, pool_ref, feat_ref, wide_ref, rhs_ref,
    coef_ref, ins, outs, sub_iota,
):
    lanes = cfg["lanes"]
    depth = cfg["depth"]
    rows = lax.broadcasted_iota(jnp.int32, (8, lanes), 0)
    ones = jnp.ones((NSUB, lanes), jnp.float32)
    nothing = jnp.zeros((8, lanes), jnp.float32)
    pad = [nothing] * ((depth - 6 * 8 - 2 * NSITE * NSUB) // 8)

    pick_rows = lax.broadcasted_iota(jnp.int32, (depth, lanes), 0)
    hit = (pick_rows == 7) | (pick_rows == 16 + 7) | (pick_rows == 40 + 7)
    pick = jnp.where(hit, 1.0, 0.0).astype(jnp.bfloat16)

    def centred(index):
        block = pool_ref[index]
        shift = jnp.where(rows == 0, off_ref[0, index], 0.0)
        shift = jnp.where(rows == 1, off_ref[1, index], shift)
        shift = jnp.where(rows == 2, -MIDDLE_Z, shift)
        moved = block + shift
        square = jnp.where(rows < 3, moved * moved, 0.0)
        return block, moved, jnp.sum(square, axis=0, keepdims=True)

    def table_dot(features, ref):
        table = jnp.concatenate([ref[c] for c in range(ref.shape[0])], axis=1)
        return jnp.dot(features, table, preferred_element_type=jnp.float32)

    def some_pool(k, carry):
        for u in range(cfg["pool_group"]):
            one_pool(k * cfg["pool_group"] + u)
        return carry

    def one_pool(index):
        block, moved, norm = centred(index)
        table = jnp.where(rows == 5, norm, moved)
        table = jnp.where(rows == 6, 1.0, table)
        table = jnp.where(rows == 7, block[STR : STR + 1, :], table)
        high, middle, low = split3(table)
        member = by_group([ones] * NSITE, block[GRP : GRP + 1, :], sub_iota)
        features = jnp.concatenate(
            [high, high, middle, middle, high, low] + member + member + pad, axis=0
        )
        features = features.T.astype(jnp.bfloat16)
        feat_ref[index] = features
        wide_ref[index] = jnp.dot(features, pick, preferred_element_type=jnp.float32)
        coef = jnp.concatenate([high, middle, low, nothing], axis=0).astype(jnp.bfloat16)
        coef_ref[index] = jnp.concatenate([coef, coef], axis=1)

    lax.fori_loop(0, cfg["pool"] // cfg["pool_group"], some_pool, 0)
    none_columns = lax.broadcasted_iota(jnp.int32, (lanes, depth), 1)
    feat_ref[cfg["pool"]] = jnp.where(none_columns == 6, 1.0, 0.0).astype(jnp.bfloat16)
    wide_ref[cfg["pool"]] = jnp.zeros((lanes, lanes), jnp.float32)
    coef_ref[cfg["pool"]] = jnp.zeros((32, 2 * lanes), jnp.bfloat16)

    spread = [lam - lam * lam for lam in lambdas]
    half = [0.5 - lam for lam in lambdas]

    def one_tile(tile, carry):
        own = (tile // cfg["rows_y"] + 1) * (cfg["rows_y"] + 2) + tile % cfg["rows_y"] + 1
        block, moved, norm = centred(own)
        group, site_row = block[GRP : GRP + 1, :], block[SIT : SIT + 1, :]
        lam, charge, strength = (block[r : r + 1, :] for r in (LAM, CHG, STR))
        ratio = charge / strength

        gap = jnp.where(rows < 3, -2.0 * moved, 0.0)
        gap = jnp.where(rows == 3, -0.5 * lam, gap)
        gap = jnp.where(rows == 5, 1.0, gap)
        gap = jnp.where(rows == 6, norm + 1.5, gap)
        pair = by_group(spread, group, sub_iota)
        far = [
            jnp.where(
                (site_row == float(site)) & (group != sub_iota + float(site * NSUB)), FAR, 0.0
            )
            for site in range(NSITE)
        ]
        columns = (
            (gap, [f - 0.5 * p for f, p in zip(far, pair)]),
            (jnp.where(rows == 3, lam, 0.0), pair),
            (jnp.where(rows == 3, 1.0, 0.0), by_group(half, group, sub_iota)),
            (jnp.where(rows == 4, ratio, 0.0), [nothing] * NSITE),
        )
        for column, (table, member) in enumerate(columns):
            high, middle, low = split3(table)
            tops = [m.astype(jnp.bfloat16).astype(jnp.float32) for m in member]
            rests = [m - t for m, t in zip(member, tops)]
            rhs_ref[column] = jnp.concatenate(
                [high, middle, high, middle, low, high] + tops + rests + pad, axis=0
            ).astype(jnp.bfloat16)

        def some_partners(k, sums):
            indices = [part_ref[tile, GROUP * k + u] for u in range(GROUP)]
            outs = [table_dot(feat_ref[index], rhs_ref) for index in indices]
            moments, fd = sums
            for index, out in zip(indices, outs):
                tops, rests = [], []
                for i in range(lanes // ROWS):
                    here = slice(ROWS * i, ROWS * i + ROWS)
                    gap2, s, w, q = (out[here, c * lanes : (c + 1) * lanes] for c in range(4))
                    eb = wide_ref[index, here, :]
                    rs = lax.rsqrt(gap2)
                    t = rs * rs * rs
                    a = eb * t
                    b = (s * t) * (a + 0.25 * q)
                    sens = (rs * (a + q) + b) * w
                    for j in range(ROWS // 8):
                        fd = fd + sens[8 * j : 8 * j + 8, :]
                    top = b.astype(jnp.bfloat16)
                    tops.append(top)
                    rests.append((b - top.astype(jnp.float32)).astype(jnp.bfloat16))
                moments = moments + jnp.dot(
                    coef_ref[index],
                    jnp.concatenate(tops + rests, axis=0),
                    preferred_element_type=jnp.float32,
                )
            return moments, fd

        groups = (count_ref[tile] + GROUP - 1) // GROUP
        moments, fd = lax.fori_loop(
            0, groups, some_partners, (jnp.zeros((32, lanes), jnp.float32), nothing)
        )
        moments = moments[0:8] + moments[8:16] + moments[16:24]
        fd = jnp.sum(fd, axis=0, keepdims=True)
        forces = moved[0:3, :] * moments[6:7, :] - moments[0:3, :]
        rs = lax.rsqrt(1.5 - 0.5 * lam)
        t = rs * rs * rs
        a, q = strength * t, ratio * charge
        itself = rs * (a + q) + lam * t * (a + 0.25 * q)
        drive = strength * (fd - 0.5 * itself)
        finish_tile(cfg, tile, (4.0 * strength) * forces, drive, block, ins, outs, sub_iota)
        return carry

    lax.fori_loop(0, cfg["tiles"], one_tile, 0)


def any_forces(cfg, count_ref, part_ref, pool_ref, col_ref, fcol_ref, ins, outs, sub_iota):
    tiles, lanes = cfg["tiles"], cfg["lanes"]
    chunk = 32

    def one_tile(tile, carry):
        own = (tile // cfg["rows_y"] + 1) * (cfg["rows_y"] + 2) + tile % cfg["rows_y"] + 1
        block = pool_ref[own]
        col_ref[...] = block.T
        count = count_ref[tile]

        def one_chunk(c, carry):
            start = pl.multiple_of(c * chunk, chunk)
            cols = col_ref[pl.ds(start, chunk), :]
            lanes_iota = lax.broadcasted_iota(jnp.int32, (chunk, lanes), 1)
            diagonal = lanes_iota == lax.broadcasted_iota(jnp.int32, (chunk, lanes), 0) + start

            def one_partner(k, sums):
                fx, fy, fz, fd = sums
                index = part_ref[tile, k]
                other = pool_ref[index]

                def own_col(row):
                    return cols[:, row : row + 1]

                def other_row(row):
                    return other[row : row + 1, :]

                dx = wrap_image(own_col(X) - other_row(X), cfg["box_x"])
                dy = wrap_image(own_col(Y) - other_row(Y), cfg["box_y"])
                dz = own_col(Z) - other_row(Z)
                r2 = dx * dx + dy * dy + dz * dz
                same = (own_col(GRP) == other_row(GRP)) & (own_col(GRP) >= 0.0)
                site = (own_col(SIT) == other_row(SIT)) & (own_col(SIT) >= 0.0)
                drop = (site & jnp.logical_not(same)) | (diagonal & (index == own))
                lam_a, lam_b = own_col(LAM), other_row(LAM)
                s = jnp.where(same, lam_a, lam_a * lam_b)
                w = jnp.where(same, 0.5, lam_b)
                e = own_col(STR) * other_row(STR)
                q = own_col(CHG) * other_row(CHG)
                rs = lax.rsqrt(1.0 + 0.5 * (1.0 - s) + r2)
                t = rs * rs * rs
                a = e * t
                b = s * t * (a + 0.25 * q)
                sens = rs * (a + q) + b
                b = jnp.where(drop, 0.0, b)
                sens = jnp.where(drop, 0.0, sens * w)
                return fx + b * dx, fy + b * dy, fz + b * dz, fd + sens

            zero = jnp.zeros((chunk, lanes), jnp.float32)
            sums = lax.fori_loop(0, count, one_partner, (zero, zero, zero, zero))
            for row, value in enumerate(sums):
                fcol_ref[pl.ds(start, chunk), row : row + 1] = jnp.sum(
                    value, axis=1, keepdims=True
                )
            return carry

        lax.fori_loop(0, lanes // chunk, one_chunk, 0)
        forces = fcol_ref[...].T
        finish_tile(
            cfg, tile, 4.0 * forces[0:3, :], forces[3:4, :], block,
            ins, outs, sub_iota,
        )
        return carry

    lax.fori_loop(0, tiles, one_tile, 0)


def finish_tile(cfg, tile, forces, drive, block, ins, outs, sub_iota):
    vel_ref, noise_ref, inv_ref = ins
    pay_ref, velo_ref, sum_ref = outs
    damping = math.exp(-friction_rate * step_size)
    inverse = inv_ref[tile]
    speeds = (
        damping * vel_ref[tile, 0:3, :]
        + step_size * forces * inverse
        + jnp.sqrt((1.0 - damping**2) * inverse) * noise_ref[0, tile]
    )
    velo_ref[tile] = speeds
    pay_ref[tile, 0:3, :] = block[0:3, :] + step_size * speeds
    group = block[GRP : GRP + 1, :]
    for site in range(NSITE):
        sum_ref[site] += jnp.where(group == sub_iota + float(site * NSUB), drive, 0.0)


def pay_sums(cfg, pay_ref, sum_ref):
    lanes = cfg["lanes"]
    share = lanes // NSITE
    lane_site = lax.broadcasted_iota(jnp.int32, (NSUB, lanes), 1) // share
    packed = jnp.zeros((NSUB, lanes), jnp.float32)
    for site in range(NSITE):
        folded = sum_ref[site]
        width = lanes
        while width > share:
            width //= 2
            folded = folded + pltpu.roll(folded, width, 1)
        packed = packed + jnp.where(lane_site == site, folded, 0.0)
    for sub in range(cfg["tiles"]):
        pay_ref[sub, 3:4, :] = (
            packed[sub : sub + 1, :] if sub < NSUB else jnp.zeros((1, lanes), jnp.float32)
        )


def step_call(cfg, moment, count, parts, places, blocks, stats, totals, vel, ang, noise, anoise, inverse):
    tiles, lanes = cfg["tiles"], cfg["lanes"]
    nb = cfg["blocks"]
    vmem = pl.BlockSpec(memory_space=pltpu.VMEM)
    smem = pl.BlockSpec(memory_space=pltpu.SMEM)
    noise_spec = pl.BlockSpec((1, tiles, 3, lanes), lambda i: (moment, 0, 0, 0))

    return pl.pallas_call(
        functools.partial(step_kernel, cfg, moment),
        grid=(1,),
        out_shape=(
            jax.ShapeDtypeStruct((tiles, 4, lanes), jnp.float32),
            jax.ShapeDtypeStruct((tiles, 3, lanes), jnp.float32),
            jax.ShapeDtypeStruct((2, NSITE, NSUB, lanes), jnp.float32),
        ),
        in_specs=[smem, smem, smem] + [vmem] * (2 * nb + 3) + [noise_spec, vmem, vmem],
        out_specs=(vmem, vmem, vmem),
        scratch_shapes=[
            pltpu.VMEM((cfg["pool"], 8, lanes), jnp.float32),
            pltpu.VMEM((lanes, 8), jnp.float32),
            pltpu.VMEM((lanes, 8), jnp.float32),
            pltpu.VMEM((NSITE, NSUB, lanes), jnp.float32),
            pltpu.VMEM((cfg["pool"] + 1, lanes, cfg["depth"]), jnp.bfloat16),
            pltpu.VMEM((cfg["pool"] + 1, lanes, lanes), jnp.float32),
            pltpu.VMEM((4, cfg["depth"], lanes), jnp.bfloat16),
            pltpu.VMEM((cfg["pool"] + 1, 32, 2 * lanes), jnp.bfloat16),
        ],
        name="langevin_step",
    )(count, parts, places, *blocks, *stats, totals, vel, ang, noise, anoise, inverse)


def make_cfg(rows_x, rows_y, lanes, count_x, count_y, offsets):
    tiles = rows_x * rows_y
    return dict(
        blocks=1 + len(offsets),
        covered=1 + len(offsets) == count_x * count_y,
        tiles=tiles,
        lanes=lanes,
        rows_y=rows_y,
        pool=(rows_x + 2) * (rows_y + 2),
        sources=pool_sources(rows_x, rows_y, count_x, count_y, offsets),
        depth=128,
        pool_group=next(g for g in (12, 6, 4, 3, 2, 1) if (rows_x + 2) * (rows_y + 2) % g == 0),
        roomy=min(rows_x * count_x, rows_y * count_y) >= 8,
        box_x=float(rows_x * count_x),
        box_y=float(rows_y * count_y),
        angle_mass=rows_x * count_x * rows_y * count_y * lanes * theta_share,
    )


def per_device(
    positions,
    velocities,
    lambda_theta,
    theta_velocity,
    source_slot,
    atom_noise,
    theta_noise,
    charges,
    strengths,
    inverse_mass,
    atom_site,
    atom_sub,
    partners,
):
    count_x, count_y = lax.axis_size("gx"), lax.axis_size("gy")
    peers = lax.axis_size("walker")
    rows_x, rows_y, lanes = charges.shape
    tiles = rows_x * rows_y
    offsets = neighbour_offsets(count_x, count_y)
    cfg = make_cfg(rows_x, rows_y, lanes, count_x, count_y, offsets)

    def gather_blocks(value):
        return [value] + [shifted(value, offset, count_x, count_y) for offset in offsets]

    is_group = atom_site < NSITE
    groups = jnp.where(is_group, atom_site * NSUB + atom_sub, -1)
    sites = jnp.where(is_group, atom_site, -1)
    stat = jnp.stack(
        [charges, strengths, groups.astype(jnp.float32), sites.astype(jnp.float32)], axis=2
    ).reshape(tiles, 4, lanes)
    stats = gather_blocks(stat)

    mine = source_slot[lax.axis_index("walker")]
    angles = jnp.stack([lambda_theta[0], theta_velocity[0]]).reshape(1, 2 * NSITE * NSUB)
    angles = jnp.pad(angles, ((0, 0), (0, lanes - 2 * NSITE * NSUB)))
    extra = jnp.broadcast_to(angles[:, None, :], (tiles, 1, lanes))
    first = jnp.concatenate([positions.reshape(tiles, 3, lanes), extra], axis=1)
    second = velocities.reshape(tiles, 3, lanes)

    def picked(value):
        everyone = lax.all_to_all(
            jnp.broadcast_to(value, (peers,) + value.shape), "walker", 0, 0, tiled=True
        )
        return lax.dynamic_index_in_dim(everyone, mine, 0, keepdims=False)

    start = picked(first)
    vel = picked(second)
    ang = start[0, 3, : 2 * NSITE * NSUB].reshape(2, NSITE, NSUB, 1)
    ang = jnp.broadcast_to(ang, (2, NSITE, NSUB, lanes))
    anoise = jnp.broadcast_to(theta_noise[0][..., None], (STEPS, NSITE, NSUB, lanes))
    noise = atom_noise.reshape(STEPS, tiles, 3, lanes)
    inverse = inverse_mass.reshape(tiles, 1, lanes)
    parts = partners.reshape(tiles, -1)
    count = jnp.sum((parts >= 0).astype(jnp.int32), axis=1)
    parts = jnp.where(parts < 0, cfg["pool"], parts)
    parts = jnp.pad(
        parts, ((0, 0), (0, -parts.shape[1] % GROUP)), constant_values=cfg["pool"]
    )

    def line(axis, rows, count):
        at = lax.axis_index(axis)
        ring = jnp.arange(rows + 2)
        turn = jnp.where(ring == 0, jnp.where(at == 0, -1.0, 0.0), 0.0)
        turn = jnp.where(ring == rows + 1, jnp.where(at == count - 1, 1.0, 0.0), turn)
        middle = at.astype(jnp.float32) * rows + 0.5 * rows
        shift = turn * (rows * count) - middle
        return shift, shift - (ring.astype(jnp.float32) - 0.5 - 0.5 * rows)

    shift_x, cell_x = line("gx", rows_x, count_x)
    shift_y, cell_y = line("gy", rows_y, count_y)
    places = jnp.stack(
        [
            jnp.broadcast_to(value, (rows_x + 2, rows_y + 2)).reshape(-1)
            for value in (shift_x[:, None], shift_y, cell_x[:, None], cell_y)
        ]
    )

    pay = start
    for moment in range(STEPS):
        blocks = gather_blocks(pay)
        if moment > 0 and not cfg["covered"]:
            totals = lax.psum(pay[:NSUB, 3, :], ("gx", "gy"))
        else:
            totals = jnp.zeros((NSUB, lanes), jnp.float32)
        pay, vel, ang = step_call(
            cfg, moment, count, parts, places, blocks, stats, totals, vel, ang, noise, anoise, inverse
        )
    packed = pay[:NSUB, 3, :]
    if cfg["covered"]:
        totals = packed
        for offset in offsets:
            totals = totals + shifted(packed, offset, count_x, count_y)
    else:
        totals = lax.psum(packed, ("gx", "gy"))
    angles, aspeeds = angle_step(ang[0], ang[1], totals, anoise[STEPS - 1], cfg["angle_mass"])
    displacement = (pay[:, 0:3, :] - start[:, 0:3, :]).reshape(positions.shape)
    return (
        displacement,
        vel.reshape(velocities.shape),
        angles[None, :, :, 0],
        aspeeds[None, :, :, 0],
    )


def solution(mesh):
    in_specs = (
        P("walker", "gx", "gy", None, None),
        P("walker", "gx", "gy", None, None),
        P("walker", None, None),
        P("walker", None, None),
        P(),
        P("walker", None, "gx", "gy", None, None),
        P("walker", None, None, None),
        P("gx", "gy", None),
        P("gx", "gy", None),
        P("gx", "gy", None),
        P("gx", "gy", None),
        P("gx", "gy", None),
        P("gx", "gy", None),
    )
    out_specs = (
        P("walker", "gx", "gy", None, None),
        P("walker", "gx", "gy", None, None),
        P("walker", None, None),
        P("walker", None, None),
    )
    return jax.shard_map(
        per_device, mesh=mesh, in_specs=in_specs, out_specs=out_specs, check_vma=False
    )
```

```python
import functools
import math

import jax
import jax.numpy as jnp
from jax import lax
from jax.experimental import pallas as pl
from jax.experimental.pallas import tpu as pltpu
from jax.sharding import PartitionSpec as P

NSITE = 4
NSUB = 8
STEPS = 4

step_size = 0.02
friction_rate = 1.0
theta_friction = 20.0
soft_alpha = 0.5
soft_beta = 0.5
theta_share = 1.0 / 1024.0

MIDDLE_Z = 1.0
REACH = 1.49
FAR = 2.0**126
ROWS = 16

X, Y, Z, LAM, CHG, STR, GRP, SIT = range(8)


def wrap_image(offset, length):
    shift = jnp.where(offset > 0.5 * length, length, 0.0)
    shift = jnp.where(offset < -0.5 * length, -length, shift)
    return offset - shift


def neighbour_offsets(count_x, count_y):
    found = []
    for di in (-1, 0, 1):
        for dj in (-1, 0, 1):
            key = (di % count_x, dj % count_y)
            if key != (0, 0) and key not in found:
                found.append(key)
    return found


def shifted(value, offset, count_x, count_y):
    pairs = []
    for i in range(count_x):
        for j in range(count_y):
            source = ((i + offset[0]) % count_x) * count_y + (j + offset[1]) % count_y
            pairs.append((source, i * count_y + j))
    return lax.ppermute(value, ("gx", "gy"), pairs)


def pool_sources(rows_x, rows_y, count_x, count_y, offsets):
    sources = []
    for pi in range(rows_x + 2):
        for pj in range(rows_y + 2):
            di = -1 if pi == 0 else (1 if pi == rows_x + 1 else 0)
            dj = -1 if pj == 0 else (1 if pj == rows_y + 1 else 0)
            key = (di % count_x, dj % count_y)
            block = 0 if key == (0, 0) else 1 + offsets.index(key)
            tile = ((pi - 1) % rows_x) * rows_y + (pj - 1) % rows_y
            sources.append((block, tile))
    return sources


def softmax_angles(angles):
    weights = jnp.exp(angles)
    return weights / jnp.sum(weights, axis=1, keepdims=True)


def angle_step(angles, speeds, packed, noise, angle_mass):
    lanes = packed.shape[1]
    share = lanes // NSITE
    lane_site = lax.broadcasted_iota(jnp.int32, packed.shape, 1) // share
    lambdas = softmax_angles(angles)
    totals = jnp.stack(
        [
            jnp.broadcast_to(
                jnp.sum(jnp.where(lane_site == site, packed, 0.0), axis=1, keepdims=True),
                packed.shape,
            )
            for site in range(NSITE)
        ]
    )
    angle_damping = math.exp(-theta_friction * step_size)
    force = -lambdas * (totals - jnp.sum(lambdas * totals, axis=1, keepdims=True))
    speeds = (
        angle_damping * speeds
        + step_size * force / angle_mass
        + math.sqrt((1.0 - angle_damping**2) / angle_mass) * noise
    )
    return angles + step_size * speeds, speeds


def lane_column(row, first, sub_iota):
    lane = lax.broadcasted_iota(jnp.int32, sub_iota.shape, 1)
    hit = lane == lax.broadcasted_iota(jnp.int32, sub_iota.shape, 0) + first
    return jnp.broadcast_to(
        jnp.sum(jnp.where(hit, row, 0.0), axis=1, keepdims=True), sub_iota.shape
    )


def noise_table(anoise_ref, moment, sub_iota):
    tables = []
    for site in range(NSITE):
        table = jnp.zeros_like(sub_iota)
        for sub in range(NSUB):
            table = jnp.where(sub_iota == float(sub), anoise_ref[0, moment, site, sub], table)
        tables.append(table)
    return jnp.stack(tables)


def packed_totals(blocks, sub_iota):
    packed = blocks[0]
    for block in blocks[1:]:
        packed = packed + block
    return packed


def step_kernel(cfg, moment, *refs):
    nb = cfg["blocks"]
    lanes = cfg["lanes"]
    refs = list(refs)

    def take(n):
        taken, refs[:n] = refs[:n], []
        return taken

    part_ref, at_ref, anoise_ref = take(3)
    coord_refs = take(nb)
    (stat_ref,) = take(1) if moment > 0 else (None,)
    (tot_ref,) = take(1) if moment > 0 and not cfg["covered"] else (None,)
    vel_ref, noise_ref, inv_ref = take(3)
    (ang_ref,) = take(1) if moment > 0 else (None,)
    last = moment == STEPS - 1
    (start_ref,) = take(1) if last else (None,)
    (out_ref,) = take(1)
    velo_ref, ango_ref = take(2)
    (stato_ref,) = take(1) if moment == 0 else (None,)
    (sumo_ref,) = take(1) if last else (None,)
    pool_ref, col_ref, fcol_ref, sum_ref, feat_ref, wide_ref, rhs_ref, coef_ref, off_ref = take(9)

    sub_iota = lax.broadcasted_iota(jnp.int32, (NSUB, lanes), 0).astype(jnp.float32)
    if moment == 0:
        row = coord_refs[0][0, 3:4, :]
        angles, aspeeds = (
            jnp.stack(
                [
                    lane_column(row, (kind * NSITE + site) * NSUB, sub_iota)
                    for site in range(NSITE)
                ]
            )
            for kind in range(2)
        )
    else:
        angles, aspeeds = ang_ref[0], ang_ref[1]
        if cfg["covered"]:
            packed = packed_totals([ref[0:NSUB, 3, :] for ref in coord_refs], sub_iota)
        else:
            packed = tot_ref[...]
        angles, aspeeds = angle_step(
            angles, aspeeds, packed, noise_table(anoise_ref, moment - 1, sub_iota),
            cfg["angle_mass"],
        )
    ango_ref[0] = angles
    ango_ref[1] = aspeeds
    lambdas = softmax_angles(angles)

    def line(axis, rows, count):
        at = at_ref[axis]
        middle = at.astype(jnp.float32) * rows + 0.5 * rows
        shifts, cells = [], []
        for ring in range(rows + 2):
            turn = 0.0
            if ring == 0:
                turn = jnp.where(at == 0, -float(rows * count), 0.0)
            if ring == rows + 1:
                turn = jnp.where(at == count - 1, float(rows * count), 0.0)
            shifts.append(turn - middle)
            cells.append(turn - middle - (ring - 0.5 - 0.5 * rows))
        return shifts, cells

    shift_x, cell_x = line(0, cfg["rows_x"], cfg["count_x"])
    shift_y, cell_y = line(1, cfg["rows_y"], cfg["count_y"])
    worst = jnp.zeros((3, lanes), jnp.float32)
    row3 = lax.broadcasted_iota(jnp.int32, (3, lanes), 0)
    for index, (block, tile) in enumerate(cfg["sources"]):
        pi, pj = index // (cfg["rows_y"] + 2), index % (cfg["rows_y"] + 2)
        off_ref[0, index] = shift_x[pi]
        off_ref[1, index] = shift_y[pj]
        if moment == 0:
            stat = coord_refs[block][tile, 4:8, :]
            stato_ref[index] = stat
        else:
            stat = stat_ref[index]
        cell = jnp.where(row3 == 0, cell_x[pi], cell_y[pj])
        cell = jnp.where(row3 == 2, -MIDDLE_Z, cell)
        coords = coord_refs[block][tile, 0:3, :]
        worst = jnp.maximum(worst, jnp.abs(coords + cell))
        pool_ref[index, 0:3, :] = coords
        pool_ref[index, 4:8, :] = stat
        group = stat[2:3, :]
        lam = jnp.zeros((NSUB, lanes), jnp.float32)
        for site in range(NSITE):
            lam = lam + jnp.where(group == sub_iota + float(site * NSUB), lambdas[site], 0.0)
        lam = jnp.sum(lam, axis=0, keepdims=True)
        pool_ref[index, 3:4, :] = jnp.where(group >= 0.0, lam, 1.0)

    stray = jnp.max(worst * jnp.where(row3 == 2, 0.5, 1.0))
    sum_ref[...] = jnp.zeros_like(sum_ref)
    fcol_ref[...] = jnp.zeros_like(fcol_ref)
    ins = (vel_ref, noise_ref, inv_ref, start_ref)
    outs = (out_ref, velo_ref, sum_ref)
    near = cfg["roomy"] & (stray < REACH)

    @pl.when(near)
    def _():
        near_forces(
            cfg, lambdas, part_ref, off_ref, pool_ref, feat_ref, wide_ref, rhs_ref,
            coef_ref, ins, outs, sub_iota,
        )

    @pl.when(jnp.logical_not(near))
    def _():
        any_forces(cfg, part_ref, pool_ref, col_ref, fcol_ref, ins, outs, sub_iota)

    packed = pack_sums(cfg, sum_ref)
    if last:
        sumo_ref[...] = packed
    else:
        for tile in range(cfg["tiles"]):
            out_ref[tile, 3:4, :] = (
                packed[tile : tile + 1, :] if tile < NSUB else jnp.zeros((1, lanes), jnp.float32)
            )


def part_of(part_ref, cfg, tile, k):
    return part_ref[tile // cfg["rows_y"], tile % cfg["rows_y"], k]


def split3(value):
    high = value.astype(jnp.bfloat16).astype(jnp.float32)
    rest = value - high
    middle = rest.astype(jnp.bfloat16).astype(jnp.float32)
    return high, middle, rest - middle


def by_group(lambdas_of_site, group, sub_iota):
    return [
        jnp.where(group == sub_iota + float(site * NSUB), lambdas_of_site[site], 0.0)
        for site in range(NSITE)
    ]


def near_forces(
    cfg, lambdas, part_ref, off_ref, pool_ref, feat_ref, wide_ref, rhs_ref,
    coef_ref, ins, outs, sub_iota,
):
    lanes = cfg["lanes"]
    depth = cfg["depth"]
    rows = lax.broadcasted_iota(jnp.int32, (8, lanes), 0)
    ones = jnp.ones((NSUB, lanes), jnp.float32)
    nothing = jnp.zeros((8, lanes), jnp.float32)
    pad = [nothing] * ((depth - 6 * 8 - 2 * NSITE * NSUB) // 8)

    pick_rows = lax.broadcasted_iota(jnp.int32, (depth, lanes), 0)
    hit = (pick_rows == 7) | (pick_rows == 16 + 7) | (pick_rows == 40 + 7)
    pick = jnp.where(hit, 1.0, 0.0).astype(jnp.bfloat16)

    def centred(index):
        block = pool_ref[index]
        shift = jnp.where(rows == 0, off_ref[0, index], 0.0)
        shift = jnp.where(rows == 1, off_ref[1, index], shift)
        shift = jnp.where(rows == 2, -MIDDLE_Z, shift)
        moved = block + shift
        square = jnp.where(rows < 3, moved * moved, 0.0)
        return block, moved, jnp.sum(square, axis=0, keepdims=True)

    def table_dot(features, ref):
        table = jnp.concatenate([ref[c] for c in range(ref.shape[0])], axis=1)
        return jnp.dot(features, table, preferred_element_type=jnp.float32)

    def some_pool(k, carry):
        for u in range(cfg["pool_group"]):
            one_pool(k * cfg["pool_group"] + u)
        return carry

    def one_pool(index):
        block, moved, norm = centred(index)
        table = jnp.where(rows == 5, norm, moved)
        table = jnp.where(rows == 6, 1.0, table)
        table = jnp.where(rows == 7, block[STR : STR + 1, :], table)
        high, middle, low = split3(table)
        member = by_group([ones] * NSITE, block[GRP : GRP + 1, :], sub_iota)
        features = jnp.concatenate(
            [high, high, middle, middle, high, low] + member + member + pad, axis=0
        )
        features = features.T.astype(jnp.bfloat16)
        feat_ref[index] = features
        wide_ref[index] = jnp.dot(features, pick, preferred_element_type=jnp.float32)
        coef = jnp.concatenate([high, middle, low, nothing], axis=0).astype(jnp.bfloat16)
        coef_ref[index] = jnp.concatenate([coef, coef], axis=1)

    lax.fori_loop(0, cfg["pool"] // cfg["pool_group"], some_pool, 0)
    none_columns = lax.broadcasted_iota(jnp.int32, (lanes, depth), 1)
    feat_ref[cfg["pool"]] = jnp.where(none_columns == 6, 1.0, 0.0).astype(jnp.bfloat16)
    wide_ref[cfg["pool"]] = jnp.zeros((lanes, lanes), jnp.float32)
    coef_ref[cfg["pool"]] = jnp.zeros((32, 2 * lanes), jnp.bfloat16)

    spread = [lam - lam * lam for lam in lambdas]
    half = [0.5 - lam for lam in lambdas]

    def one_tile(tile, carry):
        own = (tile // cfg["rows_y"] + 1) * (cfg["rows_y"] + 2) + tile % cfg["rows_y"] + 1
        block, moved, norm = centred(own)
        group, site_row = block[GRP : GRP + 1, :], block[SIT : SIT + 1, :]
        lam, charge, strength = (block[r : r + 1, :] for r in (LAM, CHG, STR))
        ratio = charge / strength

        gap = jnp.where(rows < 3, -2.0 * moved, 0.0)
        gap = jnp.where(rows == 3, -0.5 * lam, gap)
        gap = jnp.where(rows == 5, 1.0, gap)
        gap = jnp.where(rows == 6, norm + 1.5, gap)
        pair = by_group(spread, group, sub_iota)
        far = [
            jnp.where(
                (site_row == float(site)) & (group != sub_iota + float(site * NSUB)), FAR, 0.0
            )
            for site in range(NSITE)
        ]
        columns = (
            (gap, [f - 0.5 * p for f, p in zip(far, pair)]),
            (jnp.where(rows == 3, lam, 0.0), pair),
            (jnp.where(rows == 3, 1.0, 0.0), by_group(half, group, sub_iota)),
            (jnp.where(rows == 4, ratio, 0.0), [nothing] * NSITE),
        )
        for column, (table, member) in enumerate(columns):
            high, middle, low = split3(table)
            tops = [m.astype(jnp.bfloat16).astype(jnp.float32) for m in member]
            rests = [m - t for m, t in zip(member, tops)]
            rhs_ref[column] = jnp.concatenate(
                [high, middle, high, middle, low, high] + tops + rests + pad, axis=0
            ).astype(jnp.bfloat16)

        def some_partners(k, sums):
            indices = [part_of(part_ref, cfg, tile, k + u) for u in range(cfg["slots"])]
            indices = [jnp.where(index < 0, cfg["pool"], index) for index in indices]
            outs = [table_dot(feat_ref[index], rhs_ref) for index in indices]
            moments, fd = sums
            for index, out in zip(indices, outs):
                tops, rests = [], []
                for i in range(lanes // ROWS):
                    here = slice(ROWS * i, ROWS * i + ROWS)
                    gap2, s, w, q = (out[here, c * lanes : (c + 1) * lanes] for c in range(4))
                    eb = wide_ref[index, here, :]
                    rs = lax.rsqrt(gap2)
                    t = rs * rs * rs
                    a = eb * t
                    b = (s * t) * (a + 0.25 * q)
                    sens = (rs * (a + q) + b) * w
                    for j in range(ROWS // 8):
                        fd = fd + sens[8 * j : 8 * j + 8, :]
                    top = b.astype(jnp.bfloat16)
                    tops.append(top)
                    rests.append((b - top.astype(jnp.float32)).astype(jnp.bfloat16))
                moments = moments + jnp.dot(
                    coef_ref[index],
                    jnp.concatenate(tops + rests, axis=0),
                    preferred_element_type=jnp.float32,
                )
            return moments, fd

        moments, fd = some_partners(0, (jnp.zeros((32, lanes), jnp.float32), nothing))
        moments = moments[0:8] + moments[8:16] + moments[16:24]
        fd = jnp.sum(fd, axis=0, keepdims=True)
        forces = moved[0:3, :] * moments[6:7, :] - moments[0:3, :]
        rs = lax.rsqrt(1.5 - 0.5 * lam)
        t = rs * rs * rs
        a, q = strength * t, ratio * charge
        itself = rs * (a + q) + lam * t * (a + 0.25 * q)
        drive = strength * (fd - 0.5 * itself)
        finish_tile(cfg, tile, (4.0 * strength) * forces, drive, block, ins, outs, sub_iota)
        return carry

    lax.fori_loop(0, cfg["tiles"], one_tile, 0)


def any_forces(cfg, part_ref, pool_ref, col_ref, fcol_ref, ins, outs, sub_iota):
    tiles, lanes = cfg["tiles"], cfg["lanes"]
    chunk = 32

    def one_tile(tile, carry):
        own = (tile // cfg["rows_y"] + 1) * (cfg["rows_y"] + 2) + tile % cfg["rows_y"] + 1
        block = pool_ref[own]
        col_ref[...] = block.T
        count = jnp.int32(0)
        for k in range(cfg["slots"]):
            count += (part_of(part_ref, cfg, tile, k) >= 0).astype(jnp.int32)

        def one_chunk(c, carry):
            start = pl.multiple_of(c * chunk, chunk)
            cols = col_ref[pl.ds(start, chunk), :]
            lanes_iota = lax.broadcasted_iota(jnp.int32, (chunk, lanes), 1)
            diagonal = lanes_iota == lax.broadcasted_iota(jnp.int32, (chunk, lanes), 0) + start

            def one_partner(k, sums):
                fx, fy, fz, fd = sums
                index = part_of(part_ref, cfg, tile, k)
                other = pool_ref[index]

                def own_col(row):
                    return cols[:, row : row + 1]

                def other_row(row):
                    return other[row : row + 1, :]

                dx = wrap_image(own_col(X) - other_row(X), cfg["box_x"])
                dy = wrap_image(own_col(Y) - other_row(Y), cfg["box_y"])
                dz = own_col(Z) - other_row(Z)
                r2 = dx * dx + dy * dy + dz * dz
                same = (own_col(GRP) == other_row(GRP)) & (own_col(GRP) >= 0.0)
                site = (own_col(SIT) == other_row(SIT)) & (own_col(SIT) >= 0.0)
                drop = (site & jnp.logical_not(same)) | (diagonal & (index == own))
                lam_a, lam_b = own_col(LAM), other_row(LAM)
                s = jnp.where(same, lam_a, lam_a * lam_b)
                w = jnp.where(same, 0.5, lam_b)
                e = own_col(STR) * other_row(STR)
                q = own_col(CHG) * other_row(CHG)
                rs = lax.rsqrt(1.0 + 0.5 * (1.0 - s) + r2)
                t = rs * rs * rs
                a = e * t
                b = s * t * (a + 0.25 * q)
                sens = rs * (a + q) + b
                b = jnp.where(drop, 0.0, b)
                sens = jnp.where(drop, 0.0, sens * w)
                return fx + b * dx, fy + b * dy, fz + b * dz, fd + sens

            zero = jnp.zeros((chunk, lanes), jnp.float32)
            sums = lax.fori_loop(0, count, one_partner, (zero, zero, zero, zero))
            for row, value in enumerate(sums):
                fcol_ref[pl.ds(start, chunk), row : row + 1] = jnp.sum(
                    value, axis=1, keepdims=True
                )
            return carry

        lax.fori_loop(0, lanes // chunk, one_chunk, 0)
        forces = fcol_ref[...].T
        finish_tile(
            cfg, tile, 4.0 * forces[0:3, :], forces[3:4, :], block,
            ins, outs, sub_iota,
        )
        return carry

    lax.fori_loop(0, tiles, one_tile, 0)


def finish_tile(cfg, tile, forces, drive, block, ins, outs, sub_iota):
    vel_ref, noise_ref, inv_ref, start_ref = ins
    out_ref, velo_ref, sum_ref = outs
    i, j = tile // cfg["rows_y"], tile % cfg["rows_y"]
    damping = math.exp(-friction_rate * step_size)
    inverse = inv_ref[i, pl.ds(j, 1), :]
    speeds = (
        damping * vel_ref[tile, 0:3, :]
        + step_size * forces * inverse
        + jnp.sqrt((1.0 - damping**2) * inverse) * noise_ref[0, 0, i, j]
    )
    coords = block[0:3, :] + step_size * speeds
    if start_ref is None:
        velo_ref[tile, 0:3, :] = speeds
        out_ref[tile, 0:3, :] = coords
    else:
        velo_ref[0, i, j] = speeds
        out_ref[0, i, j] = coords - start_ref[tile, 0:3, :]
    group = block[GRP : GRP + 1, :]
    for site in range(NSITE):
        sum_ref[site] += jnp.where(group == sub_iota + float(site * NSUB), drive, 0.0)


def pack_sums(cfg, sum_ref):
    lanes = cfg["lanes"]
    share = lanes // NSITE
    lane_site = lax.broadcasted_iota(jnp.int32, (NSUB, lanes), 1) // share
    packed = jnp.zeros((NSUB, lanes), jnp.float32)
    for site in range(NSITE):
        folded = sum_ref[site]
        width = lanes
        while width > share:
            width //= 2
            folded = folded + pltpu.roll(folded, width, 1)
        packed = packed + jnp.where(lane_site == site, folded, 0.0)
    return packed


def step_call(cfg, moment, parts, at, anoise, blocks, stat, totals, vel, noise, inverse, ang, start):
    tiles, lanes, pool = cfg["tiles"], cfg["lanes"], cfg["pool"]
    rows_x, rows_y = cfg["rows_x"], cfg["rows_y"]
    last = moment == STEPS - 1
    vmem = pl.BlockSpec(memory_space=pltpu.VMEM)
    smem = pl.BlockSpec(memory_space=pltpu.SMEM)
    noise_spec = pl.BlockSpec(
        (1, 1, rows_x, rows_y, 3, lanes), lambda i: (0, moment, 0, 0, 0, 0)
    )
    args = [(parts, smem), (at, smem), (anoise, smem)] + [(block, vmem) for block in blocks]
    if moment > 0:
        args.append((stat, vmem))
    if totals is not None:
        args.append((totals, vmem))
    args += [(vel, vmem), (noise, noise_spec), (inverse, vmem)]
    if moment > 0:
        args.append((ang, vmem))
    if last:
        args.append((start, vmem))
    whole = (1, rows_x, rows_y, 3, lanes)
    shapes = [whole, whole] if last else [(tiles, 4, lanes), (tiles, 4, lanes)]
    shapes.append((2, NSITE, NSUB, lanes))
    if moment == 0:
        shapes.append((pool, 4, lanes))
    if last:
        shapes.append((NSUB, lanes))
    depth = cfg["depth"]
    return pl.pallas_call(
        functools.partial(step_kernel, cfg, moment),
        grid=(1,),
        out_shape=tuple(jax.ShapeDtypeStruct(shape, jnp.float32) for shape in shapes),
        in_specs=[spec for _, spec in args],
        out_specs=(vmem,) * len(shapes),
        scratch_shapes=[
            pltpu.VMEM((pool, 8, lanes), jnp.float32),
            pltpu.VMEM((lanes, 8), jnp.float32),
            pltpu.VMEM((lanes, 8), jnp.float32),
            pltpu.VMEM((NSITE, NSUB, lanes), jnp.float32),
            pltpu.VMEM((pool + 1, lanes, depth), jnp.bfloat16),
            pltpu.VMEM((pool + 1, lanes, lanes), jnp.float32),
            pltpu.VMEM((4, depth, lanes), jnp.bfloat16),
            pltpu.VMEM((pool + 1, 32, 2 * lanes), jnp.bfloat16),
            pltpu.SMEM((2, pool), jnp.float32),
        ],
        name="langevin_step",
    )(*[value for value, _ in args])


def angle_kernel(cfg, *refs):
    anoise_ref, ang_ref = refs[:2]
    tot_refs, (theta_ref, speed_ref) = refs[2:-2], refs[-2:]
    lanes = cfg["lanes"]
    sub_iota = lax.broadcasted_iota(jnp.int32, (NSUB, lanes), 0).astype(jnp.float32)
    packed = packed_totals([ref[...] for ref in tot_refs], sub_iota)
    results = angle_step(
        ang_ref[0], ang_ref[1], packed, noise_table(anoise_ref, STEPS - 1, sub_iota),
        cfg["angle_mass"],
    )
    hit = lax.broadcasted_iota(jnp.int32, (NSUB, lanes), 1) == lax.broadcasted_iota(
        jnp.int32, (NSUB, lanes), 0
    )
    for ref, result in zip((theta_ref, speed_ref), results):
        for site in range(NSITE):
            row = jnp.sum(jnp.where(hit, result[site], 0.0), axis=0, keepdims=True)
            ref[0, site : site + 1, :] = row[:, 0:NSUB]


def angle_call(cfg, anoise, ang, totals):
    vmem = pl.BlockSpec(memory_space=pltpu.VMEM)
    shape = jax.ShapeDtypeStruct((1, NSITE, NSUB), jnp.float32)
    return pl.pallas_call(
        functools.partial(angle_kernel, cfg),
        out_shape=(shape, shape),
        in_specs=[pl.BlockSpec(memory_space=pltpu.SMEM)] + [vmem] * (1 + len(totals)),
        out_specs=(vmem, vmem),
        name="last_angles",
    )(anoise, ang, *totals)


def clone(message, source_slot):
    peers = lax.axis_size("walker")
    me = lax.axis_index("walker")
    width = 2 if peers % 2 == 0 else 1
    sets = peers // width
    mine = message
    if width == 2:
        other = lax.ppermute(message, "walker", [(w, w ^ 1) for w in range(peers)])
        odd = me % 2 == 1
    else:
        other, odd = message, me < 0

    def held(slot):
        return jnp.where((slot % 2 == 1) == odd, mine, other) if width == 2 else mine

    source = source_slot[me]
    result = held(source)
    hop = (me // width - source // width) % sets
    for k in range(1, sets):
        target = (me + k * width) % peers
        sent = held(source_slot[target])
        got = lax.ppermute(
            sent, "walker", [(w, (w + k * width) % peers) for w in range(peers)]
        )
        result = jnp.where(hop == k, got, result)
    return result


def make_cfg(rows_x, rows_y, lanes, count_x, count_y, slots, offsets):
    tiles = rows_x * rows_y
    return dict(
        blocks=1 + len(offsets),
        covered=1 + len(offsets) == count_x * count_y,
        tiles=tiles,
        lanes=lanes,
        rows_x=rows_x,
        rows_y=rows_y,
        count_x=count_x,
        count_y=count_y,
        slots=slots,
        pool=(rows_x + 2) * (rows_y + 2),
        sources=pool_sources(rows_x, rows_y, count_x, count_y, offsets),
        depth=128,
        pool_group=next(g for g in (12, 6, 4, 3, 2, 1) if (rows_x + 2) * (rows_y + 2) % g == 0),
        roomy=min(rows_x * count_x, rows_y * count_y) >= 8,
        box_x=float(rows_x * count_x),
        box_y=float(rows_y * count_y),
        angle_mass=rows_x * count_x * rows_y * count_y * lanes * theta_share,
    )


def per_device(
    positions,
    velocities,
    lambda_theta,
    theta_velocity,
    source_slot,
    atom_noise,
    theta_noise,
    charges,
    strengths,
    inverse_mass,
    atom_site,
    atom_sub,
    partners,
):
    count_x, count_y = lax.axis_size("gx"), lax.axis_size("gy")
    rows_x, rows_y, lanes = charges.shape
    tiles = rows_x * rows_y
    offsets = neighbour_offsets(count_x, count_y)
    cfg = make_cfg(rows_x, rows_y, lanes, count_x, count_y, partners.shape[-1], offsets)

    def gather_blocks(value):
        return [value] + [shifted(value, offset, count_x, count_y) for offset in offsets]

    is_group = atom_site < NSITE
    groups = jnp.where(is_group, atom_site * NSUB + atom_sub, -1)
    sites = jnp.where(is_group, atom_site, -1)
    stat = jnp.stack(
        [charges, strengths, groups.astype(jnp.float32), sites.astype(jnp.float32)], axis=2
    ).reshape(tiles, 4, lanes)

    angles = jnp.stack([lambda_theta[0], theta_velocity[0]]).reshape(1, 2 * NSITE * NSUB)
    angles = jnp.pad(angles, ((0, 0), (0, lanes - 2 * NSITE * NSUB)))
    extra = jnp.broadcast_to(angles[:, None, :], (tiles, 1, lanes))
    message = jnp.concatenate(
        [
            positions.reshape(tiles, 3, lanes),
            extra,
            velocities.reshape(tiles, 3, lanes),
            jnp.zeros((tiles, 1, lanes), jnp.float32),
        ],
        axis=1,
    )
    start = clone(message, source_slot)
    vel = start[:, 4:8, :]
    at = jnp.stack([lax.axis_index("gx"), lax.axis_index("gy")])
    pay = jnp.concatenate([start[:, 0:4, :], stat], axis=1)
    first = pay
    ang = pool_stat = None
    for moment in range(STEPS):
        totals = None
        if moment > 0 and not cfg["covered"]:
            totals = lax.psum(pay[:NSUB, 3, :], ("gx", "gy"))
        outs = step_call(
            cfg, moment, partners, at, theta_noise, gather_blocks(pay), pool_stat, totals, vel,
            atom_noise, inverse_mass, ang, first,
        )
        pay, vel, ang = outs[:3]
        if moment == 0:
            pool_stat = outs[3]
    packed = outs[3]
    if cfg["covered"]:
        totals = gather_blocks(packed)
    else:
        totals = [lax.psum(packed, ("gx", "gy"))]
    theta, theta_speed = angle_call(cfg, theta_noise, ang, totals)
    return pay, vel, theta, theta_speed


def solution(mesh):
    in_specs = (
        P("walker", "gx", "gy", None, None),
        P("walker", "gx", "gy", None, None),
        P("walker", None, None),
        P("walker", None, None),
        P(),
        P("walker", None, "gx", "gy", None, None),
        P("walker", None, None, None),
        P("gx", "gy", None),
        P("gx", "gy", None),
        P("gx", "gy", None),
        P("gx", "gy", None),
        P("gx", "gy", None),
        P("gx", "gy", None),
    )
    out_specs = (
        P("walker", "gx", "gy", None, None),
        P("walker", "gx", "gy", None, None),
        P("walker", None, None),
        P("walker", None, None),
    )
    return jax.shard_map(
        per_device, mesh=mesh, in_specs=in_specs, out_specs=out_specs, check_vma=False
    )
```

```python
import functools
import math

import jax
import jax.numpy as jnp
from jax import lax
from jax.experimental import pallas as pl
from jax.experimental.pallas import tpu as pltpu
from jax.sharding import PartitionSpec as P

NSITE = 4
NSUB = 8
STEPS = 4

step_size = 0.02
friction_rate = 1.0
theta_friction = 20.0
soft_alpha = 0.5
soft_beta = 0.5
theta_share = 1.0 / 1024.0

MIDDLE_Z = 1.0
REACH = 1.49
FAR = 2.0**126
SMALL = 4 * 2**20
ROWS = 16

X, Y, Z, LAM, CHG, STR, GRP, SIT = range(8)


def wrap_image(offset, length):
    shift = jnp.where(offset > 0.5 * length, length, 0.0)
    shift = jnp.where(offset < -0.5 * length, -length, shift)
    return offset - shift


def neighbour_offsets(count_x, count_y):
    found = []
    for di in (-1, 0, 1):
        for dj in (-1, 0, 1):
            key = (di % count_x, dj % count_y)
            if key != (0, 0) and key not in found:
                found.append(key)
    return found


def shifted(value, offset, count_x, count_y):
    pairs = []
    for i in range(count_x):
        for j in range(count_y):
            source = ((i + offset[0]) % count_x) * count_y + (j + offset[1]) % count_y
            pairs.append((source, i * count_y + j))
    return lax.ppermute(value, ("gx", "gy"), pairs)


def pool_sources(rows_x, rows_y, count_x, count_y, offsets):
    sources = []
    for pi in range(rows_x + 2):
        for pj in range(rows_y + 2):
            di = -1 if pi == 0 else (1 if pi == rows_x + 1 else 0)
            dj = -1 if pj == 0 else (1 if pj == rows_y + 1 else 0)
            key = (di % count_x, dj % count_y)
            block = 0 if key == (0, 0) else 1 + offsets.index(key)
            tile = ((pi - 1) % rows_x) * rows_y + (pj - 1) % rows_y
            sources.append((block, tile))
    return sources


def softmax_angles(angles):
    weights = jnp.exp(angles)
    return weights / jnp.sum(weights, axis=1, keepdims=True)


def angle_step(angles, speeds, packed, noise, angle_mass):
    lanes = packed.shape[1]
    share = lanes // NSITE
    lane_site = lax.broadcasted_iota(jnp.int32, packed.shape, 1) // share
    lambdas = softmax_angles(angles)
    totals = jnp.stack(
        [
            jnp.broadcast_to(
                jnp.sum(jnp.where(lane_site == site, packed, 0.0), axis=1, keepdims=True),
                packed.shape,
            )
            for site in range(NSITE)
        ]
    )
    angle_damping = math.exp(-theta_friction * step_size)
    force = -lambdas * (totals - jnp.sum(lambdas * totals, axis=1, keepdims=True))
    speeds = (
        angle_damping * speeds
        + step_size * force / angle_mass
        + math.sqrt((1.0 - angle_damping**2) / angle_mass) * noise
    )
    return angles + step_size * speeds, speeds


def extra_row(cfg, number):
    return number // cfg["rows_y"], number % cfg["rows_y"]


def angle_row(ref, cfg, kind, site):
    i, j = extra_row(cfg, kind * NSITE + site)
    return ref[i, 3, j : j + 1, :]


def lane_column(row, sub_iota):
    lane = lax.broadcasted_iota(jnp.int32, sub_iota.shape, 1)
    hit = lane == lax.broadcasted_iota(jnp.int32, sub_iota.shape, 0)
    return jnp.broadcast_to(
        jnp.sum(jnp.where(hit, row, 0.0), axis=1, keepdims=True), sub_iota.shape
    )


def block_rows(ref, cfg, tile, first, last):
    i, j = tile // cfg["rows_y"], tile % cfg["rows_y"]
    return jnp.concatenate([ref[i, row, j : j + 1, :] for row in range(first, last)], axis=0)


def noise_table(anoise_ref, moment, sub_iota):
    tables = []
    for site in range(NSITE):
        table = jnp.zeros_like(sub_iota)
        for sub in range(NSUB):
            table = jnp.where(sub_iota == float(sub), anoise_ref[0, moment, site, sub], table)
        tables.append(table)
    return jnp.stack(tables)


def packed_rows(ref, cfg):
    rows_y = cfg["rows_y"]
    return jnp.concatenate([ref[i, 3] for i in range(-(-NSUB // rows_y))], axis=0)[0:NSUB]


def packed_totals(blocks):
    packed = blocks[0]
    for block in blocks[1:]:
        packed = packed + block
    return packed


def step_kernel(cfg, moment, *refs):
    nb = cfg["blocks"]
    lanes = cfg["lanes"]
    refs = list(refs)

    def take(n):
        taken, refs[:n] = refs[:n], []
        return taken

    part_ref, anoise_ref = take(2)
    coord_refs = take(nb)
    (stat_ref,) = take(1) if moment > 0 else (None,)
    (tot_ref,) = take(1) if moment > 0 and not cfg["covered"] else (None,)
    vel_ref, noise_ref, inv_ref = take(3)
    (ang_ref,) = take(1) if moment > 0 else (None,)
    last = moment == STEPS - 1
    (start_ref,) = take(1) if last else (None,)
    (out_ref,) = take(1)
    velo_ref, ango_ref = take(2)
    (stato_ref,) = take(1) if moment == 0 else (None,)
    (sumo_ref,) = take(1) if last else (None,)
    pool_ref, col_ref, fcol_ref, sum_ref, feat_ref, wide_ref, rhs_ref, coef_ref, off_ref, io_ref = take(10)

    sub_iota = lax.broadcasted_iota(jnp.int32, (NSUB, lanes), 0).astype(jnp.float32)
    if moment == 0:
        angles, aspeeds = (
            jnp.stack(
                [lane_column(angle_row(coord_refs[0], cfg, kind, site), sub_iota) for site in range(NSITE)]
            )
            for kind in range(2)
        )
    else:
        angles, aspeeds = ang_ref[0], ang_ref[1]
        if cfg["covered"]:
            packed = packed_totals([packed_rows(ref, cfg) for ref in coord_refs])
        else:
            packed = tot_ref[...]
        angles, aspeeds = angle_step(
            angles, aspeeds, packed, noise_table(anoise_ref, moment - 1, sub_iota),
            cfg["angle_mass"],
        )
    ango_ref[0] = angles
    ango_ref[1] = aspeeds
    lambdas = softmax_angles(angles)

    def line(axis, rows, count):
        at = lax.axis_index(axis)
        middle = at.astype(jnp.float32) * rows + 0.5 * rows
        shifts, cells = [], []
        for ring in range(rows + 2):
            turn = 0.0
            if ring == 0:
                turn = jnp.where(at == 0, -float(rows * count), 0.0)
            if ring == rows + 1:
                turn = jnp.where(at == count - 1, float(rows * count), 0.0)
            shifts.append(turn - middle)
            cells.append(turn - middle - (ring - 0.5 - 0.5 * rows))
        return shifts, cells

    shift_x, cell_x = line("gx", cfg["rows_x"], cfg["count_x"])
    shift_y, cell_y = line("gy", cfg["rows_y"], cfg["count_y"])
    worst = jnp.zeros((3, lanes), jnp.float32)
    row3 = lax.broadcasted_iota(jnp.int32, (3, lanes), 0)
    for index, (block, tile) in enumerate(cfg["sources"]):
        pi, pj = index // (cfg["rows_y"] + 2), index % (cfg["rows_y"] + 2)
        off_ref[0, index] = shift_x[pi]
        off_ref[1, index] = shift_y[pj]
        if moment == 0:
            stat = block_rows(coord_refs[block], cfg, tile, 4, 8)
            stato_ref[index] = stat
        else:
            stat = stat_ref[index]
        cell = jnp.where(row3 == 0, cell_x[pi], cell_y[pj])
        cell = jnp.where(row3 == 2, -MIDDLE_Z, cell)
        coords = block_rows(coord_refs[block], cfg, tile, 0, 3)
        worst = jnp.maximum(worst, jnp.abs(coords + cell))
        pool_ref[index, 0:3, :] = coords
        pool_ref[index, 4:8, :] = stat
        group = stat[2:3, :]
        lam = jnp.zeros((NSUB, lanes), jnp.float32)
        for site in range(NSITE):
            lam = lam + jnp.where(group == sub_iota + float(site * NSUB), lambdas[site], 0.0)
        lam = jnp.sum(lam, axis=0, keepdims=True)
        pool_ref[index, 3:4, :] = jnp.where(group >= 0.0, lam, 1.0)

    stray = jnp.max(worst * jnp.where(row3 == 2, 0.5, 1.0))
    for tile in range(cfg["tiles"]):
        i, j = tile // cfg["rows_y"], tile % cfg["rows_y"]
        for row in range(3):
            io_ref[tile, row : row + 1, :] = vel_ref[i, row, j : j + 1, :]
            io_ref[tile, 4 + row : 5 + row, :] = noise_ref[0, 0, i, row, j : j + 1, :]
        io_ref[tile, 3:4, :] = inv_ref[i, j : j + 1, :]

    sum_ref[...] = jnp.zeros_like(sum_ref)
    fcol_ref[...] = jnp.zeros_like(fcol_ref)
    ins = io_ref
    outs = (io_ref, sum_ref)
    near = cfg["roomy"] & (stray < REACH)

    @pl.when(near)
    def _():
        near_forces(
            cfg, lambdas, part_ref, off_ref, pool_ref, feat_ref, wide_ref, rhs_ref,
            coef_ref, ins, outs, sub_iota,
        )

    @pl.when(jnp.logical_not(near))
    def _():
        any_forces(cfg, part_ref, pool_ref, col_ref, fcol_ref, ins, outs, sub_iota)

    packed = pack_sums(cfg, sum_ref)
    for tile in range(cfg["tiles"]):
        i, j = tile // cfg["rows_y"], tile % cfg["rows_y"]
        here = slice(j, j + 1)
        for row in range(3):
            coord = io_ref[tile, row : row + 1, :]
            if last:
                coord = coord - start_ref[i, row, here, :]
            out_ref[i, row, here, :] = coord
            velo_ref[i, row, here, :] = io_ref[tile, 4 + row : 5 + row, :]
        if not last:
            out_ref[i, 3, here, :] = (
                packed[tile : tile + 1, :] if tile < NSUB else jnp.zeros((1, lanes), jnp.float32)
            )
    if last:
        sumo_ref[...] = packed


def part_of(part_ref, cfg, tile, k):
    return part_ref[tile // cfg["rows_y"], tile % cfg["rows_y"], k]


def split3(value):
    high = value.astype(jnp.bfloat16).astype(jnp.float32)
    rest = value - high
    middle = rest.astype(jnp.bfloat16).astype(jnp.float32)
    return high, middle, rest - middle


def by_group(lambdas_of_site, group, sub_iota):
    return [
        jnp.where(group == sub_iota + float(site * NSUB), lambdas_of_site[site], 0.0)
        for site in range(NSITE)
    ]


def near_forces(
    cfg, lambdas, part_ref, off_ref, pool_ref, feat_ref, wide_ref, rhs_ref,
    coef_ref, ins, outs, sub_iota,
):
    lanes = cfg["lanes"]
    depth = cfg["depth"]
    rows = lax.broadcasted_iota(jnp.int32, (8, lanes), 0)
    ones = jnp.ones((NSUB, lanes), jnp.float32)
    nothing = jnp.zeros((8, lanes), jnp.float32)
    pad = [nothing] * ((depth - 6 * 8 - 2 * NSITE * NSUB) // 8)

    pick_rows = lax.broadcasted_iota(jnp.int32, (depth, lanes), 0)
    hit = (pick_rows == 7) | (pick_rows == 16 + 7) | (pick_rows == 40 + 7)
    pick = jnp.where(hit, 1.0, 0.0).astype(jnp.bfloat16)

    def centred(index):
        block = pool_ref[index]
        shift = jnp.where(rows == 0, off_ref[0, index], 0.0)
        shift = jnp.where(rows == 1, off_ref[1, index], shift)
        shift = jnp.where(rows == 2, -MIDDLE_Z, shift)
        moved = block + shift
        square = jnp.where(rows < 3, moved * moved, 0.0)
        return block, moved, jnp.sum(square, axis=0, keepdims=True)

    def table_dot(features, ref):
        table = jnp.concatenate([ref[c] for c in range(ref.shape[0])], axis=1)
        return jnp.dot(features, table, preferred_element_type=jnp.float32)

    def some_pool(k, carry):
        for u in range(cfg["pool_group"]):
            one_pool(k * cfg["pool_group"] + u)
        return carry

    def one_pool(index):
        block, moved, norm = centred(index)
        table = jnp.where(rows == 5, norm, moved)
        table = jnp.where(rows == 6, 1.0, table)
        table = jnp.where(rows == 7, block[STR : STR + 1, :], table)
        high, middle, low = split3(table)
        member = by_group([ones] * NSITE, block[GRP : GRP + 1, :], sub_iota)
        features = jnp.concatenate(
            [high, high, middle, middle, high, low] + member + member + pad, axis=0
        )
        features = features.T.astype(jnp.bfloat16)
        feat_ref[index] = features
        wide_ref[index] = jnp.dot(features, pick, preferred_element_type=jnp.float32)
        coef = jnp.concatenate([high, middle, low, nothing], axis=0).astype(jnp.bfloat16)
        coef_ref[index] = jnp.concatenate([coef, coef], axis=1)

    lax.fori_loop(0, cfg["pool"] // cfg["pool_group"], some_pool, 0)
    none_columns = lax.broadcasted_iota(jnp.int32, (lanes, depth), 1)
    feat_ref[cfg["pool"]] = jnp.where(none_columns == 6, 1.0, 0.0).astype(jnp.bfloat16)
    wide_ref[cfg["pool"]] = jnp.zeros((lanes, lanes), jnp.float32)
    coef_ref[cfg["pool"]] = jnp.zeros((32, 2 * lanes), jnp.bfloat16)

    spread = [lam - lam * lam for lam in lambdas]
    half = [0.5 - lam for lam in lambdas]

    def one_tile(tile, carry):
        own = (tile // cfg["rows_y"] + 1) * (cfg["rows_y"] + 2) + tile % cfg["rows_y"] + 1
        block, moved, norm = centred(own)
        group, site_row = block[GRP : GRP + 1, :], block[SIT : SIT + 1, :]
        lam, charge, strength = (block[r : r + 1, :] for r in (LAM, CHG, STR))
        ratio = charge / strength

        gap = jnp.where(rows < 3, -2.0 * moved, 0.0)
        gap = jnp.where(rows == 3, -0.5 * lam, gap)
        gap = jnp.where(rows == 5, 1.0, gap)
        gap = jnp.where(rows == 6, norm + 1.5, gap)
        pair = by_group(spread, group, sub_iota)
        far = [
            jnp.where(
                (site_row == float(site)) & (group != sub_iota + float(site * NSUB)), FAR, 0.0
            )
            for site in range(NSITE)
        ]
        columns = (
            (gap, [f - 0.5 * p for f, p in zip(far, pair)]),
            (jnp.where(rows == 3, lam, 0.0), pair),
            (jnp.where(rows == 3, 1.0, 0.0), by_group(half, group, sub_iota)),
            (jnp.where(rows == 4, ratio, 0.0), [nothing] * NSITE),
        )
        for column, (table, member) in enumerate(columns):
            high, middle, low = split3(table)
            tops = [m.astype(jnp.bfloat16).astype(jnp.float32) for m in member]
            rests = [m - t for m, t in zip(member, tops)]
            rhs_ref[column] = jnp.concatenate(
                [high, middle, high, middle, low, high] + tops + rests + pad, axis=0
            ).astype(jnp.bfloat16)

        def some_partners(k, sums):
            indices = [part_of(part_ref, cfg, tile, k + u) for u in range(cfg["slots"])]
            indices = [jnp.where(index < 0, cfg["pool"], index) for index in indices]
            outs = [table_dot(feat_ref[index], rhs_ref) for index in indices]
            moments, fd = sums
            for index, out in zip(indices, outs):
                tops, rests = [], []
                for i in range(lanes // ROWS):
                    here = slice(ROWS * i, ROWS * i + ROWS)
                    gap2, s, w, q = (out[here, c * lanes : (c + 1) * lanes] for c in range(4))
                    eb = wide_ref[index, here, :]
                    rs = lax.rsqrt(gap2)
                    t = rs * rs * rs
                    a = eb * t
                    b = (s * t) * (a + 0.25 * q)
                    sens = (rs * (a + q) + b) * w
                    for j in range(ROWS // 8):
                        fd = fd + sens[8 * j : 8 * j + 8, :]
                    top = b.astype(jnp.bfloat16)
                    tops.append(top)
                    rests.append((b - top.astype(jnp.float32)).astype(jnp.bfloat16))
                moments = moments + jnp.dot(
                    coef_ref[index],
                    jnp.concatenate(tops + rests, axis=0),
                    preferred_element_type=jnp.float32,
                )
            return moments, fd

        moments, fd = some_partners(0, (jnp.zeros((32, lanes), jnp.float32), nothing))
        moments = moments[0:8] + moments[8:16] + moments[16:24]
        fd = jnp.sum(fd, axis=0, keepdims=True)
        forces = moved[0:3, :] * moments[6:7, :] - moments[0:3, :]
        rs = lax.rsqrt(1.5 - 0.5 * lam)
        t = rs * rs * rs
        a, q = strength * t, ratio * charge
        itself = rs * (a + q) + lam * t * (a + 0.25 * q)
        drive = strength * (fd - 0.5 * itself)
        finish_tile(cfg, tile, (4.0 * strength) * forces, drive, block, ins, outs, sub_iota)
        return carry

    lax.fori_loop(0, cfg["tiles"], one_tile, 0)


def any_forces(cfg, part_ref, pool_ref, col_ref, fcol_ref, ins, outs, sub_iota):
    tiles, lanes = cfg["tiles"], cfg["lanes"]
    chunk = 32

    def one_tile(tile, carry):
        own = (tile // cfg["rows_y"] + 1) * (cfg["rows_y"] + 2) + tile % cfg["rows_y"] + 1
        block = pool_ref[own]
        col_ref[...] = block.T
        count = jnp.int32(0)
        for k in range(cfg["slots"]):
            count += (part_of(part_ref, cfg, tile, k) >= 0).astype(jnp.int32)

        def one_chunk(c, carry):
            start = pl.multiple_of(c * chunk, chunk)
            cols = col_ref[pl.ds(start, chunk), :]
            lanes_iota = lax.broadcasted_iota(jnp.int32, (chunk, lanes), 1)
            diagonal = lanes_iota == lax.broadcasted_iota(jnp.int32, (chunk, lanes), 0) + start

            def one_partner(k, sums):
                fx, fy, fz, fd = sums
                index = part_of(part_ref, cfg, tile, k)
                other = pool_ref[index]

                def own_col(row):
                    return cols[:, row : row + 1]

                def other_row(row):
                    return other[row : row + 1, :]

                dx = wrap_image(own_col(X) - other_row(X), cfg["box_x"])
                dy = wrap_image(own_col(Y) - other_row(Y), cfg["box_y"])
                dz = own_col(Z) - other_row(Z)
                r2 = dx * dx + dy * dy + dz * dz
                same = (own_col(GRP) == other_row(GRP)) & (own_col(GRP) >= 0.0)
                site = (own_col(SIT) == other_row(SIT)) & (own_col(SIT) >= 0.0)
                drop = (site & jnp.logical_not(same)) | (diagonal & (index == own))
                lam_a, lam_b = own_col(LAM), other_row(LAM)
                s = jnp.where(same, lam_a, lam_a * lam_b)
                w = jnp.where(same, 0.5, lam_b)
                e = own_col(STR) * other_row(STR)
                q = own_col(CHG) * other_row(CHG)
                rs = lax.rsqrt(1.0 + 0.5 * (1.0 - s) + r2)
                t = rs * rs * rs
                a = e * t
                b = s * t * (a + 0.25 * q)
                sens = rs * (a + q) + b
                b = jnp.where(drop, 0.0, b)
                sens = jnp.where(drop, 0.0, sens * w)
                return fx + b * dx, fy + b * dy, fz + b * dz, fd + sens

            zero = jnp.zeros((chunk, lanes), jnp.float32)
            sums = lax.fori_loop(0, count, one_partner, (zero, zero, zero, zero))
            for row, value in enumerate(sums):
                fcol_ref[pl.ds(start, chunk), row : row + 1] = jnp.sum(
                    value, axis=1, keepdims=True
                )
            return carry

        lax.fori_loop(0, lanes // chunk, one_chunk, 0)
        forces = fcol_ref[...].T
        finish_tile(
            cfg, tile, 4.0 * forces[0:3, :], forces[3:4, :], block,
            ins, outs, sub_iota,
        )
        return carry

    lax.fori_loop(0, tiles, one_tile, 0)


def finish_tile(cfg, tile, forces, drive, block, ins, outs, sub_iota):
    _, sum_ref = outs
    damping = math.exp(-friction_rate * step_size)
    rows = ins[tile]
    inverse = rows[3:4, :]
    speeds = (
        damping * rows[0:3, :]
        + step_size * forces * inverse
        + jnp.sqrt((1.0 - damping**2) * inverse) * rows[4:7, :]
    )
    ins[tile, 0:3, :] = block[0:3, :] + step_size * speeds
    ins[tile, 4:7, :] = speeds
    group = block[GRP : GRP + 1, :]
    for site in range(NSITE):
        sum_ref[site] += jnp.where(group == sub_iota + float(site * NSUB), drive, 0.0)


def pack_sums(cfg, sum_ref):
    lanes = cfg["lanes"]
    share = lanes // NSITE
    lane_site = lax.broadcasted_iota(jnp.int32, (NSUB, lanes), 1) // share
    packed = jnp.zeros((NSUB, lanes), jnp.float32)
    for site in range(NSITE):
        folded = sum_ref[site]
        width = lanes
        while width > share:
            width //= 2
            folded = folded + pltpu.roll(folded, width, 1)
        packed = packed + jnp.where(lane_site == site, folded, 0.0)
    return packed


def step_call(cfg, moment, parts, anoise, blocks, stat, totals, vel, noise, inverse, ang, start):
    tiles, lanes, pool = cfg["tiles"], cfg["lanes"], cfg["pool"]
    rows_x, rows_y = cfg["rows_x"], cfg["rows_y"]
    last = moment == STEPS - 1
    vmem = pl.BlockSpec(memory_space=pltpu.VMEM)
    smem = pl.BlockSpec(memory_space=pltpu.SMEM)
    noise_spec = pl.BlockSpec(
        (1, 1, rows_x, 3, rows_y, lanes), lambda i: (0, moment, 0, 0, 0, 0)
    )
    args = [(parts, smem), (anoise, smem)] + [(block, vmem) for block in blocks]
    if moment > 0:
        args.append((stat, vmem))
    if totals is not None:
        args.append((totals, vmem))
    args += [(vel, vmem), (noise, noise_spec), (inverse, vmem)]
    if moment > 0:
        args.append((ang, vmem))
    if last:
        args.append((start, vmem))
    vectors = (rows_x, 3, rows_y, lanes)
    shapes = [vectors if last else (rows_x, 4, rows_y, lanes), vectors]
    shapes.append((2, NSITE, NSUB, lanes))
    if moment == 0:
        shapes.append((pool, 4, lanes))
    if last:
        shapes.append((NSUB, lanes))
    depth = cfg["depth"]
    return pl.pallas_call(
        functools.partial(step_kernel, cfg, moment),
        grid=(1,),
        out_shape=tuple(jax.ShapeDtypeStruct(shape, jnp.float32) for shape in shapes),
        in_specs=[spec for _, spec in args],
        out_specs=(vmem,) * len(shapes),
        scratch_shapes=[
            pltpu.VMEM((pool, 8, lanes), jnp.float32),
            pltpu.VMEM((lanes, 8), jnp.float32),
            pltpu.VMEM((lanes, 8), jnp.float32),
            pltpu.VMEM((NSITE, NSUB, lanes), jnp.float32),
            pltpu.VMEM((pool + 1, lanes, depth), jnp.bfloat16),
            pltpu.VMEM((pool + 1, lanes, lanes), jnp.float32),
            pltpu.VMEM((4, depth, lanes), jnp.bfloat16),
            pltpu.VMEM((pool + 1, 32, 2 * lanes), jnp.bfloat16),
            pltpu.SMEM((2, pool), jnp.float32),
            pltpu.VMEM((tiles, 8, lanes), jnp.float32),
        ],
        compiler_params=pltpu.CompilerParams(vmem_limit_bytes=4 * SMALL),
        name="langevin_step",
    )(*[value for value, _ in args])


def angle_kernel(cfg, *refs):
    anoise_ref, ang_ref = refs[:2]
    tot_refs, (theta_ref, speed_ref) = refs[2:-2], refs[-2:]
    lanes = cfg["lanes"]
    sub_iota = lax.broadcasted_iota(jnp.int32, (NSUB, lanes), 0).astype(jnp.float32)
    packed = packed_totals([ref[...] for ref in tot_refs])
    results = angle_step(
        ang_ref[0], ang_ref[1], packed, noise_table(anoise_ref, STEPS - 1, sub_iota),
        cfg["angle_mass"],
    )
    hit = lax.broadcasted_iota(jnp.int32, (NSUB, lanes), 1) == lax.broadcasted_iota(
        jnp.int32, (NSUB, lanes), 0
    )
    for ref, result in zip((theta_ref, speed_ref), results):
        for site in range(NSITE):
            row = jnp.sum(jnp.where(hit, result[site], 0.0), axis=0, keepdims=True)
            ref[0, site : site + 1, :] = row[:, 0:NSUB]


def angle_call(cfg, anoise, ang, totals):
    vmem = pl.BlockSpec(memory_space=pltpu.VMEM)
    shape = jax.ShapeDtypeStruct((1, NSITE, NSUB), jnp.float32)
    return pl.pallas_call(
        functools.partial(angle_kernel, cfg),
        out_shape=(shape, shape),
        in_specs=[pl.BlockSpec(memory_space=pltpu.SMEM)] + [vmem] * (1 + len(totals)),
        out_specs=(vmem, vmem),
        name="last_angles",
        compiler_params=pltpu.CompilerParams(vmem_limit_bytes=SMALL),
    )(anoise, ang, *totals)


def send_kernel(width, sets, slot_ref, mine_ref, other_ref, *out_refs):
    me = lax.axis_index("walker")
    for k, ref in enumerate(out_refs, 1):
        wanted = slot_ref[lax.rem(me + k * width, width * sets)]
        own = lax.rem(wanted, width) == lax.rem(me, width)

        @pl.when(own)
        def _():
            ref[...] = mine_ref[...]

        @pl.when(jnp.logical_not(own))
        def _():
            ref[...] = other_ref[...]


def pick_kernel(width, sets, slot_ref, *refs):
    block_refs = refs[: sets + 1]
    charge_ref, strength_ref, site_ref, sub_ref, pay_ref, vel_ref = refs[sets + 1 :]
    me = lax.axis_index("walker")
    source = slot_ref[me]
    hop = lax.rem(me // width - source // width + sets, sets)
    choice = jnp.where(hop > 0, hop + 1, (lax.rem(source, width) != lax.rem(me, width)).astype(jnp.int32))
    for k, ref in enumerate(block_refs):

        @pl.when(choice == k)
        def _():
            pay_ref[:, 0:4] = ref[:, 0:4]
            vel_ref[...] = ref[:, 4:7]

    site, sub = site_ref[...], sub_ref[...]
    grouped = site < NSITE
    pay_ref[:, 4] = charge_ref[...]
    pay_ref[:, 5] = strength_ref[...]
    pay_ref[:, 6] = jnp.where(grouped, site * NSUB + sub, -1).astype(jnp.float32)
    pay_ref[:, 7] = jnp.where(grouped, site, -1).astype(jnp.float32)


def clone(cfg, message, source_slot, charges, strengths, atom_site, atom_sub):
    peers = lax.axis_size("walker")
    width = 2 if peers % 2 == 0 else 1
    sets = peers // width
    rows_x, rows_y, lanes = charges.shape
    vmem = pl.BlockSpec(memory_space=pltpu.VMEM)
    smem = pl.BlockSpec(memory_space=pltpu.SMEM)
    other = message
    if width == 2:
        other = lax.ppermute(message, "walker", [(w, w ^ 1) for w in range(peers)])
    blocks = [message, other]
    if sets > 1:
        shape = jax.ShapeDtypeStruct(message.shape, jnp.float32)
        sent = pl.pallas_call(
            functools.partial(send_kernel, width, sets),
            out_shape=(shape,) * (sets - 1),
            in_specs=[smem, vmem, vmem],
            out_specs=(vmem,) * (sets - 1),
            name="choose_sent",
        compiler_params=pltpu.CompilerParams(vmem_limit_bytes=SMALL),
        )(source_slot, message, other)
        for k, value in enumerate(sent, 1):
            blocks.append(
                lax.ppermute(
                    value, "walker", [(w, (w + k * width) % peers) for w in range(peers)]
                )
            )
    return pl.pallas_call(
        functools.partial(pick_kernel, width, sets),
        out_shape=(
            jax.ShapeDtypeStruct((rows_x, 8, rows_y, lanes), jnp.float32),
            jax.ShapeDtypeStruct((rows_x, 3, rows_y, lanes), jnp.float32),
        ),
        in_specs=[smem] + [vmem] * (len(blocks) + 4),
        out_specs=(vmem, vmem),
        name="choose_received",
        compiler_params=pltpu.CompilerParams(vmem_limit_bytes=SMALL),
    )(source_slot, *blocks, charges, strengths, atom_site, atom_sub)


def make_cfg(rows_x, rows_y, lanes, count_x, count_y, slots, offsets):
    tiles = rows_x * rows_y
    return dict(
        blocks=1 + len(offsets),
        covered=1 + len(offsets) == count_x * count_y,
        tiles=tiles,
        lanes=lanes,
        rows_x=rows_x,
        rows_y=rows_y,
        count_x=count_x,
        count_y=count_y,
        slots=slots,
        pool=(rows_x + 2) * (rows_y + 2),
        sources=pool_sources(rows_x, rows_y, count_x, count_y, offsets),
        depth=128,
        pool_group=next(g for g in (12, 6, 4, 3, 2, 1) if (rows_x + 2) * (rows_y + 2) % g == 0),
        roomy=min(rows_x * count_x, rows_y * count_y) >= 8,
        box_x=float(rows_x * count_x),
        box_y=float(rows_y * count_y),
        angle_mass=rows_x * count_x * rows_y * count_y * lanes * theta_share,
    )


def per_device(
    positions,
    velocities,
    lambda_theta,
    theta_velocity,
    source_slot,
    atom_noise,
    theta_noise,
    charges,
    strengths,
    inverse_mass,
    atom_site,
    atom_sub,
    partners,
):
    count_x, count_y = lax.axis_size("gx"), lax.axis_size("gy")
    rows_x, rows_y, lanes = charges.shape
    tiles = rows_x * rows_y
    offsets = neighbour_offsets(count_x, count_y)
    cfg = make_cfg(rows_x, rows_y, lanes, count_x, count_y, partners.shape[-1], offsets)

    def gather_blocks(value):
        return [value] + [shifted(value, offset, count_x, count_y) for offset in offsets]

    angles = jnp.concatenate([lambda_theta[0], theta_velocity[0]], axis=0)
    angles = jnp.pad(angles, ((0, tiles - angles.shape[0]), (0, lanes - NSUB)))
    message = jnp.concatenate(
        [
            positions[0].transpose(0, 2, 1, 3),
            angles.reshape(rows_x, 1, rows_y, lanes),
            velocities[0].transpose(0, 2, 1, 3),
        ],
        axis=1,
    )
    pay, vel = clone(cfg, message, source_slot, charges, strengths, atom_site, atom_sub)
    noise = atom_noise.transpose(0, 1, 2, 4, 3, 5)
    first = pay
    ang = pool_stat = None
    for moment in range(STEPS):
        totals = None
        if moment > 0 and not cfg["covered"]:
            totals = lax.psum(pay[:, 3].reshape(tiles, lanes)[:NSUB], ("gx", "gy"))
        outs = step_call(
            cfg, moment, partners, theta_noise, gather_blocks(pay), pool_stat, totals, vel,
            noise, inverse_mass, ang, first,
        )
        pay, vel, ang = outs[:3]
        if moment == 0:
            pool_stat = outs[3]
    packed = outs[3]
    if cfg["covered"]:
        totals = gather_blocks(packed)
    else:
        totals = [lax.psum(packed, ("gx", "gy"))]
    theta, theta_speed = angle_call(cfg, theta_noise, ang, totals)
    back = lambda value: value.transpose(0, 2, 1, 3)[None]
    return back(pay), back(vel), theta, theta_speed


def solution(mesh):
    in_specs = (
        P("walker", "gx", "gy", None, None),
        P("walker", "gx", "gy", None, None),
        P("walker", None, None),
        P("walker", None, None),
        P(),
        P("walker", None, "gx", "gy", None, None),
        P("walker", None, None, None),
        P("gx", "gy", None),
        P("gx", "gy", None),
        P("gx", "gy", None),
        P("gx", "gy", None),
        P("gx", "gy", None),
        P("gx", "gy", None),
    )
    out_specs = (
        P("walker", "gx", "gy", None, None),
        P("walker", "gx", "gy", None, None),
        P("walker", None, None),
        P("walker", None, None),
    )
    return jax.shard_map(
        per_device, mesh=mesh, in_specs=in_specs, out_specs=out_specs, check_vma=False
    )
```

```python
import functools
import math

import jax
import jax.numpy as jnp
from jax import lax
from jax.experimental import pallas as pl
from jax.experimental.pallas import tpu as pltpu
from jax.sharding import PartitionSpec as P

NSITE = 4
NSUB = 8
STEPS = 4

step_size = 0.02
friction_rate = 1.0
theta_friction = 20.0
soft_alpha = 0.5
soft_beta = 0.5
theta_share = 1.0 / 1024.0

MIDDLE_Z = 1.0
REACH = 1.49
FAR = 2.0**126
SMALL = 4 * 2**20
ROWS = 16

X, Y, Z, LAM, CHG, STR, GRP, SIT = range(8)


def wrap_image(offset, length):
    shift = jnp.where(offset > 0.5 * length, length, 0.0)
    shift = jnp.where(offset < -0.5 * length, -length, shift)
    return offset - shift


def neighbour_offsets(count_x, count_y):
    found = []
    for di in (-1, 0, 1):
        for dj in (-1, 0, 1):
            key = (di % count_x, dj % count_y)
            if key != (0, 0) and key not in found:
                found.append(key)
    return found


def shifted(value, offset, count_x, count_y):
    pairs = []
    for i in range(count_x):
        for j in range(count_y):
            source = ((i + offset[0]) % count_x) * count_y + (j + offset[1]) % count_y
            pairs.append((source, i * count_y + j))
    return lax.ppermute(value, ("gx", "gy"), pairs)


def window(offset, rows_x, rows_y):
    def part(step, rows):
        return tuple(range(rows)) if step == 0 or rows <= 2 else (0, rows - 1)

    return part(offset[0], rows_x), part(offset[1], rows_y)


def sum_rows(shape):
    nr, nc = shape
    places = []
    for row in range(NSUB):
        extra, at = row // (nr * nc), row % (nr * nc)
        places.append((at // nc, 3 + extra, at % nc))
    return places


def components(shape):
    return 3 + -(-NSUB // (shape[0] * shape[1]))


def pool_sources(rows_x, rows_y, count_x, count_y, offsets):
    sources = []
    for pi in range(rows_x + 2):
        for pj in range(rows_y + 2):
            di = -1 if pi == 0 else (1 if pi == rows_x + 1 else 0)
            dj = -1 if pj == 0 else (1 if pj == rows_y + 1 else 0)
            key = (di % count_x, dj % count_y)
            block = 0 if key == (0, 0) else 1 + offsets.index(key)
            rows, cols = window(key, rows_x, rows_y)
            place = rows.index((pi - 1) % rows_x), cols.index((pj - 1) % rows_y)
            sources.append((block, place))
    return sources


def softmax_angles(angles):
    weights = jnp.exp(angles)
    return weights / jnp.sum(weights, axis=1, keepdims=True)


def angle_step(angles, speeds, packed, noise, angle_mass):
    lanes = packed.shape[1]
    share = lanes // NSITE
    lane_site = lax.broadcasted_iota(jnp.int32, packed.shape, 1) // share
    lambdas = softmax_angles(angles)
    totals = jnp.stack(
        [
            jnp.broadcast_to(
                jnp.sum(jnp.where(lane_site == site, packed, 0.0), axis=1, keepdims=True),
                packed.shape,
            )
            for site in range(NSITE)
        ]
    )
    angle_damping = math.exp(-theta_friction * step_size)
    force = -lambdas * (totals - jnp.sum(lambdas * totals, axis=1, keepdims=True))
    speeds = (
        angle_damping * speeds
        + step_size * force / angle_mass
        + math.sqrt((1.0 - angle_damping**2) / angle_mass) * noise
    )
    return angles + step_size * speeds, speeds


def lane_column(row, first, sub_iota):
    lane = lax.broadcasted_iota(jnp.int32, sub_iota.shape, 1)
    hit = lane == lax.broadcasted_iota(jnp.int32, sub_iota.shape, 0) + first
    return jnp.broadcast_to(
        jnp.sum(jnp.where(hit, row, 0.0), axis=1, keepdims=True), sub_iota.shape
    )


def block_rows(ref, place, first, last):
    i, j = place
    return jnp.concatenate([ref[i, row, j : j + 1, :] for row in range(first, last)], axis=0)


def noise_table(anoise_ref, moment, sub_iota):
    tables = []
    for site in range(NSITE):
        table = jnp.zeros_like(sub_iota)
        for sub in range(NSUB):
            table = jnp.where(sub_iota == float(sub), anoise_ref[0, moment, site, sub], table)
        tables.append(table)
    return jnp.stack(tables)


def packed_rows(ref):
    places = sum_rows((ref.shape[0], ref.shape[2]))
    return jnp.concatenate([ref[i, c, j : j + 1, :] for i, c, j in places], axis=0)


def packed_totals(blocks):
    packed = blocks[0]
    for block in blocks[1:]:
        packed = packed + block
    return packed


def step_kernel(cfg, moment, *refs):
    nb = cfg["blocks"]
    lanes = cfg["lanes"]
    refs = list(refs)

    def take(n):
        taken, refs[:n] = refs[:n], []
        return taken

    part_ref, anoise_ref = take(2)
    coord_refs = take(nb)
    (stat_ref,) = take(1) if moment > 0 else (None,)
    (tot_ref,) = take(1) if moment > 0 and not cfg["covered"] else (None,)
    vel_ref, noise_ref, inv_ref = take(3)
    (ang_ref,) = take(1)
    last = moment == STEPS - 1
    (start_ref,) = take(1) if last else (None,)
    out_refs = take(1 if last else nb)
    velo_ref, ango_ref = take(2)
    (stato_ref,) = take(1) if moment == 0 else (None,)
    (sumo_ref,) = take(1) if last else (None,)
    pool_ref, col_ref, fcol_ref, sum_ref, feat_ref, wide_ref, rhs_ref, coef_ref, off_ref, io_ref = take(10)

    sub_iota = lax.broadcasted_iota(jnp.int32, (NSUB, lanes), 0).astype(jnp.float32)
    if moment == 0:
        angles, aspeeds = (
            jnp.stack(
                [
                    lane_column(ang_ref[site : site + 1, :], kind * NSUB, sub_iota)
                    for site in range(NSITE)
                ]
            )
            for kind in range(2)
        )
    else:
        angles, aspeeds = ang_ref[0], ang_ref[1]
        if cfg["covered"]:
            packed = packed_totals([packed_rows(ref) for ref in coord_refs])
        else:
            packed = tot_ref[...]
        angles, aspeeds = angle_step(
            angles, aspeeds, packed, noise_table(anoise_ref, moment - 1, sub_iota),
            cfg["angle_mass"],
        )
    ango_ref[0] = angles
    ango_ref[1] = aspeeds
    lambdas = softmax_angles(angles)

    def line(axis, rows, count):
        at = lax.axis_index(axis)
        middle = at.astype(jnp.float32) * rows + 0.5 * rows
        shifts, cells = [], []
        for ring in range(rows + 2):
            turn = 0.0
            if ring == 0:
                turn = jnp.where(at == 0, -float(rows * count), 0.0)
            if ring == rows + 1:
                turn = jnp.where(at == count - 1, float(rows * count), 0.0)
            shifts.append(turn - middle)
            cells.append(turn - middle - (ring - 0.5 - 0.5 * rows))
        return shifts, cells

    shift_x, cell_x = line("gx", cfg["rows_x"], cfg["count_x"])
    shift_y, cell_y = line("gy", cfg["rows_y"], cfg["count_y"])
    worst = jnp.zeros((3, lanes), jnp.float32)
    row3 = lax.broadcasted_iota(jnp.int32, (3, lanes), 0)
    for index, (block, tile) in enumerate(cfg["sources"]):
        pi, pj = index // (cfg["rows_y"] + 2), index % (cfg["rows_y"] + 2)
        off_ref[0, index] = shift_x[pi]
        off_ref[1, index] = shift_y[pj]
        if moment == 0:
            stat = block_rows(coord_refs[block], tile, 3, 7)
            stato_ref[index] = stat
        else:
            stat = stat_ref[index]
        cell = jnp.where(row3 == 0, cell_x[pi], cell_y[pj])
        cell = jnp.where(row3 == 2, -MIDDLE_Z, cell)
        coords = block_rows(coord_refs[block], tile, 0, 3)
        worst = jnp.maximum(worst, jnp.abs(coords + cell))
        pool_ref[index, 0:3, :] = coords
        pool_ref[index, 4:8, :] = stat
        group = stat[2:3, :]
        lam = jnp.zeros((NSUB, lanes), jnp.float32)
        for site in range(NSITE):
            lam = lam + jnp.where(group == sub_iota + float(site * NSUB), lambdas[site], 0.0)
        lam = jnp.sum(lam, axis=0, keepdims=True)
        pool_ref[index, 3:4, :] = jnp.where(group >= 0.0, lam, 1.0)

    stray = jnp.max(worst * jnp.where(row3 == 2, 0.5, 1.0))
    for tile in range(cfg["tiles"]):
        i, j = tile // cfg["rows_y"], tile % cfg["rows_y"]
        for row in range(3):
            io_ref[tile, row : row + 1, :] = vel_ref[i, row, j : j + 1, :]
            io_ref[tile, 4 + row : 5 + row, :] = noise_ref[0, 0, i, row, j : j + 1, :]
        io_ref[tile, 3:4, :] = inv_ref[i, j : j + 1, :]

    sum_ref[...] = jnp.zeros_like(sum_ref)
    fcol_ref[...] = jnp.zeros_like(fcol_ref)
    ins = io_ref
    outs = (io_ref, sum_ref)
    near = cfg["roomy"] & (stray < REACH)

    @pl.when(near)
    def _():
        near_forces(
            cfg, lambdas, part_ref, off_ref, pool_ref, feat_ref, wide_ref, rhs_ref,
            coef_ref, ins, outs, sub_iota,
        )

    @pl.when(jnp.logical_not(near))
    def _():
        any_forces(cfg, part_ref, pool_ref, col_ref, fcol_ref, ins, outs, sub_iota)

    packed = pack_sums(cfg, sum_ref)
    for tile in range(cfg["tiles"]):
        i, j = tile // cfg["rows_y"], tile % cfg["rows_y"]
        here = slice(j, j + 1)
        for row in range(3):
            velo_ref[i, row, here, :] = io_ref[tile, 4 + row : 5 + row, :]
    for (rows, cols), ref in zip(cfg["windows"], out_refs):
        for ri, i in enumerate(rows):
            for cj, j in enumerate(cols):
                for row in range(3):
                    coord = io_ref[i * cfg["rows_y"] + j, row : row + 1, :]
                    if last:
                        coord = coord - start_ref[i, row, j : j + 1, :]
                    ref[ri, row, cj : cj + 1, :] = coord
        if not last:
            for row, (i, c, j) in enumerate(sum_rows((len(rows), len(cols)))):
                ref[i, c, j : j + 1, :] = packed[row : row + 1, :]
    if last:
        sumo_ref[...] = packed


def part_of(part_ref, cfg, tile, k):
    return part_ref[tile // cfg["rows_y"], tile % cfg["rows_y"], k]


def split3(value):
    high = value.astype(jnp.bfloat16).astype(jnp.float32)
    rest = value - high
    middle = rest.astype(jnp.bfloat16).astype(jnp.float32)
    return high, middle, rest - middle


def by_group(lambdas_of_site, group, sub_iota):
    return [
        jnp.where(group == sub_iota + float(site * NSUB), lambdas_of_site[site], 0.0)
        for site in range(NSITE)
    ]


def near_forces(
    cfg, lambdas, part_ref, off_ref, pool_ref, feat_ref, wide_ref, rhs_ref,
    coef_ref, ins, outs, sub_iota,
):
    lanes = cfg["lanes"]
    depth = cfg["depth"]
    rows = lax.broadcasted_iota(jnp.int32, (8, lanes), 0)
    ones = jnp.ones((NSUB, lanes), jnp.float32)
    nothing = jnp.zeros((8, lanes), jnp.float32)
    pad = [nothing] * ((depth - 6 * 8 - 2 * NSITE * NSUB) // 8)

    pick_rows = lax.broadcasted_iota(jnp.int32, (depth, lanes), 0)
    hit = (pick_rows == 7) | (pick_rows == 16 + 7) | (pick_rows == 40 + 7)
    pick = jnp.where(hit, 1.0, 0.0).astype(jnp.bfloat16)

    def centred(index):
        block = pool_ref[index]
        shift = jnp.where(rows == 0, off_ref[0, index], 0.0)
        shift = jnp.where(rows == 1, off_ref[1, index], shift)
        shift = jnp.where(rows == 2, -MIDDLE_Z, shift)
        moved = block + shift
        square = jnp.where(rows < 3, moved * moved, 0.0)
        return block, moved, jnp.sum(square, axis=0, keepdims=True)

    def table_dot(features, ref):
        table = jnp.concatenate([ref[c] for c in range(ref.shape[0])], axis=1)
        return jnp.dot(features, table, preferred_element_type=jnp.float32)

    def some_pool(k, carry):
        for u in range(cfg["pool_group"]):
            one_pool(k * cfg["pool_group"] + u)
        return carry

    def one_pool(index):
        block, moved, norm = centred(index)
        table = jnp.where(rows == 5, norm, moved)
        table = jnp.where(rows == 6, 1.0, table)
        table = jnp.where(rows == 7, block[STR : STR + 1, :], table)
        high, middle, low = split3(table)
        member = by_group([ones] * NSITE, block[GRP : GRP + 1, :], sub_iota)
        features = jnp.concatenate(
            [high, high, middle, middle, high, low] + member + member + pad, axis=0
        )
        features = features.T.astype(jnp.bfloat16)
        feat_ref[index] = features
        wide_ref[index] = jnp.dot(features, pick, preferred_element_type=jnp.float32)
        coef = jnp.concatenate([high, middle, low, nothing], axis=0).astype(jnp.bfloat16)
        coef_ref[index] = jnp.concatenate([coef, coef], axis=1)

    lax.fori_loop(0, cfg["pool"] // cfg["pool_group"], some_pool, 0)
    none_columns = lax.broadcasted_iota(jnp.int32, (lanes, depth), 1)
    feat_ref[cfg["pool"]] = jnp.where(none_columns == 6, 1.0, 0.0).astype(jnp.bfloat16)
    wide_ref[cfg["pool"]] = jnp.zeros((lanes, lanes), jnp.float32)
    coef_ref[cfg["pool"]] = jnp.zeros((32, 2 * lanes), jnp.bfloat16)

    spread = [lam - lam * lam for lam in lambdas]
    half = [0.5 - lam for lam in lambdas]

    def one_tile(tile, carry):
        own = (tile // cfg["rows_y"] + 1) * (cfg["rows_y"] + 2) + tile % cfg["rows_y"] + 1
        block, moved, norm = centred(own)
        group, site_row = block[GRP : GRP + 1, :], block[SIT : SIT + 1, :]
        lam, charge, strength = (block[r : r + 1, :] for r in (LAM, CHG, STR))
        ratio = charge / strength

        gap = jnp.where(rows < 3, -2.0 * moved, 0.0)
        gap = jnp.where(rows == 3, -0.5 * lam, gap)
        gap = jnp.where(rows == 5, 1.0, gap)
        gap = jnp.where(rows == 6, norm + 1.5, gap)
        pair = by_group(spread, group, sub_iota)
        far = [
            jnp.where(
                (site_row == float(site)) & (group != sub_iota + float(site * NSUB)), FAR, 0.0
            )
            for site in range(NSITE)
        ]
        columns = (
            (gap, [f - 0.5 * p for f, p in zip(far, pair)]),
            (jnp.where(rows == 3, lam, 0.0), pair),
            (jnp.where(rows == 3, 1.0, 0.0), by_group(half, group, sub_iota)),
            (jnp.where(rows == 4, ratio, 0.0), [nothing] * NSITE),
        )
        for column, (table, member) in enumerate(columns):
            high, middle, low = split3(table)
            tops = [m.astype(jnp.bfloat16).astype(jnp.float32) for m in member]
            rests = [m - t for m, t in zip(member, tops)]
            rhs_ref[column] = jnp.concatenate(
                [high, middle, high, middle, low, high] + tops + rests + pad, axis=0
            ).astype(jnp.bfloat16)

        def some_partners(k, sums):
            indices = [part_of(part_ref, cfg, tile, k + u) for u in range(cfg["slots"])]
            indices = [jnp.where(index < 0, cfg["pool"], index) for index in indices]
            outs = []
            for first in range(0, len(indices), 3):
                some = indices[first : first + 3]
                out = table_dot(jnp.concatenate([feat_ref[index] for index in some], axis=0), rhs_ref)
                outs += [out[n * lanes : (n + 1) * lanes] for n in range(len(some))]
            moments, fd = sums
            for index, out in zip(indices, outs):
                tops, rests = [], []
                for i in range(lanes // ROWS):
                    here = slice(ROWS * i, ROWS * i + ROWS)
                    gap2, s, w, q = (out[here, c * lanes : (c + 1) * lanes] for c in range(4))
                    eb = wide_ref[index, here, :]
                    rs = lax.rsqrt(gap2)
                    t = rs * rs * rs
                    a = eb * t
                    b = (s * t) * (a + 0.25 * q)
                    sens = (rs * (a + q) + b) * w
                    for j in range(ROWS // 8):
                        fd = fd + sens[8 * j : 8 * j + 8, :]
                    top = b.astype(jnp.bfloat16)
                    tops.append(top)
                    rests.append((b - top.astype(jnp.float32)).astype(jnp.bfloat16))
                moments = moments + jnp.dot(
                    coef_ref[index],
                    jnp.concatenate(tops + rests, axis=0),
                    preferred_element_type=jnp.float32,
                )
            return moments, fd

        moments, fd = some_partners(0, (jnp.zeros((32, lanes), jnp.float32), nothing))
        moments = moments[0:8] + moments[8:16] + moments[16:24]
        fd = jnp.sum(fd, axis=0, keepdims=True)
        forces = moved[0:3, :] * moments[6:7, :] - moments[0:3, :]
        rs = lax.rsqrt(1.5 - 0.5 * lam)
        t = rs * rs * rs
        a, q = strength * t, ratio * charge
        itself = rs * (a + q) + lam * t * (a + 0.25 * q)
        drive = strength * (fd - 0.5 * itself)
        finish_tile(cfg, tile, (4.0 * strength) * forces, drive, block, ins, outs, sub_iota)
        return carry

    def some_tiles(k, carry):
        for u in range(4):
            one_tile(k * 4 + u, carry)
        return carry

    lax.fori_loop(0, cfg["tiles"] // 4, some_tiles, 0)


def any_forces(cfg, part_ref, pool_ref, col_ref, fcol_ref, ins, outs, sub_iota):
    tiles, lanes = cfg["tiles"], cfg["lanes"]
    chunk = 32

    def one_tile(tile, carry):
        own = (tile // cfg["rows_y"] + 1) * (cfg["rows_y"] + 2) + tile % cfg["rows_y"] + 1
        block = pool_ref[own]
        col_ref[...] = block.T
        count = jnp.int32(0)
        for k in range(cfg["slots"]):
            count += (part_of(part_ref, cfg, tile, k) >= 0).astype(jnp.int32)

        def one_chunk(c, carry):
            start = pl.multiple_of(c * chunk, chunk)
            cols = col_ref[pl.ds(start, chunk), :]
            lanes_iota = lax.broadcasted_iota(jnp.int32, (chunk, lanes), 1)
            diagonal = lanes_iota == lax.broadcasted_iota(jnp.int32, (chunk, lanes), 0) + start

            def one_partner(k, sums):
                fx, fy, fz, fd = sums
                index = part_of(part_ref, cfg, tile, k)
                other = pool_ref[index]

                def own_col(row):
                    return cols[:, row : row + 1]

                def other_row(row):
                    return other[row : row + 1, :]

                dx = wrap_image(own_col(X) - other_row(X), cfg["box_x"])
                dy = wrap_image(own_col(Y) - other_row(Y), cfg["box_y"])
                dz = own_col(Z) - other_row(Z)
                r2 = dx * dx + dy * dy + dz * dz
                same = (own_col(GRP) == other_row(GRP)) & (own_col(GRP) >= 0.0)
                site = (own_col(SIT) == other_row(SIT)) & (own_col(SIT) >= 0.0)
                drop = (site & jnp.logical_not(same)) | (diagonal & (index == own))
                lam_a, lam_b = own_col(LAM), other_row(LAM)
                s = jnp.where(same, lam_a, lam_a * lam_b)
                w = jnp.where(same, 0.5, lam_b)
                e = own_col(STR) * other_row(STR)
                q = own_col(CHG) * other_row(CHG)
                rs = lax.rsqrt(1.0 + 0.5 * (1.0 - s) + r2)
                t = rs * rs * rs
                a = e * t
                b = s * t * (a + 0.25 * q)
                sens = rs * (a + q) + b
                b = jnp.where(drop, 0.0, b)
                sens = jnp.where(drop, 0.0, sens * w)
                return fx + b * dx, fy + b * dy, fz + b * dz, fd + sens

            zero = jnp.zeros((chunk, lanes), jnp.float32)
            sums = lax.fori_loop(0, count, one_partner, (zero, zero, zero, zero))
            for row, value in enumerate(sums):
                fcol_ref[pl.ds(start, chunk), row : row + 1] = jnp.sum(
                    value, axis=1, keepdims=True
                )
            return carry

        lax.fori_loop(0, lanes // chunk, one_chunk, 0)
        forces = fcol_ref[...].T
        finish_tile(
            cfg, tile, 4.0 * forces[0:3, :], forces[3:4, :], block,
            ins, outs, sub_iota,
        )
        return carry

    lax.fori_loop(0, tiles, one_tile, 0)


def finish_tile(cfg, tile, forces, drive, block, ins, outs, sub_iota):
    _, sum_ref = outs
    damping = math.exp(-friction_rate * step_size)
    rows = ins[tile]
    inverse = rows[3:4, :]
    speeds = (
        damping * rows[0:3, :]
        + step_size * forces * inverse
        + jnp.sqrt((1.0 - damping**2) * inverse) * rows[4:7, :]
    )
    ins[tile, 0:3, :] = block[0:3, :] + step_size * speeds
    ins[tile, 4:7, :] = speeds
    group = block[GRP : GRP + 1, :]
    for site in range(NSITE):
        sum_ref[site] += jnp.where(group == sub_iota + float(site * NSUB), drive, 0.0)


def pack_sums(cfg, sum_ref):
    lanes = cfg["lanes"]
    share = lanes // NSITE
    lane_site = lax.broadcasted_iota(jnp.int32, (NSUB, lanes), 1) // share
    packed = jnp.zeros((NSUB, lanes), jnp.float32)
    for site in range(NSITE):
        folded = sum_ref[site]
        width = lanes
        while width > share:
            width //= 2
            folded = folded + pltpu.roll(folded, width, 1)
        packed = packed + jnp.where(lane_site == site, folded, 0.0)
    return packed


def step_call(cfg, moment, parts, anoise, blocks, stat, totals, vel, noise, inverse, ang, start):
    tiles, lanes, pool = cfg["tiles"], cfg["lanes"], cfg["pool"]
    rows_x, rows_y = cfg["rows_x"], cfg["rows_y"]
    last = moment == STEPS - 1
    vmem = pl.BlockSpec(memory_space=pltpu.VMEM)
    smem = pl.BlockSpec(memory_space=pltpu.SMEM)
    noise_spec = pl.BlockSpec(
        (1, 1, rows_x, 3, rows_y, lanes), lambda i: (0, moment, 0, 0, 0, 0)
    )
    args = [(parts, smem), (anoise, smem)] + [(block, vmem) for block in blocks]
    if moment > 0:
        args.append((stat, vmem))
    if totals is not None:
        args.append((totals, vmem))
    args += [(vel, vmem), (noise, noise_spec), (inverse, vmem)]
    args.append((ang, vmem))
    if last:
        args.append((start, vmem))
    vectors = (rows_x, 3, rows_y, lanes)
    if last:
        shapes = [vectors]
    else:
        held = [(len(rows), len(cols)) for rows, cols in cfg["windows"]]
        shapes = [(nr, components((nr, nc)), nc, lanes) for nr, nc in held]
    shapes.append(vectors)
    shapes.append((2, NSITE, NSUB, lanes))
    if moment == 0:
        shapes.append((pool, 4, lanes))
    if last:
        shapes.append((NSUB, lanes))
    depth = cfg["depth"]
    return pl.pallas_call(
        functools.partial(step_kernel, cfg, moment),
        grid=(1,),
        out_shape=tuple(jax.ShapeDtypeStruct(shape, jnp.float32) for shape in shapes),
        in_specs=[spec for _, spec in args],
        out_specs=(vmem,) * len(shapes),
        scratch_shapes=[
            pltpu.VMEM((pool, 8, lanes), jnp.float32),
            pltpu.VMEM((lanes, 8), jnp.float32),
            pltpu.VMEM((lanes, 8), jnp.float32),
            pltpu.VMEM((NSITE, NSUB, lanes), jnp.float32),
            pltpu.VMEM((pool + 1, lanes, depth), jnp.bfloat16),
            pltpu.VMEM((pool + 1, lanes, lanes), jnp.float32),
            pltpu.VMEM((4, depth, lanes), jnp.bfloat16),
            pltpu.VMEM((pool + 1, 32, 2 * lanes), jnp.bfloat16),
            pltpu.SMEM((2, pool), jnp.float32),
            pltpu.VMEM((tiles, 8, lanes), jnp.float32),
        ],
        compiler_params=pltpu.CompilerParams(vmem_limit_bytes=4 * SMALL),
        name="langevin_step",
    )(*[value for value, _ in args])


def angle_kernel(cfg, *refs):
    anoise_ref, ang_ref = refs[:2]
    tot_refs, (theta_ref, speed_ref) = refs[2:-2], refs[-2:]
    lanes = cfg["lanes"]
    sub_iota = lax.broadcasted_iota(jnp.int32, (NSUB, lanes), 0).astype(jnp.float32)
    packed = packed_totals([ref[...] for ref in tot_refs])
    results = angle_step(
        ang_ref[0], ang_ref[1], packed, noise_table(anoise_ref, STEPS - 1, sub_iota),
        cfg["angle_mass"],
    )
    hit = lax.broadcasted_iota(jnp.int32, (NSUB, lanes), 1) == lax.broadcasted_iota(
        jnp.int32, (NSUB, lanes), 0
    )
    for ref, result in zip((theta_ref, speed_ref), results):
        for site in range(NSITE):
            row = jnp.sum(jnp.where(hit, result[site], 0.0), axis=0, keepdims=True)
            ref[0, site : site + 1, :] = row[:, 0:NSUB]


def angle_call(cfg, anoise, ang, totals):
    vmem = pl.BlockSpec(memory_space=pltpu.VMEM)
    shape = jax.ShapeDtypeStruct((1, NSITE, NSUB), jnp.float32)
    return pl.pallas_call(
        functools.partial(angle_kernel, cfg),
        out_shape=(shape, shape),
        in_specs=[pl.BlockSpec(memory_space=pltpu.SMEM)] + [vmem] * (1 + len(totals)),
        out_specs=(vmem, vmem),
        name="last_angles",
        compiler_params=pltpu.CompilerParams(vmem_limit_bytes=SMALL),
    )(anoise, ang, *totals)


def send_kernel(width, sets, slot_ref, mine_ref, other_ref, *out_refs):
    me = lax.axis_index("walker")
    for k, ref in enumerate(out_refs, 1):
        wanted = slot_ref[lax.rem(me + k * width, width * sets)]
        own = lax.rem(wanted, width) == lax.rem(me, width)

        @pl.when(own)
        def _():
            ref[...] = mine_ref[...]

        @pl.when(jnp.logical_not(own))
        def _():
            ref[...] = other_ref[...]


def pick_kernel(width, sets, windows, slot_ref, *refs):
    block_refs = refs[: sets + 1]
    charge_ref, strength_ref, site_ref, sub_ref = refs[sets + 1 : sets + 5]
    *pay_refs, vel_ref, ang_ref = refs[sets + 5 :]
    rows_x = vel_ref.shape[0]
    me = lax.axis_index("walker")
    source = slot_ref[me]
    hop = lax.rem(me // width - source // width + sets, sets)
    away = (lax.rem(source, width) != lax.rem(me, width)).astype(jnp.int32)
    choice = jnp.where(hop > 0, hop + 1, away)
    own_ref = pay_refs[0]
    for k, ref in enumerate(block_refs):

        @pl.when(choice == k)
        def _():
            for i in range(rows_x):
                own_ref[i, 0:3] = ref[6 * i : 6 * i + 3]
                vel_ref[i] = ref[6 * i + 3 : 6 * i + 6]
            ang_ref[...] = ref[6 * rows_x]

    site, sub = site_ref[...], sub_ref[...]
    grouped = site < NSITE
    own_ref[:, 3] = charge_ref[...]
    own_ref[:, 4] = strength_ref[...]
    own_ref[:, 5] = jnp.where(grouped, site * NSUB + sub, -1).astype(jnp.float32)
    own_ref[:, 6] = jnp.where(grouped, site, -1).astype(jnp.float32)
    for (rows, cols), ref in zip(windows[1:], pay_refs[1:]):
        for ri, i in enumerate(rows):
            for cj, j in enumerate(cols):
                ref[ri, :, cj : cj + 1, :] = own_ref[i, :, j : j + 1, :]


def pack_kernel(pos_ref, vel_ref, theta_ref, speed_ref, out_ref):
    rows_x = pos_ref.shape[0]
    for i in range(rows_x):
        out_ref[6 * i : 6 * i + 3] = pos_ref[i]
        out_ref[6 * i + 3 : 6 * i + 6] = vel_ref[i]
    out_ref[6 * rows_x] = jnp.zeros(out_ref.shape[1:], jnp.float32)
    out_ref[6 * rows_x, :, 0:NSUB] = theta_ref[0]
    out_ref[6 * rows_x, :, NSUB : 2 * NSUB] = speed_ref[0]


def clone(cfg, positions, velocities, theta, speed, source_slot, charges, strengths, atom_site, atom_sub):
    peers = lax.axis_size("walker")
    width = 2 if peers % 2 == 0 else 1
    sets = peers // width
    rows_x, rows_y, lanes = charges.shape
    vmem = pl.BlockSpec(memory_space=pltpu.VMEM)
    smem = pl.BlockSpec(memory_space=pltpu.SMEM)
    message = pl.pallas_call(
        pack_kernel,
        out_shape=jax.ShapeDtypeStruct((6 * rows_x + 1, rows_y, lanes), jnp.float32),
        in_specs=[vmem] * 4,
        out_specs=vmem,
        name="pack_walker",
        compiler_params=pltpu.CompilerParams(vmem_limit_bytes=SMALL),
    )(positions, velocities, theta, speed)
    other = message
    if width == 2:
        other = lax.ppermute(message, "walker", [(w, w ^ 1) for w in range(peers)])
    blocks = [message, other]
    if sets > 1:
        shape = jax.ShapeDtypeStruct(message.shape, jnp.float32)
        sent = pl.pallas_call(
            functools.partial(send_kernel, width, sets),
            out_shape=(shape,) * (sets - 1),
            in_specs=[smem, vmem, vmem],
            out_specs=(vmem,) * (sets - 1),
            name="choose_sent",
        compiler_params=pltpu.CompilerParams(vmem_limit_bytes=SMALL),
        )(source_slot, message, other)
        for k, value in enumerate(sent, 1):
            blocks.append(
                lax.ppermute(
                    value, "walker", [(w, (w + k * width) % peers) for w in range(peers)]
                )
            )
    shapes = [(len(rows), 7, len(cols), lanes) for rows, cols in cfg["windows"]]
    shapes += [(rows_x, 3, rows_y, lanes), (rows_y, lanes)]
    return pl.pallas_call(
        functools.partial(pick_kernel, width, sets, cfg["windows"]),
        out_shape=tuple(jax.ShapeDtypeStruct(shape, jnp.float32) for shape in shapes),
        in_specs=[smem] + [vmem] * (len(blocks) + 4),
        out_specs=(vmem,) * len(shapes),
        name="choose_received",
        compiler_params=pltpu.CompilerParams(vmem_limit_bytes=SMALL),
    )(source_slot, *blocks, charges, strengths, atom_site, atom_sub)


def make_cfg(rows_x, rows_y, lanes, count_x, count_y, slots, offsets):
    tiles = rows_x * rows_y
    return dict(
        blocks=1 + len(offsets),
        covered=1 + len(offsets) == count_x * count_y,
        tiles=tiles,
        lanes=lanes,
        rows_x=rows_x,
        rows_y=rows_y,
        count_x=count_x,
        count_y=count_y,
        slots=slots,
        pool=(rows_x + 2) * (rows_y + 2),
        windows=[window(offset, rows_x, rows_y) for offset in [(0, 0)] + offsets],
        sources=pool_sources(rows_x, rows_y, count_x, count_y, offsets),
        depth=128,
        pool_group=next(g for g in (12, 6, 4, 3, 2, 1) if (rows_x + 2) * (rows_y + 2) % g == 0),
        roomy=min(rows_x * count_x, rows_y * count_y) >= 8,
        box_x=float(rows_x * count_x),
        box_y=float(rows_y * count_y),
        angle_mass=rows_x * count_x * rows_y * count_y * lanes * theta_share,
    )


def per_device(
    positions,
    velocities,
    lambda_theta,
    theta_velocity,
    source_slot,
    atom_noise,
    theta_noise,
    charges,
    strengths,
    inverse_mass,
    atom_site,
    atom_sub,
    partners,
):
    count_x, count_y = lax.axis_size("gx"), lax.axis_size("gy")
    rows_x, rows_y, lanes = charges.shape
    tiles = rows_x * rows_y
    offsets = neighbour_offsets(count_x, count_y)
    cfg = make_cfg(rows_x, rows_y, lanes, count_x, count_y, partners.shape[-1], offsets)

    def gather_blocks(values):
        return [values[0]] + [
            shifted(value, offset, count_x, count_y) for value, offset in zip(values[1:], offsets)
        ]

    *pays, vel, ang = clone(
        cfg, positions[0].transpose(0, 2, 1, 3), velocities[0].transpose(0, 2, 1, 3),
        lambda_theta, theta_velocity, source_slot, charges, strengths, atom_site, atom_sub,
    )
    noise = atom_noise.transpose(0, 1, 2, 4, 3, 5)
    first = pays[0]
    pool_stat = None
    for moment in range(STEPS):
        totals = None
        if moment > 0 and not cfg["covered"]:
            totals = lax.psum(pays[0][:, 3].reshape(tiles, lanes)[:NSUB], ("gx", "gy"))
        outs = step_call(
            cfg, moment, partners, theta_noise, gather_blocks(pays), pool_stat, totals, vel,
            noise, inverse_mass, ang, first,
        )
        own = cfg["blocks"] if moment < STEPS - 1 else 1
        pays, (vel, ang, *rest) = outs[:own], outs[own:]
        if moment == 0:
            pool_stat = rest[0]
    packed = rest[0]
    if cfg["covered"]:
        totals = gather_blocks([packed] * cfg["blocks"])
    else:
        totals = [lax.psum(packed, ("gx", "gy"))]
    theta, theta_speed = angle_call(cfg, theta_noise, ang, totals)
    back = lambda value: value.transpose(0, 2, 1, 3)[None]
    return back(pays[0]), back(vel), theta, theta_speed


def solution(mesh):
    in_specs = (
        P("walker", "gx", "gy", None, None),
        P("walker", "gx", "gy", None, None),
        P("walker", None, None),
        P("walker", None, None),
        P(),
        P("walker", None, "gx", "gy", None, None),
        P("walker", None, None, None),
        P("gx", "gy", None),
        P("gx", "gy", None),
        P("gx", "gy", None),
        P("gx", "gy", None),
        P("gx", "gy", None),
        P("gx", "gy", None),
    )
    out_specs = (
        P("walker", "gx", "gy", None, None),
        P("walker", "gx", "gy", None, None),
        P("walker", None, None),
        P("walker", None, None),
    )
    return jax.shard_map(
        per_device, mesh=mesh, in_specs=in_specs, out_specs=out_specs, check_vma=False
    )
```

```python
import functools
import math

import jax
import jax.numpy as jnp
from jax import lax
from jax.experimental import pallas as pl
from jax.experimental.pallas import tpu as pltpu
from jax.sharding import PartitionSpec as P

NSITE = 4
NSUB = 8
STEPS = 4

step_size = 0.02
friction_rate = 1.0
theta_friction = 20.0
soft_alpha = 0.5
soft_beta = 0.5
theta_share = 1.0 / 1024.0

MIDDLE_Z = 1.0
REACH = 1.49
FAR = 2.0**126
SMALL = 4 * 2**20
ROWS = 16

X, Y, Z, LAM, CHG, STR, GRP, SIT = range(8)


def wrap_image(offset, length):
    shift = jnp.where(offset > 0.5 * length, length, 0.0)
    shift = jnp.where(offset < -0.5 * length, -length, shift)
    return offset - shift


def neighbour_offsets(count_x, count_y):
    found = []
    for di in (-1, 0, 1):
        for dj in (-1, 0, 1):
            key = (di % count_x, dj % count_y)
            if key != (0, 0) and key not in found:
                found.append(key)
    return found


def shifted(value, offset, count_x, count_y):
    pairs = []
    for i in range(count_x):
        for j in range(count_y):
            source = ((i + offset[0]) % count_x) * count_y + (j + offset[1]) % count_y
            pairs.append((source, i * count_y + j))
    return lax.ppermute(value, ("gx", "gy"), pairs)


def window(offset, rows_x, rows_y):
    def part(step, rows):
        return tuple(range(rows)) if step == 0 or rows <= 2 else (0, rows - 1)

    return part(offset[0], rows_x), part(offset[1], rows_y)


def sum_rows(shape):
    nr, nc = shape
    places = []
    for row in range(NSUB):
        extra, at = row // (nr * nc), row % (nr * nc)
        places.append((at // nc, 3 + extra, at % nc))
    return places


def components(shape):
    return 3 + -(-NSUB // (shape[0] * shape[1]))


def pool_sources(rows_x, rows_y, count_x, count_y, offsets):
    sources = []
    for pi in range(rows_x + 2):
        for pj in range(rows_y + 2):
            di = -1 if pi == 0 else (1 if pi == rows_x + 1 else 0)
            dj = -1 if pj == 0 else (1 if pj == rows_y + 1 else 0)
            key = (di % count_x, dj % count_y)
            block = 0 if key == (0, 0) else 1 + offsets.index(key)
            rows, cols = window(key, rows_x, rows_y)
            place = rows.index((pi - 1) % rows_x), cols.index((pj - 1) % rows_y)
            sources.append((block, place))
    return sources


def softmax_angles(angles):
    weights = jnp.exp(angles)
    return weights / jnp.sum(weights, axis=1, keepdims=True)


def angle_step(angles, speeds, packed, noise, angle_mass):
    lanes = packed.shape[1]
    share = lanes // NSITE
    lane_site = lax.broadcasted_iota(jnp.int32, packed.shape, 1) // share
    lambdas = softmax_angles(angles)
    totals = jnp.stack(
        [
            jnp.broadcast_to(
                jnp.sum(jnp.where(lane_site == site, packed, 0.0), axis=1, keepdims=True),
                packed.shape,
            )
            for site in range(NSITE)
        ]
    )
    angle_damping = math.exp(-theta_friction * step_size)
    force = -lambdas * (totals - jnp.sum(lambdas * totals, axis=1, keepdims=True))
    speeds = (
        angle_damping * speeds
        + step_size * force / angle_mass
        + math.sqrt((1.0 - angle_damping**2) / angle_mass) * noise
    )
    return angles + step_size * speeds, speeds


def lane_column(row, first, sub_iota):
    shape = (sub_iota.shape[0], row.shape[1])
    hit = lax.broadcasted_iota(jnp.int32, shape, 1) == (
        lax.broadcasted_iota(jnp.int32, shape, 0) + first
    )
    return jnp.broadcast_to(
        jnp.sum(jnp.where(hit, row, 0.0), axis=1, keepdims=True), sub_iota.shape
    )


def block_rows(ref, place, first, last):
    i, j = place
    return jnp.concatenate([ref[i, row, j : j + 1, :] for row in range(first, last)], axis=0)


def noise_table(anoise_ref, moment, sub_iota):
    return jnp.stack(
        [
            lane_column(anoise_ref[0, moment, site : site + 1, :], 0, sub_iota)
            for site in range(NSITE)
        ]
    )


def packed_rows(ref):
    places = sum_rows((ref.shape[0], ref.shape[2]))
    return jnp.concatenate([ref[i, c, j : j + 1, :] for i, c, j in places], axis=0)


def packed_totals(blocks):
    packed = blocks[0]
    for block in blocks[1:]:
        packed = packed + block
    return packed


def step_kernel(cfg, moment, *refs):
    nb = cfg["blocks"]
    lanes = cfg["lanes"]
    refs = list(refs)

    def take(n):
        taken, refs[:n] = refs[:n], []
        return taken

    part_hbm, anoise_ref = take(2)
    coord_refs = take(nb)
    (stat_ref,) = take(1) if moment > 0 else (None,)
    (tot_ref,) = take(1) if moment > 0 and not cfg["covered"] else (None,)
    vel_ref, noise_ref, inv_ref = take(3)
    (ang_ref,) = take(1)
    last = moment == STEPS - 1
    (start_ref,) = take(1) if last else (None,)
    out_refs = take(1 if last else nb)
    velo_ref, ango_ref = take(2)
    (stato_ref,) = take(1) if moment == 0 else (None,)
    (sumo_ref,) = take(1) if last else (None,)
    pool_ref, col_ref, fcol_ref, sum_ref, feat_ref, wide_ref, rhs_ref, coef_ref, off_ref, io_ref = take(10)
    part_ref, part_sem = take(2)
    part_copy = pltpu.make_async_copy(part_hbm, part_ref, part_sem)
    part_copy.start()

    sub_iota = lax.broadcasted_iota(jnp.int32, (NSUB, lanes), 0).astype(jnp.float32)
    if moment == 0:
        angles, aspeeds = (
            jnp.stack(
                [
                    lane_column(ang_ref[site : site + 1, :], kind * NSUB, sub_iota)
                    for site in range(NSITE)
                ]
            )
            for kind in range(2)
        )
    else:
        angles, aspeeds = ang_ref[0], ang_ref[1]
        if cfg["covered"]:
            packed = packed_totals([packed_rows(ref) for ref in coord_refs])
        else:
            packed = tot_ref[...]
        angles, aspeeds = angle_step(
            angles, aspeeds, packed, noise_table(anoise_ref, moment - 1, sub_iota),
            cfg["angle_mass"],
        )
    ango_ref[0] = angles
    ango_ref[1] = aspeeds
    lambdas = softmax_angles(angles)

    def line(axis, rows, count):
        at = lax.axis_index(axis)
        middle = at.astype(jnp.float32) * rows + 0.5 * rows
        shifts, cells = [], []
        for ring in range(rows + 2):
            turn = 0.0
            if ring == 0:
                turn = jnp.where(at == 0, -float(rows * count), 0.0)
            if ring == rows + 1:
                turn = jnp.where(at == count - 1, float(rows * count), 0.0)
            shifts.append(turn - middle)
            cells.append(turn - middle - (ring - 0.5 - 0.5 * rows))
        return shifts, cells

    shift_x, cell_x = line("gx", cfg["rows_x"], cfg["count_x"])
    shift_y, cell_y = line("gy", cfg["rows_y"], cfg["count_y"])
    worst = jnp.zeros((3, lanes), jnp.float32)
    row3 = lax.broadcasted_iota(jnp.int32, (3, lanes), 0)
    for index, (block, tile) in enumerate(cfg["sources"]):
        pi, pj = index // (cfg["rows_y"] + 2), index % (cfg["rows_y"] + 2)
        off_ref[0, index] = shift_x[pi]
        off_ref[1, index] = shift_y[pj]
        if moment == 0:
            stat = block_rows(coord_refs[block], tile, 3, 7)
            stato_ref[index] = stat
        else:
            stat = stat_ref[index]
        cell = jnp.where(row3 == 0, cell_x[pi], cell_y[pj])
        cell = jnp.where(row3 == 2, -MIDDLE_Z, cell)
        coords = block_rows(coord_refs[block], tile, 0, 3)
        worst = jnp.maximum(worst, jnp.abs(coords + cell))
        pool_ref[index, 0:3, :] = coords
        pool_ref[index, 4:8, :] = stat
        group = stat[2:3, :]
        lam = jnp.zeros((NSUB, lanes), jnp.float32)
        for site in range(NSITE):
            lam = lam + jnp.where(group == sub_iota + float(site * NSUB), lambdas[site], 0.0)
        lam = jnp.sum(lam, axis=0, keepdims=True)
        pool_ref[index, 3:4, :] = jnp.where(group >= 0.0, lam, 1.0)

    stray = jnp.max(worst * jnp.where(row3 == 2, 0.5, 1.0))
    for tile in range(cfg["tiles"]):
        i, j = tile // cfg["rows_y"], tile % cfg["rows_y"]
        for row in range(3):
            io_ref[tile, row : row + 1, :] = vel_ref[i, row, j : j + 1, :]
            io_ref[tile, 4 + row : 5 + row, :] = noise_ref[0, 0, i, row, j : j + 1, :]
        io_ref[tile, 3:4, :] = inv_ref[i, j : j + 1, :]

    sum_ref[...] = jnp.zeros_like(sum_ref)
    fcol_ref[...] = jnp.zeros_like(fcol_ref)
    ins = io_ref
    outs = (io_ref, sum_ref)
    near = cfg["roomy"] & (stray < REACH)

    part_copy.wait()

    @pl.when(near)
    def _():
        near_forces(
            cfg, lambdas, part_ref, off_ref, pool_ref, feat_ref, wide_ref, rhs_ref,
            coef_ref, ins, outs, sub_iota,
        )

    @pl.when(jnp.logical_not(near))
    def _():
        any_forces(cfg, part_ref, pool_ref, col_ref, fcol_ref, ins, outs, sub_iota)

    packed = pack_sums(cfg, sum_ref)
    for tile in range(cfg["tiles"]):
        i, j = tile // cfg["rows_y"], tile % cfg["rows_y"]
        here = slice(j, j + 1)
        for row in range(3):
            velo_ref[i, row, here, :] = io_ref[tile, 4 + row : 5 + row, :]
    for (rows, cols), ref in zip(cfg["windows"], out_refs):
        for ri, i in enumerate(rows):
            for cj, j in enumerate(cols):
                for row in range(3):
                    coord = io_ref[i * cfg["rows_y"] + j, row : row + 1, :]
                    if last:
                        coord = coord - start_ref[i, row, j : j + 1, :]
                    ref[ri, row, cj : cj + 1, :] = coord
        if not last:
            for row, (i, c, j) in enumerate(sum_rows((len(rows), len(cols)))):
                ref[i, c, j : j + 1, :] = packed[row : row + 1, :]
    if last:
        sumo_ref[...] = packed


def part_of(part_ref, cfg, tile, k):
    return part_ref[tile // cfg["rows_y"], tile % cfg["rows_y"], k]


def split3(value):
    high = value.astype(jnp.bfloat16).astype(jnp.float32)
    rest = value - high
    middle = rest.astype(jnp.bfloat16).astype(jnp.float32)
    return high, middle, rest - middle


def by_group(lambdas_of_site, group, sub_iota):
    return [
        jnp.where(group == sub_iota + float(site * NSUB), lambdas_of_site[site], 0.0)
        for site in range(NSITE)
    ]


def near_forces(
    cfg, lambdas, part_ref, off_ref, pool_ref, feat_ref, wide_ref, rhs_ref,
    coef_ref, ins, outs, sub_iota,
):
    lanes = cfg["lanes"]
    depth = cfg["depth"]
    rows = lax.broadcasted_iota(jnp.int32, (8, lanes), 0)
    ones = jnp.ones((NSUB, lanes), jnp.float32)
    nothing = jnp.zeros((8, lanes), jnp.float32)
    pad = [nothing] * ((depth - 6 * 8 - 2 * NSITE * NSUB) // 8)

    pick_rows = lax.broadcasted_iota(jnp.int32, (depth, lanes), 0)
    hit = (pick_rows == 7) | (pick_rows == 16 + 7) | (pick_rows == 40 + 7)
    pick = jnp.where(hit, 1.0, 0.0).astype(jnp.bfloat16)

    def centred(index):
        block = pool_ref[index]
        shift = jnp.where(rows == 0, off_ref[0, index], 0.0)
        shift = jnp.where(rows == 1, off_ref[1, index], shift)
        shift = jnp.where(rows == 2, -MIDDLE_Z, shift)
        moved = block + shift
        square = jnp.where(rows < 3, moved * moved, 0.0)
        return block, moved, jnp.sum(square, axis=0, keepdims=True)

    def table_dot(features, ref):
        table = jnp.concatenate([ref[c] for c in range(ref.shape[0])], axis=1)
        return jnp.dot(features, table, preferred_element_type=jnp.float32)

    def some_pool(k, carry):
        for u in range(cfg["pool_group"]):
            one_pool(k * cfg["pool_group"] + u)
        return carry

    def one_pool(index):
        block, moved, norm = centred(index)
        table = jnp.where(rows == 5, norm, moved)
        table = jnp.where(rows == 6, 1.0, table)
        table = jnp.where(rows == 7, block[STR : STR + 1, :], table)
        high, middle, low = split3(table)
        member = by_group([ones] * NSITE, block[GRP : GRP + 1, :], sub_iota)
        features = jnp.concatenate(
            [high, high, middle, middle, high, low] + member + member + pad, axis=0
        )
        features = features.T.astype(jnp.bfloat16)
        feat_ref[index] = features
        wide_ref[index] = jnp.dot(features, pick, preferred_element_type=jnp.float32)
        coef = jnp.concatenate([high, middle, low, nothing], axis=0).astype(jnp.bfloat16)
        coef_ref[index] = jnp.concatenate([coef, coef], axis=1)

    lax.fori_loop(0, cfg["pool"] // cfg["pool_group"], some_pool, 0)
    none_columns = lax.broadcasted_iota(jnp.int32, (lanes, depth), 1)
    feat_ref[cfg["pool"]] = jnp.where(none_columns == 6, 1.0, 0.0).astype(jnp.bfloat16)
    wide_ref[cfg["pool"]] = jnp.zeros((lanes, lanes), jnp.float32)
    coef_ref[cfg["pool"]] = jnp.zeros((32, 2 * lanes), jnp.bfloat16)

    spread = [lam - lam * lam for lam in lambdas]
    half = [0.5 - lam for lam in lambdas]

    def one_tile(tile, carry):
        own = (tile // cfg["rows_y"] + 1) * (cfg["rows_y"] + 2) + tile % cfg["rows_y"] + 1
        block, moved, norm = centred(own)
        group, site_row = block[GRP : GRP + 1, :], block[SIT : SIT + 1, :]
        lam, charge, strength = (block[r : r + 1, :] for r in (LAM, CHG, STR))
        ratio = charge / strength

        gap = jnp.where(rows < 3, -2.0 * moved, 0.0)
        gap = jnp.where(rows == 3, -0.5 * lam, gap)
        gap = jnp.where(rows == 5, 1.0, gap)
        gap = jnp.where(rows == 6, norm + 1.5, gap)
        pair = by_group(spread, group, sub_iota)
        far = [
            jnp.where(
                (site_row == float(site)) & (group != sub_iota + float(site * NSUB)), FAR, 0.0
            )
            for site in range(NSITE)
        ]
        columns = (
            (gap, [f - 0.5 * p for f, p in zip(far, pair)]),
            (jnp.where(rows == 3, lam, 0.0), pair),
            (jnp.where(rows == 3, 1.0, 0.0), by_group(half, group, sub_iota)),
            (jnp.where(rows == 4, ratio, 0.0), [nothing] * NSITE),
        )
        for column, (table, member) in enumerate(columns):
            high, middle, low = split3(table)
            tops = [m.astype(jnp.bfloat16).astype(jnp.float32) for m in member]
            rests = [m - t for m, t in zip(member, tops)]
            rhs_ref[column] = jnp.concatenate(
                [high, middle, high, middle, low, high] + tops + rests + pad, axis=0
            ).astype(jnp.bfloat16)

        def some_partners(k, sums):
            indices = [part_of(part_ref, cfg, tile, k + u) for u in range(cfg["slots"])]
            indices = [jnp.where(index < 0, cfg["pool"], index) for index in indices]
            outs = []
            for first in range(0, len(indices), 3):
                some = indices[first : first + 3]
                out = table_dot(jnp.concatenate([feat_ref[index] for index in some], axis=0), rhs_ref)
                outs += [out[n * lanes : (n + 1) * lanes] for n in range(len(some))]
            moments, fd = sums
            for index, out in zip(indices, outs):
                tops, rests = [], []
                for i in range(lanes // ROWS):
                    here = slice(ROWS * i, ROWS * i + ROWS)
                    gap2, s, w, q = (out[here, c * lanes : (c + 1) * lanes] for c in range(4))
                    eb = wide_ref[index, here, :]
                    rs = lax.rsqrt(gap2)
                    t = rs * rs * rs
                    a = eb * t
                    b = (s * t) * (a + 0.25 * q)
                    sens = (rs * (a + q) + b) * w
                    for j in range(ROWS // 8):
                        fd = fd + sens[8 * j : 8 * j + 8, :]
                    top = b.astype(jnp.bfloat16)
                    tops.append(top)
                    rests.append((b - top.astype(jnp.float32)).astype(jnp.bfloat16))
                moments = moments + jnp.dot(
                    coef_ref[index],
                    jnp.concatenate(tops + rests, axis=0),
                    preferred_element_type=jnp.float32,
                )
            return moments, fd

        moments, fd = some_partners(0, (jnp.zeros((32, lanes), jnp.float32), nothing))
        moments = moments[0:8] + moments[8:16] + moments[16:24]
        fd = jnp.sum(fd, axis=0, keepdims=True)
        forces = moved[0:3, :] * moments[6:7, :] - moments[0:3, :]
        rs = lax.rsqrt(1.5 - 0.5 * lam)
        t = rs * rs * rs
        a, q = strength * t, ratio * charge
        itself = rs * (a + q) + lam * t * (a + 0.25 * q)
        drive = strength * (fd - 0.5 * itself)
        finish_tile(cfg, tile, (4.0 * strength) * forces, drive, block, ins, outs, sub_iota)
        return carry

    def some_tiles(k, carry):
        for u in range(4):
            one_tile(k * 4 + u, carry)
        return carry

    lax.fori_loop(0, cfg["tiles"] // 4, some_tiles, 0)


def any_forces(cfg, part_ref, pool_ref, col_ref, fcol_ref, ins, outs, sub_iota):
    tiles, lanes = cfg["tiles"], cfg["lanes"]
    chunk = 32

    def one_tile(tile, carry):
        own = (tile // cfg["rows_y"] + 1) * (cfg["rows_y"] + 2) + tile % cfg["rows_y"] + 1
        block = pool_ref[own]
        col_ref[...] = block.T
        count = jnp.int32(0)
        for k in range(cfg["slots"]):
            count += (part_of(part_ref, cfg, tile, k) >= 0).astype(jnp.int32)

        def one_chunk(c, carry):
            start = pl.multiple_of(c * chunk, chunk)
            cols = col_ref[pl.ds(start, chunk), :]
            lanes_iota = lax.broadcasted_iota(jnp.int32, (chunk, lanes), 1)
            diagonal = lanes_iota == lax.broadcasted_iota(jnp.int32, (chunk, lanes), 0) + start

            def one_partner(k, sums):
                fx, fy, fz, fd = sums
                index = part_of(part_ref, cfg, tile, k)
                other = pool_ref[index]

                def own_col(row):
                    return cols[:, row : row + 1]

                def other_row(row):
                    return other[row : row + 1, :]

                dx = wrap_image(own_col(X) - other_row(X), cfg["box_x"])
                dy = wrap_image(own_col(Y) - other_row(Y), cfg["box_y"])
                dz = own_col(Z) - other_row(Z)
                r2 = dx * dx + dy * dy + dz * dz
                same = (own_col(GRP) == other_row(GRP)) & (own_col(GRP) >= 0.0)
                site = (own_col(SIT) == other_row(SIT)) & (own_col(SIT) >= 0.0)
                drop = (site & jnp.logical_not(same)) | (diagonal & (index == own))
                lam_a, lam_b = own_col(LAM), other_row(LAM)
                s = jnp.where(same, lam_a, lam_a * lam_b)
                w = jnp.where(same, 0.5, lam_b)
                e = own_col(STR) * other_row(STR)
                q = own_col(CHG) * other_row(CHG)
                rs = lax.rsqrt(1.0 + 0.5 * (1.0 - s) + r2)
                t = rs * rs * rs
                a = e * t
                b = s * t * (a + 0.25 * q)
                sens = rs * (a + q) + b
                b = jnp.where(drop, 0.0, b)
                sens = jnp.where(drop, 0.0, sens * w)
                return fx + b * dx, fy + b * dy, fz + b * dz, fd + sens

            zero = jnp.zeros((chunk, lanes), jnp.float32)
            sums = lax.fori_loop(0, count, one_partner, (zero, zero, zero, zero))
            for row, value in enumerate(sums):
                fcol_ref[pl.ds(start, chunk), row : row + 1] = jnp.sum(
                    value, axis=1, keepdims=True
                )
            return carry

        lax.fori_loop(0, lanes // chunk, one_chunk, 0)
        forces = fcol_ref[...].T
        finish_tile(
            cfg, tile, 4.0 * forces[0:3, :], forces[3:4, :], block,
            ins, outs, sub_iota,
        )
        return carry

    lax.fori_loop(0, tiles, one_tile, 0)


def finish_tile(cfg, tile, forces, drive, block, ins, outs, sub_iota):
    _, sum_ref = outs
    damping = math.exp(-friction_rate * step_size)
    rows = ins[tile]
    inverse = rows[3:4, :]
    speeds = (
        damping * rows[0:3, :]
        + step_size * forces * inverse
        + jnp.sqrt((1.0 - damping**2) * inverse) * rows[4:7, :]
    )
    ins[tile, 0:3, :] = block[0:3, :] + step_size * speeds
    ins[tile, 4:7, :] = speeds
    group = block[GRP : GRP + 1, :]
    for site in range(NSITE):
        sum_ref[site] += jnp.where(group == sub_iota + float(site * NSUB), drive, 0.0)


def pack_sums(cfg, sum_ref):
    lanes = cfg["lanes"]
    share = lanes // NSITE
    lane_site = lax.broadcasted_iota(jnp.int32, (NSUB, lanes), 1) // share
    packed = jnp.zeros((NSUB, lanes), jnp.float32)
    for site in range(NSITE):
        folded = sum_ref[site]
        width = lanes
        while width > share:
            width //= 2
            folded = folded + pltpu.roll(folded, width, 1)
        packed = packed + jnp.where(lane_site == site, folded, 0.0)
    return packed


def step_call(cfg, moment, parts, anoise, blocks, stat, totals, vel, noise, inverse, ang, start):
    tiles, lanes, pool = cfg["tiles"], cfg["lanes"], cfg["pool"]
    rows_x, rows_y = cfg["rows_x"], cfg["rows_y"]
    last = moment == STEPS - 1
    vmem = pl.BlockSpec(memory_space=pltpu.VMEM)
    noise_spec = pl.BlockSpec(
        (1, 1, rows_x, 3, rows_y, lanes), lambda i: (0, moment, 0, 0, 0, 0)
    )
    args = [(parts, pl.BlockSpec(memory_space=pltpu.HBM)), (anoise, vmem)] + [(block, vmem) for block in blocks]
    if moment > 0:
        args.append((stat, vmem))
    if totals is not None:
        args.append((totals, vmem))
    args += [(vel, vmem), (noise, noise_spec), (inverse, vmem)]
    args.append((ang, vmem))
    if last:
        args.append((start, vmem))
    vectors = (rows_x, 3, rows_y, lanes)
    if last:
        shapes = [vectors]
    else:
        held = [(len(rows), len(cols)) for rows, cols in cfg["windows"]]
        shapes = [(nr, components((nr, nc)), nc, lanes) for nr, nc in held]
    shapes.append(vectors)
    shapes.append((2, NSITE, NSUB, lanes))
    if moment == 0:
        shapes.append((pool, 4, lanes))
    if last:
        shapes.append((NSUB, lanes))
    depth = cfg["depth"]
    return pl.pallas_call(
        functools.partial(step_kernel, cfg, moment),
        grid=(1,),
        out_shape=tuple(jax.ShapeDtypeStruct(shape, jnp.float32) for shape in shapes),
        in_specs=[spec for _, spec in args],
        out_specs=(vmem,) * len(shapes),
        scratch_shapes=[
            pltpu.VMEM((pool, 8, lanes), jnp.float32),
            pltpu.VMEM((lanes, 8), jnp.float32),
            pltpu.VMEM((lanes, 8), jnp.float32),
            pltpu.VMEM((NSITE, NSUB, lanes), jnp.float32),
            pltpu.VMEM((pool + 1, lanes, depth), jnp.bfloat16),
            pltpu.VMEM((pool + 1, lanes, lanes), jnp.float32),
            pltpu.VMEM((4, depth, lanes), jnp.bfloat16),
            pltpu.VMEM((pool + 1, 32, 2 * lanes), jnp.bfloat16),
            pltpu.SMEM((2, pool), jnp.float32),
            pltpu.VMEM((tiles, 8, lanes), jnp.float32),
            pltpu.SMEM(parts.shape, jnp.int32),
            pltpu.SemaphoreType.DMA(()),
        ],
        compiler_params=pltpu.CompilerParams(vmem_limit_bytes=4 * SMALL),
        name="langevin_step",
    )(*[value for value, _ in args])


def angle_kernel(cfg, *refs):
    anoise_ref, ang_ref, disp_ref, vel_ref = refs[:4]
    *tot_refs, theta_ref, speed_ref, dispo_ref, velo_ref, sems = refs[4:]
    lanes = cfg["lanes"]
    copies = [
        pltpu.make_async_copy(disp_ref, dispo_ref, sems.at[0]),
        pltpu.make_async_copy(vel_ref, velo_ref, sems.at[1]),
    ]
    for copy in copies:
        copy.start()
    sub_iota = lax.broadcasted_iota(jnp.int32, (NSUB, lanes), 0).astype(jnp.float32)
    packed = packed_totals([ref[...] for ref in tot_refs])
    results = angle_step(
        ang_ref[0], ang_ref[1], packed, noise_table(anoise_ref, STEPS - 1, sub_iota),
        cfg["angle_mass"],
    )
    hit = lax.broadcasted_iota(jnp.int32, (NSUB, lanes), 1) == lax.broadcasted_iota(
        jnp.int32, (NSUB, lanes), 0
    )
    for ref, result in zip((theta_ref, speed_ref), results):
        for site in range(NSITE):
            row = jnp.sum(jnp.where(hit, result[site], 0.0), axis=0, keepdims=True)
            ref[0, site : site + 1, :] = row[:, 0:NSUB]
    for copy in copies:
        copy.wait()


def angle_call(cfg, anoise, ang, disp, vel, totals):
    vmem = pl.BlockSpec(memory_space=pltpu.VMEM)
    hbm = pl.BlockSpec(memory_space=pltpu.HBM)
    shape = jax.ShapeDtypeStruct((1, NSITE, NSUB), jnp.float32)
    vectors = jax.ShapeDtypeStruct(disp.shape, jnp.float32)
    return pl.pallas_call(
        functools.partial(angle_kernel, cfg),
        out_shape=(shape, shape, vectors, vectors),
        in_specs=[vmem] * (4 + len(totals)),
        out_specs=(vmem, vmem, hbm, hbm),
        scratch_shapes=[pltpu.SemaphoreType.DMA((2,))],
        name="last_angles",
        compiler_params=pltpu.CompilerParams(vmem_limit_bytes=SMALL),
    )(anoise, ang, disp, vel, *totals)


def send_kernel(width, sets, slot_ref, mine_ref, other_ref, *out_refs):
    me = lax.axis_index("walker")
    for k, ref in enumerate(out_refs, 1):
        wanted = slot_of(slot_ref, lax.rem(me + k * width, width * sets))
        own = lax.rem(wanted, width) == lax.rem(me, width)

        @pl.when(own)
        def _():
            ref[...] = mine_ref[...]

        @pl.when(jnp.logical_not(own))
        def _():
            ref[...] = other_ref[...]


def pick_kernel(width, sets, windows, slot_ref, *refs):
    block_refs = refs[: sets + 1]
    charge_ref, strength_ref, site_ref, sub_ref = refs[sets + 1 : sets + 5]
    *pay_refs, vel_ref, ang_ref = refs[sets + 5 :]
    rows_x = vel_ref.shape[0]
    me = lax.axis_index("walker")
    source = slot_of(slot_ref, me)
    hop = lax.rem(me // width - source // width + sets, sets)
    away = (lax.rem(source, width) != lax.rem(me, width)).astype(jnp.int32)
    choice = jnp.where(hop > 0, hop + 1, away)
    own_ref = pay_refs[0]
    for k, ref in enumerate(block_refs):

        @pl.when(choice == k)
        def _():
            for i in range(rows_x):
                own_ref[i, 0:3] = ref[6 * i : 6 * i + 3]
                vel_ref[i] = ref[6 * i + 3 : 6 * i + 6]
            ang_ref[...] = ref[6 * rows_x]

    site, sub = site_ref[...], sub_ref[...]
    grouped = site < NSITE
    own_ref[:, 3] = charge_ref[...]
    own_ref[:, 4] = strength_ref[...]
    own_ref[:, 5] = jnp.where(grouped, site * NSUB + sub, -1).astype(jnp.float32)
    own_ref[:, 6] = jnp.where(grouped, site, -1).astype(jnp.float32)
    for (rows, cols), ref in zip(windows[1:], pay_refs[1:]):
        for ri, i in enumerate(rows):
            for cj, j in enumerate(cols):
                ref[ri, :, cj : cj + 1, :] = own_ref[i, :, j : j + 1, :]


def pack_kernel(pos_ref, vel_ref, theta_ref, speed_ref, out_ref, angle_ref, sems):
    rows_x = pos_ref.shape[0]
    copies = [
        pltpu.make_async_copy(theta_ref.at[0], angle_ref.at[0], sems.at[0]),
        pltpu.make_async_copy(speed_ref.at[0], angle_ref.at[1], sems.at[1]),
    ]
    for i in range(rows_x):
        for kind, ref in enumerate((pos_ref, vel_ref)):
            copies.append(
                pltpu.make_async_copy(
                    ref.at[i], out_ref.at[pl.ds(6 * i + 3 * kind, 3)], sems.at[2 + 2 * i + kind]
                )
            )
    for copy in copies:
        copy.start()
    out_ref[6 * rows_x] = jnp.zeros(out_ref.shape[1:], jnp.float32)
    for copy in copies:
        copy.wait()
    for kind in range(2):
        out_ref[6 * rows_x, :, kind * NSUB : (kind + 1) * NSUB] = angle_ref[kind]


def slot_of(slot_ref, index):
    slots = slot_ref[...].astype(jnp.float32)
    lane = lax.broadcasted_iota(jnp.int32, slots.shape, 1)
    return jnp.sum(jnp.where(lane == index, slots, 0.0)).astype(jnp.int32)


def clone(cfg, positions, velocities, theta, speed, source_slot, charges, strengths, atom_site, atom_sub):
    peers = lax.axis_size("walker")
    width = 2 if peers % 2 == 0 else 1
    sets = peers // width
    rows_x, rows_y, lanes = charges.shape
    vmem = pl.BlockSpec(memory_space=pltpu.VMEM)
    message = pl.pallas_call(
        pack_kernel,
        out_shape=jax.ShapeDtypeStruct((6 * rows_x + 1, rows_y, lanes), jnp.float32),
        in_specs=[pl.BlockSpec(memory_space=pltpu.HBM)] * 4,
        out_specs=vmem,
        scratch_shapes=[
            pltpu.VMEM((2, NSITE, NSUB), jnp.float32),
            pltpu.SemaphoreType.DMA((2 + 2 * rows_x,)),
        ],
        name="pack_walker",
        compiler_params=pltpu.CompilerParams(vmem_limit_bytes=SMALL),
    )(positions, velocities, theta, speed)
    source_slot = source_slot.reshape(1, peers)
    other = message
    if width == 2:
        other = lax.ppermute(message, "walker", [(w, w ^ 1) for w in range(peers)])
    blocks = [message, other]
    if sets > 1:
        shape = jax.ShapeDtypeStruct(message.shape, jnp.float32)
        sent = pl.pallas_call(
            functools.partial(send_kernel, width, sets),
            out_shape=(shape,) * (sets - 1),
            in_specs=[vmem, vmem, vmem],
            out_specs=(vmem,) * (sets - 1),
            name="choose_sent",
        compiler_params=pltpu.CompilerParams(vmem_limit_bytes=SMALL),
        )(source_slot, message, other)
        for k, value in enumerate(sent, 1):
            blocks.append(
                lax.ppermute(
                    value, "walker", [(w, (w + k * width) % peers) for w in range(peers)]
                )
            )
    shapes = [(len(rows), 7, len(cols), lanes) for rows, cols in cfg["windows"]]
    shapes += [(rows_x, 3, rows_y, lanes), (rows_y, lanes)]
    return pl.pallas_call(
        functools.partial(pick_kernel, width, sets, cfg["windows"]),
        out_shape=tuple(jax.ShapeDtypeStruct(shape, jnp.float32) for shape in shapes),
        in_specs=[vmem] * (len(blocks) + 5),
        out_specs=(vmem,) * len(shapes),
        name="choose_received",
        compiler_params=pltpu.CompilerParams(vmem_limit_bytes=SMALL),
    )(source_slot, *blocks, charges, strengths, atom_site, atom_sub)


def make_cfg(rows_x, rows_y, lanes, count_x, count_y, slots, offsets):
    tiles = rows_x * rows_y
    return dict(
        blocks=1 + len(offsets),
        covered=1 + len(offsets) == count_x * count_y,
        tiles=tiles,
        lanes=lanes,
        rows_x=rows_x,
        rows_y=rows_y,
        count_x=count_x,
        count_y=count_y,
        slots=slots,
        pool=(rows_x + 2) * (rows_y + 2),
        windows=[window(offset, rows_x, rows_y) for offset in [(0, 0)] + offsets],
        sources=pool_sources(rows_x, rows_y, count_x, count_y, offsets),
        depth=128,
        pool_group=next(g for g in (36, 6, 4, 3, 2, 1) if (rows_x + 2) * (rows_y + 2) % g == 0),
        roomy=min(rows_x * count_x, rows_y * count_y) >= 8,
        box_x=float(rows_x * count_x),
        box_y=float(rows_y * count_y),
        angle_mass=rows_x * count_x * rows_y * count_y * lanes * theta_share,
    )


def per_device(
    positions,
    velocities,
    lambda_theta,
    theta_velocity,
    source_slot,
    atom_noise,
    theta_noise,
    charges,
    strengths,
    inverse_mass,
    atom_site,
    atom_sub,
    partners,
):
    count_x, count_y = lax.axis_size("gx"), lax.axis_size("gy")
    rows_x, rows_y, lanes = charges.shape
    tiles = rows_x * rows_y
    offsets = neighbour_offsets(count_x, count_y)
    cfg = make_cfg(rows_x, rows_y, lanes, count_x, count_y, partners.shape[-1], offsets)

    def gather_blocks(values):
        return [values[0]] + [
            shifted(value, offset, count_x, count_y) for value, offset in zip(values[1:], offsets)
        ]

    *pays, vel, ang = clone(
        cfg, positions[0].transpose(0, 2, 1, 3), velocities[0].transpose(0, 2, 1, 3),
        lambda_theta, theta_velocity, source_slot, charges, strengths, atom_site, atom_sub,
    )
    noise = atom_noise.transpose(0, 1, 2, 4, 3, 5)
    first = pays[0]
    pool_stat = None
    for moment in range(STEPS):
        totals = None
        if moment > 0 and not cfg["covered"]:
            totals = lax.psum(pays[0][:, 3].reshape(tiles, lanes)[:NSUB], ("gx", "gy"))
        outs = step_call(
            cfg, moment, partners, theta_noise, gather_blocks(pays), pool_stat, totals, vel,
            noise, inverse_mass, ang, first,
        )
        own = cfg["blocks"] if moment < STEPS - 1 else 1
        pays, (vel, ang, *rest) = outs[:own], outs[own:]
        if moment == 0:
            pool_stat = rest[0]
    packed = rest[0]
    if cfg["covered"]:
        totals = gather_blocks([packed] * cfg["blocks"])
    else:
        totals = [lax.psum(packed, ("gx", "gy"))]
    theta, theta_speed, disp, vel = angle_call(cfg, theta_noise, ang, pays[0], vel, totals)
    back = lambda value: value.transpose(0, 2, 1, 3)[None]
    return back(disp), back(vel), theta, theta_speed


def solution(mesh):
    in_specs = (
        P("walker", "gx", "gy", None, None),
        P("walker", "gx", "gy", None, None),
        P("walker", None, None),
        P("walker", None, None),
        P(),
        P("walker", None, "gx", "gy", None, None),
        P("walker", None, None, None),
        P("gx", "gy", None),
        P("gx", "gy", None),
        P("gx", "gy", None),
        P("gx", "gy", None),
        P("gx", "gy", None),
        P("gx", "gy", None),
    )
    out_specs = (
        P("walker", "gx", "gy", None, None),
        P("walker", "gx", "gy", None, None),
        P("walker", None, None),
        P("walker", None, None),
    )
    return jax.shard_map(
        per_device, mesh=mesh, in_specs=in_specs, out_specs=out_specs, check_vma=False
    )
```

```python
import functools
import math

import jax
import jax.numpy as jnp
from jax import lax
from jax.experimental import pallas as pl
from jax.experimental.pallas import tpu as pltpu
from jax.sharding import PartitionSpec as P

NSITE = 4
NSUB = 8
STEPS = 4

step_size = 0.02
friction_rate = 1.0
theta_friction = 20.0
soft_alpha = 0.5
soft_beta = 0.5
theta_share = 1.0 / 1024.0

MIDDLE_Z = 1.0
REACH = 1.49
FAR = 2.0**126
GROUP = 2
AHEAD = 2
SMALL = 4 * 2**20
ROWS = 16

X, Y, Z, LAM, CHG, STR, GRP, SIT = range(8)


def wrap_image(offset, length):
    shift = jnp.where(offset > 0.5 * length, length, 0.0)
    shift = jnp.where(offset < -0.5 * length, -length, shift)
    return offset - shift


def neighbour_offsets(count_x, count_y):
    found = []
    for di in (-1, 0, 1):
        for dj in (-1, 0, 1):
            key = (di % count_x, dj % count_y)
            if key != (0, 0) and key not in found:
                found.append(key)
    return found


def shifted(value, offset, count_x, count_y):
    pairs = []
    for i in range(count_x):
        for j in range(count_y):
            source = ((i + offset[0]) % count_x) * count_y + (j + offset[1]) % count_y
            pairs.append((source, i * count_y + j))
    return lax.ppermute(value, ("gx", "gy"), pairs)


def window(offset, rows_x, rows_y):
    def part(step, rows):
        return tuple(range(rows)) if step == 0 or rows <= 2 else (0, rows - 1)

    return part(offset[0], rows_x), part(offset[1], rows_y)


def sum_rows(shape):
    nr, nc = shape
    places = []
    for row in range(NSUB):
        extra, at = row // (nr * nc), row % (nr * nc)
        places.append((at // nc, 3 + extra, at % nc))
    return places


def components(shape):
    return 3 + -(-NSUB // (shape[0] * shape[1]))


def pool_sources(rows_x, rows_y, count_x, count_y, offsets):
    sources = []
    for pi in range(rows_x + 2):
        for pj in range(rows_y + 2):
            di = -1 if pi == 0 else (1 if pi == rows_x + 1 else 0)
            dj = -1 if pj == 0 else (1 if pj == rows_y + 1 else 0)
            key = (di % count_x, dj % count_y)
            block = 0 if key == (0, 0) else 1 + offsets.index(key)
            rows, cols = window(key, rows_x, rows_y)
            place = rows.index((pi - 1) % rows_x), cols.index((pj - 1) % rows_y)
            sources.append((block, place))
    return sources


def softmax_angles(angles):
    weights = jnp.exp(angles)
    return weights / jnp.sum(weights, axis=1, keepdims=True)


def angle_step(angles, speeds, packed, noise, angle_mass):
    lanes = packed.shape[1]
    share = lanes // NSITE
    lane_site = lax.broadcasted_iota(jnp.int32, packed.shape, 1) // share
    lambdas = softmax_angles(angles)
    totals = jnp.stack(
        [
            jnp.broadcast_to(
                jnp.sum(jnp.where(lane_site == site, packed, 0.0), axis=1, keepdims=True),
                packed.shape,
            )
            for site in range(NSITE)
        ]
    )
    angle_damping = math.exp(-theta_friction * step_size)
    force = -lambdas * (totals - jnp.sum(lambdas * totals, axis=1, keepdims=True))
    speeds = (
        angle_damping * speeds
        + step_size * force / angle_mass
        + math.sqrt((1.0 - angle_damping**2) / angle_mass) * noise
    )
    return angles + step_size * speeds, speeds


def lane_column(row, first, sub_iota):
    shape = (sub_iota.shape[0], row.shape[1])
    hit = lax.broadcasted_iota(jnp.int32, shape, 1) == (
        lax.broadcasted_iota(jnp.int32, shape, 0) + first
    )
    return jnp.broadcast_to(
        jnp.sum(jnp.where(hit, row, 0.0), axis=1, keepdims=True), sub_iota.shape
    )


def block_rows(ref, place, first, last):
    i, j = place
    return jnp.concatenate([ref[i, row, j : j + 1, :] for row in range(first, last)], axis=0)


def noise_table(anoise_ref, moment, sub_iota):
    return jnp.stack(
        [
            lane_column(anoise_ref[0, moment, site : site + 1, :], 0, sub_iota)
            for site in range(NSITE)
        ]
    )


def packed_rows(ref):
    places = sum_rows((ref.shape[0], ref.shape[2]))
    return jnp.concatenate([ref[i, c, j : j + 1, :] for i, c, j in places], axis=0)


def packed_totals(blocks):
    packed = blocks[0]
    for block in blocks[1:]:
        packed = packed + block
    return packed


def step_kernel(cfg, moment, *refs):
    nb = cfg["blocks"]
    lanes = cfg["lanes"]
    refs = list(refs)

    def take(n):
        taken, refs[:n] = refs[:n], []
        return taken

    part_hbm, anoise_ref = take(2)
    coord_refs = take(nb)
    (stat_ref,) = take(1) if moment > 0 else (None,)
    (tot_ref,) = take(1) if moment > 0 and not cfg["covered"] else (None,)
    vel_ref, noise_ref, inv_ref = take(3)
    (ang_ref,) = take(1)
    last = moment == STEPS - 1
    (start_ref,) = take(1) if last else (None,)
    out_refs = take(1 if last else nb)
    velo_ref, ango_ref = take(2)
    (stato_ref,) = take(1) if moment == 0 else (None,)
    (sumo_ref,) = take(1) if last else (None,)
    pool_ref, col_ref, fcol_ref, sum_ref, feat_ref, wide_ref, rhs_ref, coef_ref, off_ref, io_ref, tall_ref, begin_ref, weight_ref = take(13)
    part_ref, part_sem = take(2)
    part_copy = pltpu.make_async_copy(part_hbm, part_ref, part_sem)
    part_copy.start()

    sub_iota = lax.broadcasted_iota(jnp.int32, (NSUB, lanes), 0).astype(jnp.float32)
    if moment == 0:
        angles, aspeeds = (
            jnp.stack(
                [
                    lane_column(ang_ref[site : site + 1, :], kind * NSUB, sub_iota)
                    for site in range(NSITE)
                ]
            )
            for kind in range(2)
        )
    else:
        angles, aspeeds = ang_ref[0], ang_ref[1]
        if cfg["covered"]:
            packed = packed_totals([packed_rows(ref) for ref in coord_refs])
        else:
            packed = tot_ref[...]
        angles, aspeeds = angle_step(
            angles, aspeeds, packed, noise_table(anoise_ref, moment - 1, sub_iota),
            cfg["angle_mass"],
        )
    ango_ref[0] = angles
    ango_ref[1] = aspeeds
    lambdas = softmax_angles(angles)

    def line(axis, rows, count):
        at = lax.axis_index(axis)
        middle = at.astype(jnp.float32) * rows + 0.5 * rows
        shifts, cells = [], []
        for ring in range(rows + 2):
            turn = 0.0
            if ring == 0:
                turn = jnp.where(at == 0, -float(rows * count), 0.0)
            if ring == rows + 1:
                turn = jnp.where(at == count - 1, float(rows * count), 0.0)
            shifts.append(turn - middle)
            cells.append(turn - middle - (ring - 0.5 - 0.5 * rows))
        return shifts, cells

    shift_x, cell_x = line("gx", cfg["rows_x"], cfg["count_x"])
    shift_y, cell_y = line("gy", cfg["rows_y"], cfg["count_y"])
    worst = jnp.zeros((3, lanes), jnp.float32)
    row3 = lax.broadcasted_iota(jnp.int32, (3, lanes), 0)
    for index, (block, tile) in enumerate(cfg["sources"]):
        pi, pj = index // (cfg["rows_y"] + 2), index % (cfg["rows_y"] + 2)
        off_ref[0, index] = shift_x[pi]
        off_ref[1, index] = shift_y[pj]
        if moment == 0:
            stat = block_rows(coord_refs[block], tile, 3, 7)
            stato_ref[index] = stat
        else:
            stat = stat_ref[index]
        cell = jnp.where(row3 == 0, cell_x[pi], cell_y[pj])
        cell = jnp.where(row3 == 2, -MIDDLE_Z, cell)
        coords = block_rows(coord_refs[block], tile, 0, 3)
        worst = jnp.maximum(worst, jnp.abs(coords + cell))
        pool_ref[index, 0:3, :] = coords
        pool_ref[index, 4:8, :] = stat
        group = stat[2:3, :]
        lam = jnp.zeros((NSUB, lanes), jnp.float32)
        for site in range(NSITE):
            lam = lam + jnp.where(group == sub_iota + float(site * NSUB), lambdas[site], 0.0)
        lam = jnp.sum(lam, axis=0, keepdims=True)
        pool_ref[index, 3:4, :] = jnp.where(group >= 0.0, lam, 1.0)

    stray = jnp.max(worst * jnp.where(row3 == 2, 0.5, 1.0))
    for tile in range(cfg["tiles"]):
        i, j = tile // cfg["rows_y"], tile % cfg["rows_y"]
        for row in range(3):
            io_ref[tile, row : row + 1, :] = vel_ref[i, row, j : j + 1, :]
            io_ref[tile, 4 + row : 5 + row, :] = noise_ref[0, 0, i, row, j : j + 1, :]
        io_ref[tile, 3:4, :] = inv_ref[i, j : j + 1, :]

    sum_ref[...] = jnp.zeros_like(sum_ref)
    fcol_ref[...] = jnp.zeros_like(fcol_ref)
    ins = io_ref
    outs = (io_ref, sum_ref)
    near = cfg["roomy"] & (stray < REACH)

    part_copy.wait()

    @pl.when(near)
    def _():
        near_forces(
            cfg, lambdas, part_ref, off_ref, pool_ref, feat_ref, wide_ref, rhs_ref,
            coef_ref, tall_ref, begin_ref, weight_ref, ins, outs, sub_iota,
        )

    @pl.when(jnp.logical_not(near))
    def _():
        any_forces(cfg, part_ref, pool_ref, col_ref, fcol_ref, ins, outs, sub_iota)

    packed = pack_sums(cfg, sum_ref)
    for tile in range(cfg["tiles"]):
        i, j = tile // cfg["rows_y"], tile % cfg["rows_y"]
        here = slice(j, j + 1)
        for row in range(3):
            velo_ref[i, row, here, :] = io_ref[tile, 4 + row : 5 + row, :]
    for (rows, cols), ref in zip(cfg["windows"], out_refs):
        for ri, i in enumerate(rows):
            for cj, j in enumerate(cols):
                for row in range(3):
                    coord = io_ref[i * cfg["rows_y"] + j, row : row + 1, :]
                    if last:
                        coord = coord - start_ref[i, row, j : j + 1, :]
                    ref[ri, row, cj : cj + 1, :] = coord
        if not last:
            for row, (i, c, j) in enumerate(sum_rows((len(rows), len(cols)))):
                ref[i, c, j : j + 1, :] = packed[row : row + 1, :]
    if last:
        sumo_ref[...] = packed


def part_of(part_ref, cfg, tile, k):
    return part_ref[tile // cfg["rows_y"], tile % cfg["rows_y"], k]


def split3(value):
    high = value.astype(jnp.bfloat16).astype(jnp.float32)
    rest = value - high
    middle = rest.astype(jnp.bfloat16).astype(jnp.float32)
    return high, middle, rest - middle


def by_group(lambdas_of_site, group, sub_iota):
    return [
        jnp.where(group == sub_iota + float(site * NSUB), lambdas_of_site[site], 0.0)
        for site in range(NSITE)
    ]


def near_forces(
    cfg, lambdas, part_ref, off_ref, pool_ref, feat_ref, wide_ref, rhs_ref,
    coef_ref, tall_ref, begin_ref, weight_ref, ins, outs, sub_iota,
):
    lanes = cfg["lanes"]
    depth = cfg["depth"]
    rows = lax.broadcasted_iota(jnp.int32, (8, lanes), 0)
    ones = jnp.ones((NSUB, lanes), jnp.float32)
    nothing = jnp.zeros((8, lanes), jnp.float32)
    pad = [nothing] * ((depth - 6 * 8 - 2 * NSITE * NSUB) // 8)

    pick_rows = lax.broadcasted_iota(jnp.int32, (depth, lanes), 0)
    hit = (pick_rows == 7) | (pick_rows == 16 + 7) | (pick_rows == 40 + 7)
    pick = jnp.where(hit, 1.0, 0.0).astype(jnp.bfloat16)

    def centred(index):
        block = pool_ref[index]
        shift = jnp.where(rows == 0, off_ref[0, index], 0.0)
        shift = jnp.where(rows == 1, off_ref[1, index], shift)
        shift = jnp.where(rows == 2, -MIDDLE_Z, shift)
        moved = block + shift
        square = jnp.where(rows < 3, moved * moved, 0.0)
        return block, moved, jnp.sum(square, axis=0, keepdims=True)

    def table_dot(features, ref):
        table = jnp.concatenate([ref[c] for c in range(ref.shape[0])], axis=1)
        return jnp.dot(features, table, preferred_element_type=jnp.float32)

    def some_pool(k, carry):
        for u in range(cfg["pool_group"]):
            one_pool(k * cfg["pool_group"] + u)
        return carry

    def one_pool(index):
        block, moved, norm = centred(index)
        table = jnp.where(rows == 5, norm, moved)
        table = jnp.where(rows == 6, 1.0, table)
        table = jnp.where(rows == 7, block[STR : STR + 1, :], table)
        high, middle, low = split3(table)
        member = by_group([ones] * NSITE, block[GRP : GRP + 1, :], sub_iota)
        features = jnp.concatenate(
            [high, high, middle, middle, high, low] + member + member + pad, axis=0
        )
        features = features.T.astype(jnp.bfloat16)
        feat_ref[index] = features
        wide_ref[index] = jnp.dot(features, pick, preferred_element_type=jnp.float32)
        coef = jnp.concatenate([high, middle, low, nothing], axis=0).astype(jnp.bfloat16)
        coef = jnp.concatenate([coef] + [m.astype(jnp.bfloat16) for m in member], axis=0)
        coef_ref[index] = jnp.concatenate([coef, coef], axis=1)

    lax.fori_loop(0, cfg["pool"] // cfg["pool_group"], some_pool, 0)
    none_columns = lax.broadcasted_iota(jnp.int32, (lanes, depth), 1)
    feat_ref[cfg["pool"]] = jnp.where(none_columns == 6, 1.0, 0.0).astype(jnp.bfloat16)
    wide_ref[cfg["pool"]] = jnp.zeros((lanes, lanes), jnp.float32)
    coef_ref[cfg["pool"]] = jnp.zeros((64, 2 * lanes), jnp.bfloat16)

    spread = [lam - lam * lam for lam in lambdas]
    half = [0.5 - lam for lam in lambdas]
    rows_x, rows_y = cfg["rows_x"], cfg["rows_y"]
    _, sum_ref = outs
    tall_ref[...] = jnp.zeros_like(tall_ref)
    begin_ref[...] = jnp.zeros_like(begin_ref)

    def own_tile(i, j):
        return (i + 1) * (rows_y + 2) + j + 1

    def own_table(i, j):
        block, moved, norm = centred(own_tile(i, j))
        group, site_row = block[GRP : GRP + 1, :], block[SIT : SIT + 1, :]
        lam, charge, strength = (block[r : r + 1, :] for r in (LAM, CHG, STR))
        gap = jnp.where(rows < 3, -2.0 * moved, 0.0)
        gap = jnp.where(rows == 3, -0.5 * lam, gap)
        gap = jnp.where(rows == 5, 1.0, gap)
        gap = jnp.where(rows == 6, norm + 1.5, gap)
        pair = by_group(spread, group, sub_iota)
        far = [
            jnp.where(
                (site_row == float(site)) & (group != sub_iota + float(site * NSUB)), FAR, 0.0
            )
            for site in range(NSITE)
        ]
        columns = (
            (gap, [f - 0.5 * p for f, p in zip(far, pair)]),
            (jnp.where(rows == 3, lam, 0.0), pair),
            (jnp.where(rows == 4, charge / strength, 0.0), [nothing] * NSITE),
        )
        for column, (table, member) in enumerate(columns):
            high, middle, low = split3(table)
            tops = [m.astype(jnp.bfloat16).astype(jnp.float32) for m in member]
            rests = [m - t for m, t in zip(member, tops)]
            rhs_ref[i * rows_y + j, column] = jnp.concatenate(
                [high, middle, high, middle, low, high] + tops + rests + pad, axis=0
            ).astype(jnp.bfloat16)
        weight = jnp.where(rows < 3, moved * strength, jnp.where(rows == 6, strength, 0.0))
        weight = jnp.concatenate([*split3(weight), nothing], axis=0).astype(jnp.bfloat16)
        weight_ref[i * rows_y + j] = jnp.concatenate([weight, weight], axis=1)

    for i in range(rows_x):
        for j in range(rows_y):
            own_table(i, j)

    def three(value):
        return value[0:8] + value[8:16] + value[16:24]

    def tables(i, j, steps):
        own = own_tile(i, j)
        indices = []
        for di, dj in steps:
            index = own + di * (rows_y + 2) + dj
            listed = part_ref[i, j, (di + 1) * 3 + dj + 1] > 0
            indices.append(jnp.where(listed, index, cfg["pool"]))
        out = table_dot(
            jnp.concatenate([feat_ref[index] for index in indices], axis=0),
            rhs_ref.at[i * rows_y + j],
        )
        return indices, [out[n * lanes : (n + 1) * lanes] for n in range(len(steps))]

    def all_pairs(i, work):
        ready = [tables(i, *work[n]) for n in range(AHEAD)]
        for n, (j, steps) in enumerate(work):
            if n + AHEAD < len(work):
                ready.append(tables(i, *work[n + AHEAD]))
            indices, outs = ready[n]
            for step, values in zip(steps, some_pairs(i, j, steps, indices, outs)):
                yield j, step, values

    def groups(work):
        return [
            (j, steps[first : first + GROUP])
            for j, steps in work
            for first in range(0, len(steps), GROUP)
        ]

    def some_pairs(i, j, steps, indices, outs):
        results = []
        for out, index, step in zip(outs, indices, steps):
            pieces = [[], [], [], []]
            for r in range(lanes // ROWS):
                here = slice(ROWS * r, ROWS * r + ROWS)
                gap2, s, q = (out[here, c * lanes : (c + 1) * lanes] for c in range(3))
                eb = wide_ref[index, ROWS * r : ROWS * r + ROWS, :]
                rs = lax.rsqrt(gap2)
                t = rs * rs * rs
                a = eb * t
                b = (s * t) * (a + 0.25 * q)
                sens = rs * (a + q) + b
                for kind, value in enumerate((b, sens)):
                    top = value.astype(jnp.bfloat16)
                    pieces[2 * kind].append(top)
                    pieces[2 * kind + 1].append(
                        (value - top.astype(jnp.float32)).astype(jnp.bfloat16)
                    )
            b_top, b_rest, s_top, s_rest = (jnp.concatenate(p, axis=0) for p in pieces)
            moments = jnp.dot(
                coef_ref[index, 0:32], jnp.concatenate([b_top, b_rest], axis=0),
                preferred_element_type=jnp.float32,
            )
            drives = jnp.dot(
                coef_ref[index], jnp.concatenate([s_top, s_rest], axis=0),
                preferred_element_type=jnp.float32,
            )
            if step > (0, 0):
                back = lax.dot_general(
                    weight_ref[i * rows_y + j], jnp.concatenate([b_top, b_rest], axis=1), (((1,), (1,)), ((), ())),
                    preferred_element_type=jnp.float32,
                )
                tall_ref[index] += three(back)
            results.append((three(moments), three(drives[0:32]), drives[32:64]))
        return results

    def add(total, values):
        return [x + y for x, y in zip(total, values)]

    work = []
    for j in range(rows_y):
        steps = [
            (-1, d) for d in (-1, 0, 1) if not (j == 0 and d == -1 or j == rows_y - 1 and d == 1)
        ]
        work.append((j, steps))
    empty = [nothing, nothing, jnp.zeros((NSITE * NSUB, lanes), jnp.float32)]
    border = [empty] * rows_y
    for j, _, values in all_pairs(0, groups(work)):
        border[j] = add(border[j], values)
    for j, total in enumerate(border):
        begin_ref[j] = jnp.concatenate(total, axis=0)

    def one_row(i, carry):
        inner = jnp.where(i < rows_x - 1, 1.0, 0.0)
        work = []
        for j in range(rows_y):
            steps = [(0, 0), (0, 1), (1, -1), (1, 0), (1, 1)]
            steps += [(0, -1), (-1, -1)] if j == 0 else []
            steps += [(-1, 1)] if j == rows_y - 1 else []
            work.append((j, steps))
        zero = jnp.zeros((NSITE * NSUB, lanes), jnp.float32)
        sums = [
            [begin_ref[j, 0:8], begin_ref[j, 8:16], begin_ref[j, 16:], zero, zero]
            for j in range(rows_y)
        ]
        for j, (di, dj), (m, d, g) in all_pairs(i, groups(work)):
            if (di, dj) <= (0, 0) or not 0 <= j + dj < rows_y:
                kind = 2
            else:
                kind = 3 if di == 0 else 4
            sums[j][0] = sums[j][0] + m
            sums[j][1] = sums[j][1] + d
            sums[j][kind] = sums[j][kind] + g
        kept = []
        for j, (moments, drive, once, twice, below) in enumerate(sums):
            block, moved, _ = centred(own_tile(i, j))
            kept.append((block, moved, moments, drive, once + twice + below, twice + inner * below))
        for j, (block, moved, moments, drive, once, twice) in enumerate(kept):
            group = block[GRP : GRP + 1, :]
            lam, charge, strength = (block[r : r + 1, :] for r in (LAM, CHG, STR))
            others = tall_ref[own_tile(i, j)]
            forces = strength * (moved[0:3] * moments[6:7] - moments[0:3])
            forces = forces + (moved[0:3] * others[6:7] - others[0:3])
            rs = lax.rsqrt(1.5 - 0.5 * lam)
            t = rs * rs * rs
            a, q = strength * t, charge * charge / strength
            itself = rs * (a + q) + lam * t * (a + 0.25 * q)
            mine = by_group([ones] * NSITE, group, sub_iota)
            for site in range(NSITE):
                here = slice(site * NSUB, site * NSUB + NSUB)
                both = once[here] + twice[here]
                value = mine[site] * (drive[3:4] - 0.5 * itself + half[site] * both)
                sum_ref[site] += strength * (value + lam * twice[here])
            finish_tile(cfg, i * rows_y + j, 4.0 * forces, None, block, ins, outs, sub_iota)
        begin_ref[...] = jnp.zeros_like(begin_ref)
        return carry

    lax.fori_loop(0, rows_x, one_row, 0)


def any_forces(cfg, part_ref, pool_ref, col_ref, fcol_ref, ins, outs, sub_iota):
    tiles, lanes = cfg["tiles"], cfg["lanes"]
    chunk = 32

    def one_tile(tile, carry):
        own = (tile // cfg["rows_y"] + 1) * (cfg["rows_y"] + 2) + tile % cfg["rows_y"] + 1
        block = pool_ref[own]
        col_ref[...] = block.T

        def one_chunk(c, carry):
            start = pl.multiple_of(c * chunk, chunk)
            cols = col_ref[pl.ds(start, chunk), :]
            lanes_iota = lax.broadcasted_iota(jnp.int32, (chunk, lanes), 1)
            diagonal = lanes_iota == lax.broadcasted_iota(jnp.int32, (chunk, lanes), 0) + start

            def one_partner(k, sums):
                fx, fy, fz, fd = sums
                index = own + (k // 3 - 1) * (cfg["rows_y"] + 2) + k % 3 - 1
                listed = part_of(part_ref, cfg, tile, k) > 0
                other = pool_ref[index]

                def own_col(row):
                    return cols[:, row : row + 1]

                def other_row(row):
                    return other[row : row + 1, :]

                dx = wrap_image(own_col(X) - other_row(X), cfg["box_x"])
                dy = wrap_image(own_col(Y) - other_row(Y), cfg["box_y"])
                dz = own_col(Z) - other_row(Z)
                r2 = dx * dx + dy * dy + dz * dz
                same = (own_col(GRP) == other_row(GRP)) & (own_col(GRP) >= 0.0)
                site = (own_col(SIT) == other_row(SIT)) & (own_col(SIT) >= 0.0)
                drop = (site & jnp.logical_not(same)) | (diagonal & (index == own)) | jnp.logical_not(listed)
                lam_a, lam_b = own_col(LAM), other_row(LAM)
                s = jnp.where(same, lam_a, lam_a * lam_b)
                w = jnp.where(same, 0.5, lam_b)
                e = own_col(STR) * other_row(STR)
                q = own_col(CHG) * other_row(CHG)
                rs = lax.rsqrt(1.0 + 0.5 * (1.0 - s) + r2)
                t = rs * rs * rs
                a = e * t
                b = s * t * (a + 0.25 * q)
                sens = rs * (a + q) + b
                b = jnp.where(drop, 0.0, b)
                sens = jnp.where(drop, 0.0, sens * w)
                return fx + b * dx, fy + b * dy, fz + b * dz, fd + sens

            zero = jnp.zeros((chunk, lanes), jnp.float32)
            sums = lax.fori_loop(0, 9, one_partner, (zero, zero, zero, zero))
            for row, value in enumerate(sums):
                fcol_ref[pl.ds(start, chunk), row : row + 1] = jnp.sum(
                    value, axis=1, keepdims=True
                )
            return carry

        lax.fori_loop(0, lanes // chunk, one_chunk, 0)
        forces = fcol_ref[...].T
        finish_tile(
            cfg, tile, 4.0 * forces[0:3, :], forces[3:4, :], block,
            ins, outs, sub_iota,
        )
        return carry

    lax.fori_loop(0, tiles, one_tile, 0)


def finish_tile(cfg, tile, forces, drive, block, ins, outs, sub_iota):
    _, sum_ref = outs
    damping = math.exp(-friction_rate * step_size)
    rows = ins[tile]
    inverse = rows[3:4, :]
    speeds = (
        damping * rows[0:3, :]
        + step_size * forces * inverse
        + jnp.sqrt((1.0 - damping**2) * inverse) * rows[4:7, :]
    )
    ins[tile, 0:3, :] = block[0:3, :] + step_size * speeds
    ins[tile, 4:7, :] = speeds
    if drive is None:
        return
    group = block[GRP : GRP + 1, :]
    for site in range(NSITE):
        sum_ref[site] += jnp.where(group == sub_iota + float(site * NSUB), drive, 0.0)


def pack_sums(cfg, sum_ref):
    lanes = cfg["lanes"]
    share = lanes // NSITE
    lane_site = lax.broadcasted_iota(jnp.int32, (NSUB, lanes), 1) // share
    packed = jnp.zeros((NSUB, lanes), jnp.float32)
    for site in range(NSITE):
        folded = sum_ref[site]
        width = lanes
        while width > share:
            width //= 2
            folded = folded + pltpu.roll(folded, width, 1)
        packed = packed + jnp.where(lane_site == site, folded, 0.0)
    return packed


def step_call(cfg, moment, parts, anoise, blocks, stat, totals, vel, noise, inverse, ang, start):
    tiles, lanes, pool = cfg["tiles"], cfg["lanes"], cfg["pool"]
    rows_x, rows_y = cfg["rows_x"], cfg["rows_y"]
    last = moment == STEPS - 1
    vmem = pl.BlockSpec(memory_space=pltpu.VMEM)
    noise_spec = pl.BlockSpec(
        (1, 1, rows_x, 3, rows_y, lanes), lambda i: (0, moment, 0, 0, 0, 0)
    )
    args = [(parts, pl.BlockSpec(memory_space=pltpu.HBM)), (anoise, vmem)] + [(block, vmem) for block in blocks]
    if moment > 0:
        args.append((stat, vmem))
    if totals is not None:
        args.append((totals, vmem))
    args += [(vel, vmem), (noise, noise_spec), (inverse, vmem)]
    args.append((ang, vmem))
    if last:
        args.append((start, vmem))
    vectors = (rows_x, 3, rows_y, lanes)
    if last:
        shapes = [vectors]
    else:
        held = [(len(rows), len(cols)) for rows, cols in cfg["windows"]]
        shapes = [(nr, components((nr, nc)), nc, lanes) for nr, nc in held]
    shapes.append(vectors)
    shapes.append((2, NSITE, NSUB, lanes))
    if moment == 0:
        shapes.append((pool, 4, lanes))
    if last:
        shapes.append((NSUB, lanes))
    depth = cfg["depth"]
    return pl.pallas_call(
        functools.partial(step_kernel, cfg, moment),
        grid=(1,),
        out_shape=tuple(jax.ShapeDtypeStruct(shape, jnp.float32) for shape in shapes),
        in_specs=[spec for _, spec in args],
        out_specs=(vmem,) * len(shapes),
        scratch_shapes=[
            pltpu.VMEM((pool, 8, lanes), jnp.float32),
            pltpu.VMEM((lanes, 8), jnp.float32),
            pltpu.VMEM((lanes, 8), jnp.float32),
            pltpu.VMEM((NSITE, NSUB, lanes), jnp.float32),
            pltpu.VMEM((pool + 1, lanes, depth), jnp.bfloat16),
            pltpu.VMEM((pool + 1, lanes, lanes), jnp.float32),
            pltpu.VMEM((tiles, 3, depth, lanes), jnp.bfloat16),
            pltpu.VMEM((pool + 1, 64, 2 * lanes), jnp.bfloat16),
            pltpu.SMEM((2, pool), jnp.float32),
            pltpu.VMEM((tiles, 8, lanes), jnp.float32),
            pltpu.VMEM((pool + 1, 8, lanes), jnp.float32),
            pltpu.VMEM((rows_y, 16 + NSITE * NSUB, lanes), jnp.float32),
            pltpu.VMEM((tiles, 32, 2 * lanes), jnp.bfloat16),
            pltpu.SMEM(parts.shape, jnp.int32),
            pltpu.SemaphoreType.DMA(()),
        ],
        compiler_params=pltpu.CompilerParams(vmem_limit_bytes=4 * SMALL),
        name="langevin_step",
    )(*[value for value, _ in args])


def angle_kernel(cfg, *refs):
    anoise_ref, ang_ref, disp_ref, vel_ref = refs[:4]
    *tot_refs, theta_ref, speed_ref, dispo_ref, velo_ref, sems = refs[4:]
    lanes = cfg["lanes"]
    copies = [
        pltpu.make_async_copy(disp_ref, dispo_ref, sems.at[0]),
        pltpu.make_async_copy(vel_ref, velo_ref, sems.at[1]),
    ]
    for copy in copies:
        copy.start()
    sub_iota = lax.broadcasted_iota(jnp.int32, (NSUB, lanes), 0).astype(jnp.float32)
    packed = packed_totals([ref[...] for ref in tot_refs])
    results = angle_step(
        ang_ref[0], ang_ref[1], packed, noise_table(anoise_ref, STEPS - 1, sub_iota),
        cfg["angle_mass"],
    )
    hit = lax.broadcasted_iota(jnp.int32, (NSUB, lanes), 1) == lax.broadcasted_iota(
        jnp.int32, (NSUB, lanes), 0
    )
    for ref, result in zip((theta_ref, speed_ref), results):
        for site in range(NSITE):
            row = jnp.sum(jnp.where(hit, result[site], 0.0), axis=0, keepdims=True)
            ref[0, site : site + 1, :] = row[:, 0:NSUB]
    for copy in copies:
        copy.wait()


def angle_call(cfg, anoise, ang, disp, vel, totals):
    vmem = pl.BlockSpec(memory_space=pltpu.VMEM)
    hbm = pl.BlockSpec(memory_space=pltpu.HBM)
    shape = jax.ShapeDtypeStruct((1, NSITE, NSUB), jnp.float32)
    vectors = jax.ShapeDtypeStruct(disp.shape, jnp.float32)
    return pl.pallas_call(
        functools.partial(angle_kernel, cfg),
        out_shape=(shape, shape, vectors, vectors),
        in_specs=[vmem] * (4 + len(totals)),
        out_specs=(vmem, vmem, hbm, hbm),
        scratch_shapes=[pltpu.SemaphoreType.DMA((2,))],
        name="last_angles",
        compiler_params=pltpu.CompilerParams(vmem_limit_bytes=SMALL),
    )(anoise, ang, disp, vel, *totals)


def send_kernel(width, sets, slot_ref, mine_ref, other_ref, *out_refs):
    me = lax.axis_index("walker")
    for k, ref in enumerate(out_refs, 1):
        wanted = slot_of(slot_ref, lax.rem(me + k * width, width * sets))
        own = lax.rem(wanted, width) == lax.rem(me, width)

        @pl.when(own)
        def _():
            ref[...] = mine_ref[...]

        @pl.when(jnp.logical_not(own))
        def _():
            ref[...] = other_ref[...]


def pick_kernel(width, sets, windows, slot_ref, *refs):
    block_refs = refs[: sets + 1]
    charge_ref, strength_ref, site_ref, sub_ref = refs[sets + 1 : sets + 5]
    *pay_refs, vel_ref, ang_ref = refs[sets + 5 :]
    rows_x = vel_ref.shape[0]
    me = lax.axis_index("walker")
    source = slot_of(slot_ref, me)
    hop = lax.rem(me // width - source // width + sets, sets)
    away = (lax.rem(source, width) != lax.rem(me, width)).astype(jnp.int32)
    choice = jnp.where(hop > 0, hop + 1, away)
    own_ref = pay_refs[0]
    for k, ref in enumerate(block_refs):

        @pl.when(choice == k)
        def _():
            for i in range(rows_x):
                own_ref[i, 0:3] = ref[6 * i : 6 * i + 3]
                vel_ref[i] = ref[6 * i + 3 : 6 * i + 6]
            ang_ref[...] = ref[6 * rows_x]

    site, sub = site_ref[...], sub_ref[...]
    grouped = site < NSITE
    own_ref[:, 3] = charge_ref[...]
    own_ref[:, 4] = strength_ref[...]
    own_ref[:, 5] = jnp.where(grouped, site * NSUB + sub, -1).astype(jnp.float32)
    own_ref[:, 6] = jnp.where(grouped, site, -1).astype(jnp.float32)
    for (rows, cols), ref in zip(windows[1:], pay_refs[1:]):
        for ri, i in enumerate(rows):
            for cj, j in enumerate(cols):
                ref[ri, :, cj : cj + 1, :] = own_ref[i, :, j : j + 1, :]


def pack_kernel(pos_ref, vel_ref, theta_ref, speed_ref, out_ref, angle_ref, sems):
    rows_x = pos_ref.shape[0]
    copies = [
        pltpu.make_async_copy(theta_ref.at[0], angle_ref.at[0], sems.at[0]),
        pltpu.make_async_copy(speed_ref.at[0], angle_ref.at[1], sems.at[1]),
    ]
    for i in range(rows_x):
        for kind, ref in enumerate((pos_ref, vel_ref)):
            copies.append(
                pltpu.make_async_copy(
                    ref.at[i], out_ref.at[pl.ds(6 * i + 3 * kind, 3)], sems.at[2 + 2 * i + kind]
                )
            )
    for copy in copies:
        copy.start()
    out_ref[6 * rows_x] = jnp.zeros(out_ref.shape[1:], jnp.float32)
    for copy in copies:
        copy.wait()
    for kind in range(2):
        out_ref[6 * rows_x, :, kind * NSUB : (kind + 1) * NSUB] = angle_ref[kind]


def slot_of(slot_ref, index):
    slots = slot_ref[...].astype(jnp.float32)
    lane = lax.broadcasted_iota(jnp.int32, slots.shape, 1)
    return jnp.sum(jnp.where(lane == index, slots, 0.0)).astype(jnp.int32)


def clone(cfg, positions, velocities, theta, speed, source_slot, charges, strengths, atom_site, atom_sub):
    peers = lax.axis_size("walker")
    width = 2 if peers % 2 == 0 else 1
    sets = peers // width
    rows_x, rows_y, lanes = charges.shape
    vmem = pl.BlockSpec(memory_space=pltpu.VMEM)
    message = pl.pallas_call(
        pack_kernel,
        out_shape=jax.ShapeDtypeStruct((6 * rows_x + 1, rows_y, lanes), jnp.float32),
        in_specs=[pl.BlockSpec(memory_space=pltpu.HBM)] * 4,
        out_specs=vmem,
        scratch_shapes=[
            pltpu.VMEM((2, NSITE, NSUB), jnp.float32),
            pltpu.SemaphoreType.DMA((2 + 2 * rows_x,)),
        ],
        name="pack_walker",
    )(positions, velocities, theta, speed)
    source_slot = source_slot.reshape(1, peers)
    other = message
    if width == 2:
        other = lax.ppermute(message, "walker", [(w, w ^ 1) for w in range(peers)])
    blocks = [message, other]
    if sets > 1:
        shape = jax.ShapeDtypeStruct(message.shape, jnp.float32)
        sent = pl.pallas_call(
            functools.partial(send_kernel, width, sets),
            out_shape=(shape,) * (sets - 1),
            in_specs=[vmem, vmem, vmem],
            out_specs=(vmem,) * (sets - 1),
            name="choose_sent",
        compiler_params=pltpu.CompilerParams(vmem_limit_bytes=SMALL),
        )(source_slot, message, other)
        for k, value in enumerate(sent, 1):
            blocks.append(
                lax.ppermute(
                    value, "walker", [(w, (w + k * width) % peers) for w in range(peers)]
                )
            )
    shapes = [(len(rows), 7, len(cols), lanes) for rows, cols in cfg["windows"]]
    shapes += [(rows_x, 3, rows_y, lanes), (rows_y, lanes)]
    return pl.pallas_call(
        functools.partial(pick_kernel, width, sets, cfg["windows"]),
        out_shape=tuple(jax.ShapeDtypeStruct(shape, jnp.float32) for shape in shapes),
        in_specs=[vmem] * (len(blocks) + 5),
        out_specs=(vmem,) * len(shapes),
        name="choose_received",
        compiler_params=pltpu.CompilerParams(vmem_limit_bytes=SMALL),
    )(source_slot, *blocks, charges, strengths, atom_site, atom_sub)


def make_cfg(rows_x, rows_y, lanes, count_x, count_y, slots, offsets):
    tiles = rows_x * rows_y
    return dict(
        blocks=1 + len(offsets),
        covered=1 + len(offsets) == count_x * count_y,
        tiles=tiles,
        lanes=lanes,
        rows_x=rows_x,
        rows_y=rows_y,
        count_x=count_x,
        count_y=count_y,
        slots=slots,
        pool=(rows_x + 2) * (rows_y + 2),
        windows=[window(offset, rows_x, rows_y) for offset in [(0, 0)] + offsets],
        sources=pool_sources(rows_x, rows_y, count_x, count_y, offsets),
        depth=128,
        pool_group=next(g for g in (36, 6, 4, 3, 2, 1) if (rows_x + 2) * (rows_y + 2) % g == 0),
        roomy=min(rows_x * count_x, rows_y * count_y) >= 8,
        box_x=float(rows_x * count_x),
        box_y=float(rows_y * count_y),
        angle_mass=rows_x * count_x * rows_y * count_y * lanes * theta_share,
    )


def per_device(
    positions,
    velocities,
    lambda_theta,
    theta_velocity,
    source_slot,
    atom_noise,
    theta_noise,
    charges,
    strengths,
    inverse_mass,
    atom_site,
    atom_sub,
    partners,
):
    count_x, count_y = lax.axis_size("gx"), lax.axis_size("gy")
    rows_x, rows_y, lanes = charges.shape
    tiles = rows_x * rows_y
    offsets = neighbour_offsets(count_x, count_y)
    cfg = make_cfg(rows_x, rows_y, lanes, count_x, count_y, partners.shape[-1], offsets)

    def gather_blocks(values):
        return [values[0]] + [
            shifted(value, offset, count_x, count_y) for value, offset in zip(values[1:], offsets)
        ]

    *pays, vel, ang = clone(
        cfg, positions[0].transpose(0, 2, 1, 3), velocities[0].transpose(0, 2, 1, 3),
        lambda_theta, theta_velocity, source_slot, charges, strengths, atom_site, atom_sub,
    )
    noise = atom_noise.transpose(0, 1, 2, 4, 3, 5)
    at_x = jnp.arange(rows_x)[:, None, None] + 1 + jnp.arange(9) // 3 - 1
    at_y = jnp.arange(rows_y)[:, None] + 1 + jnp.arange(9) % 3 - 1
    entries = at_x * (rows_y + 2) + at_y
    listed = jnp.any(partners[..., None, :] == entries[..., None], axis=-1).astype(jnp.int32)
    first = pays[0]
    pool_stat = None
    for moment in range(STEPS):
        totals = None
        if moment > 0 and not cfg["covered"]:
            totals = lax.psum(pays[0][:, 3].reshape(tiles, lanes)[:NSUB], ("gx", "gy"))
        outs = step_call(
            cfg, moment, listed, theta_noise, gather_blocks(pays), pool_stat, totals, vel,
            noise, inverse_mass, ang, first,
        )
        own = cfg["blocks"] if moment < STEPS - 1 else 1
        pays, (vel, ang, *rest) = outs[:own], outs[own:]
        if moment == 0:
            pool_stat = rest[0]
    packed = rest[0]
    if cfg["covered"]:
        totals = gather_blocks([packed] * cfg["blocks"])
    else:
        totals = [lax.psum(packed, ("gx", "gy"))]
    theta, theta_speed, disp, vel = angle_call(cfg, theta_noise, ang, pays[0], vel, totals)
    back = lambda value: value.transpose(0, 2, 1, 3)[None]
    return back(disp), back(vel), theta, theta_speed


def solution(mesh):
    in_specs = (
        P("walker", "gx", "gy", None, None),
        P("walker", "gx", "gy", None, None),
        P("walker", None, None),
        P("walker", None, None),
        P(),
        P("walker", None, "gx", "gy", None, None),
        P("walker", None, None, None),
        P("gx", "gy", None),
        P("gx", "gy", None),
        P("gx", "gy", None),
        P("gx", "gy", None),
        P("gx", "gy", None),
        P("gx", "gy", None),
    )
    out_specs = (
        P("walker", "gx", "gy", None, None),
        P("walker", "gx", "gy", None, None),
        P("walker", None, None),
        P("walker", None, None),
    )
    return jax.shard_map(
        per_device, mesh=mesh, in_specs=in_specs, out_specs=out_specs, check_vma=False
    )
```
